128 devices in a mesh: seq: 16 (over z, x), tp: 8 (over y, core).
Axes of the slice: x: 4, y: 4, z: 4, core: 2. Of those that a mesh axis runs over, the one named last changes fastest.
Arguments:
- token_inputs: bfloat16 [4, 128, 5120], P(None, 'seq'), may hold values from -6 to 6
- attn_gain: float32 [5120], replicated, may hold values from 0.1 to 1.9
- w_query: bfloat16 [5120, 4096], P(None, 'tp'), may hold values from -0.078125 to 0.078125
- key_projection: bfloat16 [5120, 1024], P(None, 'tp'), may hold values from -0.078125 to 0.078125
- value_projection: bfloat16 [5120, 1024], P(None, 'tp'), may hold values from -0.078125 to 0.078125
- w_output: bfloat16 [4096, 5120], P('tp'), may hold values from -0.09375 to 0.09375
- mlp_gain: float32 [5120], replicated, may hold values from 0.1 to 1.9
- w_gate: bfloat16 [5120, 32768], P(None, ('seq', 'tp')), may hold values from -0.078125 to 0.078125
- w_up: bfloat16 [5120, 32768], P(None, ('seq', 'tp')), may hold values from -0.078125 to 0.078125
- w_down: bfloat16 [32768, 5120], P(('seq', 'tp')), may hold values from -0.03125 to 0.03125
- key_cache: bfloat16 [576, 8, 256, 128], P('seq', 'tp'), may hold values from -300 to 300
- paged_value_cache: bfloat16 [576, 8, 256, 128], P('seq', 'tp'), may hold values from -6 to 6
- cache_lengths: int32 [128], replicated, may hold values from 1 to 32768, as said below
- page_request: int32 [576], P('seq'), may hold values from -1 to 127, as said below
- page_number: int32 [576], P('seq'), may hold values from 0 to 127, as said below
- request_slot: int32 [128], replicated, may hold values from 0 to 127, each once
Outputs:
- attended: bfloat16 [4, 128, 5120], P(None, 'seq')
- layer_out: bfloat16 [4, 128, 5120], P(None, 'seq')
The draws below stay inside these ranges and needn't reach their ends.
Inputs may be any that keep to these rules, and one draw needn't show every extreme that they name: `cache_lengths`: one request holds exactly 32768 positions. `page_request`: the pages of request r that hold its positions are numbered 0 to ceil(cache_lengths[r] / 256) - 1, and each of them is held by exactly one pool page; every other pool page is free (-1), and some page is free. `page_number`: 0 on free pages.
All inputs are finite; a program needn't handle non-finite values.
Results may differ from the reference program's by a relative error of at most 0.012.
Values may be sent and summed in bfloat16 or wider, within the bound.
A program may use at most 128 MiB of HBM per device.

```python
import jax
import jax.numpy as jnp
from jax import lax

MODEL_WIDTH = 5120
QUERY_HEADS = 32
KEY_VALUE_HEADS = 8
HEAD_SIZE = 128
FF = 32768
STEPS = 4
PAGE_POSITIONS = 256
MAXPAGES = 128
REQUEST_COUNT = 128
POOL_PAGES = 576


def page_layout(key):
    layout_key = jax.random.fold_in(key, 23)
    key_big, key_pages, key_tails, key_order = jax.random.split(layout_key, 4)
    request_ids = jnp.arange(REQUEST_COUNT, dtype=jnp.int32)
    biggest = jax.random.randint(key_big, (), 0, REQUEST_COUNT)
    other_most = (POOL_PAGES - MAXPAGES - 1) // (REQUEST_COUNT - 1)
    page_counts = jax.random.randint(key_pages, (REQUEST_COUNT,), 1, other_most + 1)
    page_counts = jnp.where(request_ids == biggest, MAXPAGES, page_counts).astype(jnp.int32)
    tail_tokens = jax.random.randint(key_tails, (REQUEST_COUNT,), 1, PAGE_POSITIONS + 1)
    tail_tokens = jnp.where(request_ids == biggest, PAGE_POSITIONS, tail_tokens).astype(jnp.int32)
    lengths = (page_counts - 1) * PAGE_POSITIONS + tail_tokens
    pool_order = jax.random.permutation(key_order, REQUEST_COUNT)
    ordered_counts = page_counts[pool_order]
    ordered_starts = (jnp.cumsum(ordered_counts) - ordered_counts).astype(jnp.int32)
    starts = jnp.zeros((REQUEST_COUNT,), jnp.int32).at[pool_order].set(ordered_starts)
    pool_slots = jnp.arange(POOL_PAGES, dtype=jnp.int32)
    inside = (pool_slots[:, None] >= starts[None, :]) & (pool_slots[:, None] < (starts + page_counts)[None, :])
    page_owner = jnp.where(jnp.any(inside, axis=1), jnp.sum(jnp.where(inside, request_ids[None, :], 0), axis=1), -1)
    number = jnp.where(page_owner >= 0, pool_slots - starts[jnp.maximum(page_owner, 0)], 0)
    return (lengths.astype(jnp.int32), page_owner.astype(jnp.int32), number.astype(jnp.int32))


def draw_cache_lengths(key, part):
    return page_layout(key)[0]


def draw_page_request(key, part):
    return page_layout(key)[1]


def draw_page_number(key, part):
    return page_layout(key)[2]


def draw_key_cache(key, part):
    noise_key = jax.random.fold_in(jax.random.fold_in(key, 5), 0)
    array_shape = (POOL_PAGES, KEY_VALUE_HEADS, PAGE_POSITIONS, HEAD_SIZE)
    result = jax.random.truncated_normal(noise_key, -6.0, 6.0, array_shape, jnp.float32)
    return result.astype(jnp.bfloat16)


def shard_levels(own_key, dims, pieces, low, top_value):
    def one(axis_at, shards_of):
        steps = jax.random.uniform(jax.random.fold_in(jax.random.fold_in(own_key, 6), axis_at), (shards_of,), jnp.float32, low / len(pieces), top_value / len(pieces))
        return jnp.repeat(jnp.exp(steps), dims[axis_at] // shards_of).reshape((-1,) + (1,) * (len(dims) - axis_at - 1))

    factor_of = one(*pieces[0])
    for cut in pieces[1:]:
        factor_of = factor_of * one(*cut)
    return factor_of


def gaussian(key, shape, width, reach, shards=(), held_as=jnp.bfloat16):
    array = width * jax.random.normal(key, shape, jnp.float32)
    if shards:
        array = array * shard_levels(key, shape, shards, -0.22, 0.18)
    return jnp.clip(array, -reach, reach).astype(held_as)


def setup_inputs(seed: int = 0) -> dict:
    arg_keys = jax.random.split(jax.random.key(seed), 17)
    token_inputs = gaussian(arg_keys[0], (STEPS, REQUEST_COUNT, MODEL_WIDTH), 1.0, 6.0, ((1, 16),))
    attn_gain = jnp.clip(1.0 + 0.18 * jax.random.normal(arg_keys[1], (MODEL_WIDTH,), jnp.float32), 0.1, 1.9)
    w_query = gaussian(arg_keys[2], (MODEL_WIDTH, QUERY_HEADS * HEAD_SIZE), MODEL_WIDTH ** -0.5, 0.078125, ((1, 8),))
    key_projection = gaussian(arg_keys[3], (MODEL_WIDTH, KEY_VALUE_HEADS * HEAD_SIZE), MODEL_WIDTH ** -0.5, 0.078125, ((1, 8),))
    value_projection = gaussian(arg_keys[4], (MODEL_WIDTH, KEY_VALUE_HEADS * HEAD_SIZE), MODEL_WIDTH ** -0.5, 0.078125, ((1, 8),))
    w_output = gaussian(arg_keys[5], (QUERY_HEADS * HEAD_SIZE, MODEL_WIDTH), (QUERY_HEADS * HEAD_SIZE) ** -0.5, 0.09375, ((0, 8),))
    mlp_gain = jnp.clip(1.0 + 0.18 * jax.random.normal(arg_keys[6], (MODEL_WIDTH,), jnp.float32), 0.1, 1.9)
    w_gate = gaussian(arg_keys[7], (MODEL_WIDTH, FF), MODEL_WIDTH ** -0.5, 0.078125, ((1, 128),))
    w_up = gaussian(arg_keys[8], (MODEL_WIDTH, FF), MODEL_WIDTH ** -0.5, 0.078125, ((1, 128),))
    w_down = gaussian(arg_keys[9], (FF, MODEL_WIDTH), FF ** -0.5, 0.03125, ((0, 128),))
    key_cache = draw_key_cache(jax.random.fold_in(arg_keys[16], 71), 0)
    paged_value_cache = gaussian(arg_keys[11], (POOL_PAGES, KEY_VALUE_HEADS, PAGE_POSITIONS, HEAD_SIZE), 1.0, 6.0, ((0, 16), (1, 8)))
    cache_lengths = draw_cache_lengths(jax.random.fold_in(arg_keys[16], 71), 0)
    page_request = draw_page_request(jax.random.fold_in(arg_keys[16], 71), 0)
    page_number = draw_page_number(jax.random.fold_in(arg_keys[16], 71), 0)
    request_slot = jax.random.permutation(arg_keys[15], REQUEST_COUNT).astype(jnp.int32)
    return {"token_inputs": token_inputs, "attn_gain": attn_gain, "w_query": w_query, "key_projection": key_projection, "value_projection": value_projection, "w_output": w_output, "mlp_gain": mlp_gain, "w_gate": w_gate, "w_up": w_up, "w_down": w_down, "key_cache": key_cache, "paged_value_cache": paged_value_cache, "cache_lengths": cache_lengths, "page_request": page_request, "page_number": page_number, "request_slot": request_slot}


rope_theta = 100000000.0
norm_eps = 1e-05
masked_low = -1e+30

def rms_norm(values, gain):
    floats = values.astype(jnp.float32)
    square_mean = lax.optimization_barrier(jnp.mean(floats * floats, axis=-1, keepdims=True))
    return floats * lax.rsqrt(square_mean + norm_eps) * gain

def apply_rotary(values, token_position):
    half_dim = values.shape[-1] // 2
    exponent = jnp.arange(half_dim, dtype=jnp.float32) * (2.0 / values.shape[-1])
    inverse_freq = rope_theta ** (-exponent)
    angles = token_position.astype(jnp.float32)[:, None] * inverse_freq[None, :]
    angles = angles[:, None, :]
    cosine = jnp.cos(angles)
    sine_part = jnp.sin(angles)
    first_half = values[..., :half_dim]
    second_half = values[..., half_dim:]
    return jnp.concatenate([first_half * cosine - second_half * sine_part, second_half * cosine + first_half * sine_part], axis=-1)

def cache_part(query_head_rows, key_cache, paged_value_cache, page_req, token_mask, page_live):
    request_ids = jnp.arange(REQUEST_COUNT, dtype=jnp.int32)

    def per_head(operands):
        keys_head, values_head, query_head = operands
        page_query = query_head[page_req].astype(jnp.float32)
        scores = jnp.einsum('pgd,ptd->pgt', page_query, keys_head.astype(jnp.float32)) * HEAD_SIZE ** (-0.5)
        scores = jnp.where(token_mask[:, None, :], scores, masked_low)
        page_max = lax.optimization_barrier(jnp.max(scores, axis=-1))
        weights = jnp.where(token_mask[:, None, :], jnp.exp(scores - page_max[..., None]), 0.0)
        page_sum = lax.optimization_barrier(jnp.sum(weights, axis=-1))
        rounded = lax.optimization_barrier(weights.astype(jnp.bfloat16))
        page_acc = jnp.einsum('pgt,ptd->pgd', rounded.astype(jnp.float32), values_head.astype(jnp.float32))
        page_owner = (page_req[None, :] == request_ids[:, None]) & page_live[None, :]
        req_max = lax.optimization_barrier(jnp.max(jnp.where(page_owner[:, :, None], page_max[None], masked_low), axis=1))
        factor = jnp.exp(page_max - req_max[page_req])
        onehot = page_owner.astype(jnp.float32)
        req_sum = jnp.einsum('rp,pg->rg', onehot, page_sum * factor, precision=lax.Precision.HIGHEST)
        req_acc = jnp.einsum('rp,pgd->rgd', onehot, page_acc * factor[..., None], precision=lax.Precision.HIGHEST)
        return (req_max, req_sum, req_acc)
    head_max, head_sum, head_acc = lax.map(per_head, (jnp.swapaxes(key_cache, 0, 1), jnp.swapaxes(paged_value_cache, 0, 1), jnp.swapaxes(query_head_rows, 0, 1)))
    return (jnp.swapaxes(head_max, 0, 1), jnp.swapaxes(head_sum, 0, 1), jnp.swapaxes(head_acc, 0, 1))

def reference(token_inputs, attn_gain, w_query, key_projection, value_projection, w_output, mlp_gain, w_gate, w_up, w_down, key_cache, paged_value_cache, cache_lengths, page_request, page_number, request_slot):
    heads_per_group = QUERY_HEADS // KEY_VALUE_HEADS
    inverse_slot = jnp.zeros((REQUEST_COUNT,), jnp.int32).at[request_slot].set(jnp.arange(REQUEST_COUNT, dtype=jnp.int32))
    page_live = page_request >= 0
    page_req = jnp.where(page_live, page_request, 0).astype(jnp.int32)
    token_pos = page_number[:, None] * PAGE_POSITIONS + jnp.arange(PAGE_POSITIONS, dtype=jnp.int32)[None, :]
    token_mask = page_live[:, None] & (token_pos < cache_lengths[page_req][:, None])
    recent_keys = []
    recent_values = []
    attended_list = []
    output_list = []
    for step_index in range(STEPS):
        hidden_in = token_inputs[step_index][request_slot]
        token_position = cache_lengths + step_index
        normalized_input = rms_norm(hidden_in, attn_gain).astype(jnp.bfloat16)
        query_head_rows = apply_rotary(jnp.dot(normalized_input, w_query, preferred_element_type=jnp.float32).reshape(REQUEST_COUNT, QUERY_HEADS, HEAD_SIZE), token_position)
        query_head_rows = query_head_rows.astype(jnp.bfloat16).reshape(REQUEST_COUNT, KEY_VALUE_HEADS, heads_per_group, HEAD_SIZE)
        fresh_key = apply_rotary(jnp.dot(normalized_input, key_projection, preferred_element_type=jnp.float32).reshape(REQUEST_COUNT, KEY_VALUE_HEADS, HEAD_SIZE), token_position).astype(jnp.bfloat16)
        fresh_value = jnp.dot(normalized_input, value_projection, preferred_element_type=jnp.float32).astype(jnp.bfloat16).reshape(REQUEST_COUNT, KEY_VALUE_HEADS, HEAD_SIZE)
        recent_keys.append(fresh_key)
        recent_values.append(fresh_value)
        cache_max, cache_sum, cache_acc = cache_part(query_head_rows, key_cache, paged_value_cache, page_req, token_mask, page_live)
        stacked_keys = jnp.stack(recent_keys).astype(jnp.float32)
        stacked_values = jnp.stack(recent_values).astype(jnp.float32)
        recent_scores = jnp.einsum('rkgd,jrkd->rkgj', query_head_rows.astype(jnp.float32), stacked_keys) * HEAD_SIZE ** (-0.5)
        recent_max = lax.optimization_barrier(jnp.max(recent_scores, axis=-1))
        recent_weights = jnp.exp(recent_scores - recent_max[..., None])
        recent_sum = lax.optimization_barrier(jnp.sum(recent_weights, axis=-1))
        rounded = lax.optimization_barrier(recent_weights.astype(jnp.bfloat16))
        recent_acc = jnp.einsum('rkgj,jrkd->rkgd', rounded.astype(jnp.float32), stacked_values)
        total_max = jnp.maximum(cache_max, recent_max)
        cache_factor = jnp.exp(cache_max - total_max)
        recent_factor = jnp.exp(recent_max - total_max)
        total_sum = cache_sum * cache_factor + recent_sum * recent_factor
        total_acc = cache_acc * cache_factor[..., None] + recent_acc * recent_factor[..., None]
        attention = (total_acc / total_sum[..., None]).astype(jnp.bfloat16).reshape(REQUEST_COUNT, QUERY_HEADS * HEAD_SIZE)
        attended = (hidden_in.astype(jnp.float32) + jnp.dot(attention, w_output, preferred_element_type=jnp.float32)).astype(jnp.bfloat16)
        normed_mlp = rms_norm(attended, mlp_gain).astype(jnp.bfloat16)
        gate_proj = jnp.dot(normed_mlp, w_gate, preferred_element_type=jnp.float32)
        up_proj = jnp.dot(normed_mlp, w_up, preferred_element_type=jnp.float32)
        activation = (jax.nn.silu(gate_proj) * up_proj).astype(jnp.bfloat16)
        layer_out = (attended.astype(jnp.float32) + jnp.dot(activation, w_down, preferred_element_type=jnp.float32)).astype(jnp.bfloat16)
        attended_list.append(attended[inverse_slot])
        output_list.append(layer_out[inverse_slot])
    return (jnp.stack(attended_list), jnp.stack(output_list))
```

```python
import functools

import jax
import jax.numpy as jnp
from jax import lax
from jax.experimental import pallas as pl
from jax.experimental.pallas import tpu as pltpu
from jax.sharding import PartitionSpec as P

STEPS = 4
rope_theta = 100000000.0
norm_eps = 1e-05
masked_low = -1e30


def rms_norm(values, gain):
    floats = values.astype(jnp.float32)
    square_mean = jnp.mean(floats * floats, axis=-1, keepdims=True)
    return floats * lax.rsqrt(square_mean + norm_eps) * gain


def rotary_tables(token_position, head_dim):
    half_dim = head_dim // 2
    exponent = jnp.arange(half_dim, dtype=jnp.float32) * (2.0 / head_dim)
    inverse_freq = rope_theta ** (-exponent)
    angles = token_position.astype(jnp.float32)[:, None] * inverse_freq[None, :]
    return jnp.cos(angles), jnp.sin(angles)


def rotate(values, cosine, sine):
    half = values.shape[-1] // 2
    a = values[..., :half]
    b = values[..., half:]
    return jnp.concatenate([a * cosine - b * sine, b * cosine + a * sine], axis=-1)


def paged_kernel(pages, rows_ref, valid_ref, q_ref, k_ref, v_ref, o_ref, lse_ref, m_s, l_s, acc_s):
    step = pl.program_id(0)
    scale = k_ref.shape[-1] ** (-0.5)

    @pl.when(step == 0)
    def _():
        m_s[...] = jnp.full_like(m_s, masked_low)
        l_s[...] = jnp.zeros_like(l_s)
        acc_s[...] = jnp.zeros_like(acc_s)

    stats = []
    for i in range(pages):
        page = step * pages + i
        row = rows_ref[page]
        valid = valid_ref[page]
        q = q_ref[row]
        s = (
            lax.dot_general(
                q, k_ref[i], (((1,), (1,)), ((), ())), preferred_element_type=jnp.float32
            )
            * scale
        )
        live = lax.broadcasted_iota(jnp.int32, s.shape, 1) < valid
        s = jnp.where(live, s, masked_low)
        m = jnp.max(s, axis=-1, keepdims=True)
        w = jnp.where(live, jnp.exp(s - m), 0.0)
        l = jnp.sum(w, axis=-1, keepdims=True)
        acc = jnp.dot(w.astype(jnp.bfloat16), v_ref[i], preferred_element_type=jnp.float32)
        stats.append((row, m, l, acc))
    for row, m, l, acc in stats:
        m_old = m_s[row]
        m_new = jnp.maximum(m_old, m)
        a_old = jnp.exp(m_old - m_new)
        a_new = jnp.exp(m - m_new)
        m_s[row] = m_new
        l_s[row] = l_s[row] * a_old + l * a_new
        acc_s[row] = acc_s[row] * a_old + acc * a_new

    @pl.when(step == pl.num_programs(0) - 1)
    def _():
        l = l_s[...]
        safe = jnp.where(l > 0.0, l, 1.0)
        o_ref[...] = (acc_s[...] / safe).astype(o_ref.dtype)
        lse = jnp.where(l > 0.0, m_s[...] + jnp.log(safe), masked_low)
        eye = lax.broadcasted_iota(jnp.int32, lse.shape, 1) == lax.broadcasted_iota(
            jnp.int32, lse.shape, 2
        )
        lse_ref[...] = jnp.sum(jnp.where(eye, lse, 0.0), axis=1)


def paged_attention(rows, valid, queries, keys, values):
    total, group, dim = queries.shape
    count, length, _ = keys.shape
    pages = next(n for n in (6, 4, 3, 2, 1) if count % n == 0)
    return pl.pallas_call(
        functools.partial(paged_kernel, pages),
        grid_spec=pltpu.PrefetchScalarGridSpec(
            num_scalar_prefetch=2,
            grid=(count // pages,),
            in_specs=[
                pl.BlockSpec((total, group, dim), lambda i, *_: (0, 0, 0)),
                pl.BlockSpec((pages, length, dim), lambda i, *_: (i, 0, 0)),
                pl.BlockSpec((pages, length, dim), lambda i, *_: (i, 0, 0)),
            ],
            out_specs=[
                pl.BlockSpec((total, group, dim), lambda i, *_: (0, 0, 0)),
                pl.BlockSpec((total, dim), lambda i, *_: (0, 0)),
            ],
            scratch_shapes=[
                pltpu.VMEM((total, group, dim), jnp.float32),
                pltpu.VMEM((total, group, dim), jnp.float32),
                pltpu.VMEM((total, group, dim), jnp.float32),
            ],
        ),
        out_shape=[
            jax.ShapeDtypeStruct((total, group, dim), jnp.bfloat16),
            jax.ShapeDtypeStruct((total, dim), jnp.float32),
        ],
        name="paged_attention",
    )(rows, valid, queries, keys, values)


def local(
    token_inputs,
    attn_gain,
    w_query,
    key_projection,
    value_projection,
    w_output,
    mlp_gain,
    w_gate,
    w_up,
    w_down,
    key_cache,
    paged_value_cache,
    cache_lengths,
    page_request,
    page_number,
    request_slot,
):
    steps, row_count, width = token_inputs.shape
    seq = lax.axis_size("seq")
    total_rows = row_count * seq
    page_count, kv_local, page_size, head_dim = key_cache.shape
    group = w_query.shape[1] // head_dim
    scale = head_dim ** (-0.5)
    first_row = lax.axis_index("seq") * row_count
    own_rows = first_row + jnp.arange(row_count, dtype=jnp.int32)
    own_match = request_slot[None, :] == own_rows[:, None]
    row_lengths = jnp.sum(jnp.where(own_match, cache_lengths[None, :], 0), axis=1)
    page_live = page_request >= 0
    page_req = jnp.where(page_live, page_request, 0)
    req_match = page_req[:, None] == jnp.arange(total_rows, dtype=jnp.int32)[None, :]
    page_row = jnp.sum(jnp.where(req_match, request_slot[None, :], 0), axis=1)
    page_len = jnp.sum(jnp.where(req_match, cache_lengths[None, :], 0), axis=1)
    valid = jnp.where(page_live, jnp.clip(page_len - page_number * page_size, 0, page_size), 0)

    x = token_inputs.reshape(steps * row_count, width)
    normed = rms_norm(x, attn_gain).astype(jnp.bfloat16)
    position = (jnp.arange(steps, dtype=jnp.int32)[:, None] + row_lengths[None, :]).reshape(-1)
    cosine, sine = rotary_tables(position, head_dim)
    q = jnp.dot(normed, w_query, preferred_element_type=jnp.float32)
    q = rotate(q.reshape(-1, group, head_dim), cosine[:, None], sine[:, None])
    q = q.astype(jnp.bfloat16).reshape(steps, row_count, group, head_dim)
    fresh_k = rotate(
        jnp.dot(normed, key_projection, preferred_element_type=jnp.float32), cosine, sine
    )
    fresh_k = fresh_k.astype(jnp.bfloat16).reshape(steps, row_count, head_dim)
    fresh_v = jnp.dot(normed, value_projection, preferred_element_type=jnp.float32)
    fresh_v = fresh_v.astype(jnp.bfloat16).reshape(steps, row_count, head_dim)
    q = jnp.swapaxes(q, 0, 1).reshape(row_count, steps * group, head_dim)
    all_q = lax.all_gather(q, "seq", axis=0, tiled=True)
    part, lse = paged_attention(
        page_row, valid, all_q, key_cache[:, 0], paged_value_cache[:, 0]
    )
    part = lax.all_to_all(part.reshape(seq, row_count, steps * group, head_dim), "seq", 0, 0)
    lse = lax.all_to_all(lse.reshape(seq, row_count, head_dim), "seq", 0, 0)
    lse = lse[:, :, : steps * group]
    s = jnp.einsum("rqd,jrd->rqj", q, fresh_k, preferred_element_type=jnp.float32) * scale
    allowed = (
        jnp.arange(steps)[None, :] <= (jnp.arange(steps * group) // group)[:, None]
    )
    s = jnp.where(allowed[None], s, masked_low)
    recent_max = jnp.max(s, axis=-1)
    w = jnp.where(allowed[None], jnp.exp(s - recent_max[..., None]), 0.0)
    recent_sum = jnp.sum(w, axis=-1)
    recent_acc = jnp.einsum(
        "rqj,jrd->rqd", w.astype(jnp.bfloat16), fresh_v, preferred_element_type=jnp.float32
    )
    top = jnp.maximum(jnp.max(lse, axis=0), recent_max)
    factor = jnp.exp(lse - top[None])
    fresh_factor = jnp.exp(recent_max - top)
    total = jnp.sum(factor, axis=0) + recent_sum * fresh_factor
    acc = jnp.sum(part.astype(jnp.float32) * factor[..., None], axis=0)
    acc = acc + recent_acc * fresh_factor[..., None]
    attention = (acc / total[..., None]).astype(jnp.bfloat16)
    attention = jnp.swapaxes(attention.reshape(row_count, steps, group * head_dim), 0, 1)
    attention = attention.reshape(steps * row_count, group * head_dim)
    head_part = jnp.dot(attention, w_output, preferred_element_type=jnp.float32)
    attended = (x.astype(jnp.float32) + lax.psum(head_part, "tp")).astype(jnp.bfloat16)
    normed_mlp = rms_norm(attended, mlp_gain).astype(jnp.bfloat16)
    everyone = lax.all_gather(normed_mlp, "seq", axis=0, tiled=True)
    gate = jnp.dot(everyone, w_gate, preferred_element_type=jnp.float32)
    up = jnp.dot(everyone, w_up, preferred_element_type=jnp.float32)
    activation = (jax.nn.silu(gate) * up).astype(jnp.bfloat16)
    partial = jnp.dot(activation, w_down, preferred_element_type=jnp.float32)
    mlp = lax.psum_scatter(partial, "seq", scatter_dimension=0, tiled=True)
    mlp = lax.psum(mlp, "tp")
    layer_out = (attended.astype(jnp.float32) + mlp).astype(jnp.bfloat16)
    shape = (steps, row_count, width)
    return attended.reshape(shape), layer_out.reshape(shape)


def solution(mesh):
    in_specs = (
        P(None, "seq", None),
        P(),
        P(None, "tp"),
        P(None, "tp"),
        P(None, "tp"),
        P("tp", None),
        P(),
        P(None, ("seq", "tp")),
        P(None, ("seq", "tp")),
        P(("seq", "tp"), None),
        P("seq", "tp", None, None),
        P("seq", "tp", None, None),
        P(),
        P("seq"),
        P("seq"),
        P(),
    )
    out_specs = (P(None, "seq", None), P(None, "seq", None))
    return jax.shard_map(local, mesh=mesh, in_specs=in_specs, out_specs=out_specs, check_vma=False)
```

```python
import functools

import jax
import jax.numpy as jnp
from jax import lax
from jax.experimental import pallas as pl
from jax.experimental.pallas import tpu as pltpu
from jax.sharding import PartitionSpec as P

STEPS = 4
rope_theta = 100000000.0
norm_eps = 1e-05
masked_low = -1e30


def rms_norm(values, gain):
    floats = values.astype(jnp.float32)
    square_mean = jnp.mean(floats * floats, axis=-1, keepdims=True)
    return floats * lax.rsqrt(square_mean + norm_eps) * gain


def rotary_tables(token_position, head_dim):
    half_dim = head_dim // 2
    exponent = jnp.arange(half_dim, dtype=jnp.float32) * (2.0 / head_dim)
    inverse_freq = rope_theta ** (-exponent)
    angles = token_position.astype(jnp.float32)[:, None] * inverse_freq[None, :]
    return jnp.cos(angles), jnp.sin(angles)


def rotate(values, cosine, sine):
    half = values.shape[-1] // 2
    a = values[..., :half]
    b = values[..., half:]
    return jnp.concatenate([a * cosine - b * sine, b * cosine + a * sine], axis=-1)


def paged_kernel(pages, rows_ref, valid_ref, q_ref, k_ref, v_ref, o_ref, lse_ref, m_s, l_s, acc_s):
    step = pl.program_id(0)
    scale = k_ref.shape[-1] ** (-0.5)

    @pl.when(step == 0)
    def _():
        m_s[...] = jnp.full_like(m_s, masked_low)
        l_s[...] = jnp.zeros_like(l_s)
        acc_s[...] = jnp.zeros_like(acc_s)

    stats = []
    for i in range(pages):
        page = step * pages + i
        row = rows_ref[page]
        valid = valid_ref[page]
        q = q_ref[row]
        s = (
            lax.dot_general(
                q, k_ref[i], (((1,), (1,)), ((), ())), preferred_element_type=jnp.float32
            )
            * scale
        )
        live = lax.broadcasted_iota(jnp.int32, s.shape, 1) < valid
        s = jnp.where(live, s, masked_low)
        m = jnp.max(s, axis=-1, keepdims=True)
        w = jnp.where(live, jnp.exp(s - m), 0.0)
        l = jnp.sum(w, axis=-1, keepdims=True)
        acc = jnp.dot(w.astype(jnp.bfloat16), v_ref[i], preferred_element_type=jnp.float32)
        stats.append((row, m, l, acc))
    for row, m, l, acc in stats:
        m_old = m_s[row]
        m_new = jnp.maximum(m_old, m)
        a_old = jnp.exp(m_old - m_new)
        a_new = jnp.exp(m - m_new)
        m_s[row] = m_new
        l_s[row] = l_s[row] * a_old + l * a_new
        acc_s[row] = acc_s[row] * a_old + acc * a_new

    @pl.when(step == pl.num_programs(0) - 1)
    def _():
        l = l_s[...]
        safe = jnp.where(l > 0.0, l, 1.0)
        o_ref[...] = (acc_s[...] / safe).astype(o_ref.dtype)
        lse = jnp.where(l > 0.0, m_s[...] + jnp.log(safe), masked_low)
        eye = lax.broadcasted_iota(jnp.int32, lse.shape, 1) == lax.broadcasted_iota(
            jnp.int32, lse.shape, 2
        )
        lse_ref[...] = jnp.sum(jnp.where(eye, lse, 0.0), axis=1)


def paged_attention(rows, valid, queries, keys, values):
    total, group, dim = queries.shape
    count, length, _ = keys.shape
    pages = next(n for n in (6, 4, 3, 2, 1) if count % n == 0)
    return pl.pallas_call(
        functools.partial(paged_kernel, pages),
        grid_spec=pltpu.PrefetchScalarGridSpec(
            num_scalar_prefetch=2,
            grid=(count // pages,),
            in_specs=[
                pl.BlockSpec((total, group, dim), lambda i, *_: (0, 0, 0)),
                pl.BlockSpec((pages, length, dim), lambda i, *_: (i, 0, 0)),
                pl.BlockSpec((pages, length, dim), lambda i, *_: (i, 0, 0)),
            ],
            out_specs=[
                pl.BlockSpec((total, group, dim), lambda i, *_: (0, 0, 0)),
                pl.BlockSpec((total, dim), lambda i, *_: (0, 0)),
            ],
            scratch_shapes=[
                pltpu.VMEM((total, group, dim), jnp.float32),
                pltpu.VMEM((total, group, dim), jnp.float32),
                pltpu.VMEM((total, group, dim), jnp.float32),
            ],
        ),
        out_shape=[
            jax.ShapeDtypeStruct((total, group, dim), jnp.bfloat16),
            jax.ShapeDtypeStruct((total, dim), jnp.float32),
        ],
        name="paged_attention",
    )(rows, valid, queries, keys, values)


AXES = (("y", "x", "z"), ("x", "z", "y"), ("z", "y", "x"))
MESH = pl.DeviceIdType.MESH


class Place:
    def __init__(self):
        s = lax.axis_index("seq")
        t = lax.axis_index("tp")
        self.at = {"z": s // 4, "x": s % 4, "y": t // 2}
        self.core = t % 2
        self.s = s
        self.t = t

    def shifted(self, axis, by):
        return lax.rem(self.at[axis] + (by + 4), 4)

    def device(self, axis=None, by=0, flip=False):
        at = dict(self.at)
        if axis is not None:
            at[axis] = self.shifted(axis, by)
        core = 1 - self.core if flip else self.core
        return {"seq": at["z"] * 4 + at["x"], "tp": at["y"] * 2 + core}


class Wire:
    def __init__(self, send_sem, recv_sem):
        self.send_sem = send_sem
        self.recv_sem = recv_sem
        self.used = 0
        self.sent = []

    def slot(self):
        self.used += 1
        return self.used - 1

    def send(self, slot, src, dst, device):
        copy = pltpu.make_async_remote_copy(
            src_ref=src,
            dst_ref=dst,
            send_sem=self.send_sem.at[slot],
            recv_sem=self.recv_sem.at[slot],
            device_id=device,
            device_id_type=MESH,
        )
        copy.start()
        self.sent.append(copy)

    def recv(self, slot, dst, device):
        pltpu.make_async_remote_copy(
            src_ref=dst,
            dst_ref=dst,
            send_sem=self.send_sem.at[slot],
            recv_sem=self.recv_sem.at[slot],
            device_id=device,
            device_id_type=MESH,
        ).wait_recv()

    def drain(self):
        for copy in self.sent:
            copy.wait_send()


def greet(place):
    barrier = pltpu.get_barrier_semaphore()
    peers = [{"seq": place.s, "tp": lax.rem(place.t + j, 8)} for j in range(1, 8)]
    peers += [place.device(axis, by) for axis in ("x", "z") for by in (1, 2, 3)]
    for peer in peers:
        pl.semaphore_signal(barrier, inc=1, device_id=peer, device_id_type=MESH)
    return barrier, len(peers)


class Gather:
    def __init__(self, wire, place, axes, buf):
        self.wire, self.place, self.buf = wire, place, buf
        self.a, self.b, self.c = axes
        self.slots_a = [wire.slot() for _ in range(3)]
        self.slots_b = [wire.slot() for _ in range(4)]
        self.slots_c = [[wire.slot() for _ in range(4)] for _ in range(4)]
        self.slots_p = [[wire.slot() for _ in range(4)] for _ in range(4)]

    def group(self, db, dc, core=None):
        place = self.place
        core = place.core if core is None else core
        return self.buf.at[core, place.shifted(self.c, dc), place.shifted(self.b, db)]

    def half(self, db, dc, which):
        place = self.place
        return self.buf.at[
            place.core, place.shifted(self.c, dc), place.shifted(self.b, db), pl.ds(2 * which, 2)
        ]

    def block(self, da):
        place = self.place
        return self.buf.at[
            place.core, place.at[self.c], place.at[self.b], place.shifted(self.a, da)
        ]

    def open(self):
        mine = self.block(0)
        for j in (2, 1, 3):
            self.wire.send(self.slots_a[j - 1], mine, mine, self.place.device(self.a, j))

    def spread(self, db):
        mine = self.group(db, 0)
        slots = self.slots_c[db]
        self.wire.send(slots[0], mine, mine, self.place.device(self.c, 1))
        self.wire.send(slots[1], mine, mine, self.place.device(self.c, -1))
        self.over(db, 0)

    def over(self, db, dc):
        mine = self.group(db, dc)
        self.wire.send(self.slots_p[db][dc], mine, mine, self.place.device(flip=True))

    def line(self):
        for j in (1, 3, 2):
            self.wire.recv(self.slots_a[j - 1], self.block(-j), self.place.device(self.a, -j))
        mine = self.group(0, 0)
        self.wire.send(self.slots_b[0], mine, mine, self.place.device(self.b, 1))
        self.wire.send(self.slots_b[1], mine, mine, self.place.device(self.b, -1))
        self.spread(0)

    def plane_near(self):
        place, wire = self.place, self.wire
        wire.recv(self.slots_b[0], self.group(-1, 0), place.device(self.b, -1))
        part = self.half(-1, 0, 0)
        wire.send(self.slots_b[2], part, part, place.device(self.b, 1))
        wire.recv(self.slots_b[1], self.group(1, 0), place.device(self.b, 1))
        part = self.half(1, 0, 1)
        wire.send(self.slots_b[3], part, part, place.device(self.b, -1))
        self.spread(3)
        self.spread(1)

    def plane_far(self):
        place, wire = self.place, self.wire
        wire.recv(self.slots_b[2], self.half(2, 0, 0), place.device(self.b, -1))
        wire.recv(self.slots_b[3], self.half(2, 0, 1), place.device(self.b, 1))
        self.spread(2)

    def space_near(self, db):
        place, wire = self.place, self.wire
        slots = self.slots_c[db]
        wire.recv(slots[0], self.group(db, -1), place.device(self.c, -1))
        part = self.half(db, -1, 0)
        wire.send(slots[2], part, part, place.device(self.c, 1))
        wire.recv(slots[1], self.group(db, 1), place.device(self.c, 1))
        part = self.half(db, 1, 1)
        wire.send(slots[3], part, part, place.device(self.c, -1))
        self.over(db, 3)
        self.over(db, 1)

    def space_far(self, db):
        place, wire = self.place, self.wire
        slots = self.slots_c[db]
        wire.recv(slots[2], self.half(db, 2, 0), place.device(self.c, -1))
        wire.recv(slots[3], self.half(db, 2, 1), place.device(self.c, 1))
        self.over(db, 2)

    def other_core(self):
        place = self.place
        for db in (0, 3, 1, 2):
            for dc in (0, 3, 1, 2):
                self.wire.recv(
                    self.slots_p[db][dc],
                    self.group(db, dc, 1 - place.core),
                    place.device(flip=True),
                )


def add_into(dst, src, count):
    def body(i, carry):
        total = dst[i].astype(jnp.float32) + src[i].astype(jnp.float32)
        dst[i] = total.astype(dst.dtype)
        return carry

    lax.fori_loop(0, count, body, 0)


class Scatter:
    def __init__(self, wire, place, axis, piece, relay, near):
        self.wire, self.place, self.axis = wire, place, axis
        self.piece, self.relay, self.near = piece, relay, near
        self.slots = [wire.slot() for _ in range(6)]

    def open(self):
        w, p = self.wire, self.place
        up, down = p.device(self.axis, 1), p.device(self.axis, -1)
        w.send(self.slots[0], self.piece(2, 0), self.relay.at[0], up)
        w.send(self.slots[1], self.piece(2, 1), self.relay.at[1], down)
        w.send(self.slots[2], self.piece(1, 1), self.near.at[0, 1], up)
        w.send(self.slots[3], self.piece(-1, 0), self.near.at[1, 0], down)

    def pass_on(self, count):
        w, p = self.wire, self.place
        up, down = p.device(self.axis, 1), p.device(self.axis, -1)
        w.recv(self.slots[0], self.relay.at[0], down)
        add_into(self.piece(1, 0), self.relay.at[0], count)
        w.send(self.slots[4], self.piece(1, 0), self.near.at[0, 0], up)
        w.recv(self.slots[1], self.relay.at[1], up)
        add_into(self.piece(-1, 1), self.relay.at[1], count)
        w.send(self.slots[5], self.piece(-1, 1), self.near.at[1, 1], down)

    def close(self):
        w, p = self.wire, self.place
        up, down = p.device(self.axis, 1), p.device(self.axis, -1)
        w.recv(self.slots[2], self.near.at[0, 1], down)
        w.recv(self.slots[3], self.near.at[1, 0], up)
        w.recv(self.slots[4], self.near.at[0, 0], down)
        w.recv(self.slots[5], self.near.at[1, 1], up)


def slots_needed():
    class Count:
        def __init__(self):
            self.n = 0

        def slot(self):
            self.n += 1
            return self.n - 1

    return 7 + 3 * (3 + 4 + 16 + 16) + 12 + 3 * (6 + 6 + 3) + 7


def block_kernel(
    widths,
    att_ref,
    x_ref,
    wo_hbm,
    wgu_hbm,
    wd_hbm,
    attended_ref,
    layer_ref,
    wo,
    wgu,
    wd,
    s1,
    r1,
    g0,
    g1,
    g2,
    acc,
    squares,
    act,
    p0,
    p1,
    p2,
    o0,
    o1,
    o2,
    rc0,
    rc1,
    rc2,
    nc0,
    nc1,
    nc2,
    q0,
    q1,
    q2,
    rb0,
    rb1,
    rb2,
    nb0,
    nb1,
    nb2,
    ta0,
    ta1,
    ta2,
    ra0,
    ra1,
    ra2,
    mine_s,
    last,
    load_sem,
    send_sem,
    recv_sem,
):
    place = Place()
    t, core = place.t, place.core
    ff = wd.shape[0]
    cols = sum(widths)
    starts = (0, widths[0], widths[0] + widths[1])
    wire = Wire(send_sem, recv_sem)
    barrier, peers = greet(place)
    loads = [
        pltpu.make_async_copy(src, dst, load_sem.at[i])
        for i, (src, dst) in enumerate(((wo_hbm, wo), (wgu_hbm, wgu), (wd_hbm, wd)))
    ]
    for load in loads:
        load.start()
    loads[0].wait()

    def columns(index, start=0, size=cols):
        return pl.ds(pl.multiple_of(index * cols + start, 128), size)

    slots1 = [wire.slot() for _ in range(7)]
    heads = att_ref[...]
    own = None
    for j in (4, 3, 5, 2, 6, 1, 7, 0):
        to = lax.rem(t + j, 8)
        part = jnp.dot(heads, wo[:, columns(to)], preferred_element_type=jnp.float32)
        if j == 0:
            own = part
            break
        s1[j - 1] = part.astype(s1.dtype)
        if j == 4:
            pl.semaphore_wait(barrier, peers)
        wire.send(slots1[j - 1], s1.at[j - 1], r1.at[j - 1], {"seq": place.s, "tp": to})
    total = own + x_ref[:, columns(t)].astype(jnp.float32)
    for j in (1, 7, 2, 6, 3, 5, 4):
        wire.recv(slots1[j - 1], r1.at[j - 1], {"seq": place.s, "tp": lax.rem(t + 8 - j, 8)})
        total = total + r1[j - 1].astype(jnp.float32)
    mine = total.astype(jnp.bfloat16)
    mine_s[...] = mine

    gs = (g0, g1, g2)
    gathers = [Gather(wire, place, axes, buf) for axes, buf in zip(AXES, gs)]
    for g, w, start in zip(gathers, widths, starts):
        g.buf[core, place.at[g.c], place.at[g.b], place.at[g.a]] = mine[:, start : start + w]
        g.open()
    for g in gathers:
        g.line()
    for g in gathers:
        g.plane_near()
    for g in gathers:
        g.space_near(0)
    for g in gathers:
        g.plane_far()
    for db in (3, 1, 2):
        for g in gathers:
            g.space_near(db)
    for db in (0, 3, 1, 2):
        for g in gathers:
            g.space_far(db)
    for g in gathers:
        g.other_core()

    loads[1].wait()
    acc[...] = jnp.zeros_like(acc)
    squares[...] = jnp.zeros_like(squares)

    def rows_of(k, c, y):
        if k == 0:
            v = gs[0][c, :, :, y]
        elif k == 1:
            v = gs[1][c, y]
        else:
            v = jnp.stack(
                [jnp.stack([gs[2][c, x, y, z] for x in range(4)]) for z in range(4)]
            )
        return v.reshape(512, v.shape[-1])

    def up_body(i, carry):
        c, y = i // 4, i % 4
        tt = y * 2 + c
        for k in range(3):
            v = rows_of(k, c, y)
            w = wgu[columns(tt, starts[k], widths[k]), :]
            acc[...] += jnp.dot(v, w, preferred_element_type=jnp.float32)
            sq = None
            for n in range(widths[k] // 128):
                f = v[:, n * 128 : n * 128 + 128].astype(jnp.float32)
                sq = f * f if sq is None else sq + f * f
            squares[...] += sq
        return carry

    lax.fori_loop(0, 8, up_body, 0)

    def act_body(i, carry):
        rows = pl.ds(pl.multiple_of(i * 128, 128), 128)
        mean = jnp.sum(squares[rows, :], axis=-1, keepdims=True) / (8 * cols)
        r = lax.rsqrt(mean + norm_eps)
        gate = acc[rows, :ff] * r
        up = acc[rows, ff:] * r
        act[rows, :] = (gate / (1.0 + jnp.exp(-gate)) * up).astype(act.dtype)
        return carry

    lax.fori_loop(0, 4, act_body, 0)
    loads[2].wait()

    ps, os_ = (p0, p1, p2), (o0, o1, o2)

    def at_y(k, ref, y):
        return ref.at[:, :, y] if k == 0 else (ref.at[y] if k == 1 else ref.at[:, y])

    def down_rows(tt, z):
        rows = act[pl.ds(pl.multiple_of(z * 128, 128), 128), :]
        return jnp.dot(rows, wd[:, columns(tt)], preferred_element_type=jnp.float32)

    slots_o = [[wire.slot() for _ in range(3)] for _ in range(4)]
    for y in range(4):

        def other_body(z, carry):
            d = down_rows(y * 2 + 1 - core, z).astype(jnp.bfloat16).reshape(4, 32, cols)
            ps[0][1 - core, z, :, y] = d[:, :, : widths[0]]
            ps[1][1 - core, y, z] = d[:, :, starts[1] : starts[2]]
            for x in range(4):
                ps[2][1 - core, x, y, z] = d[x, :, starts[2] :]
            return carry

        lax.fori_loop(0, 4, other_body, 0)
        for k in range(3):
            wire.send(
                slots_o[y][k],
                at_y(k, ps[k].at[1 - core], y),
                at_y(k, os_[k], y),
                place.device(flip=True),
            )
    for y in range(4):
        for k in range(3):
            wire.recv(slots_o[y][k], at_y(k, os_[k], y), place.device(flip=True))

        def own_body(z, carry):
            d = down_rows(y * 2 + core, z).reshape(4, 32, cols)
            d0 = d[:, :, : widths[0]] + os_[0][z, :, y].astype(jnp.float32)
            ps[0][core, z, :, y] = d0.astype(jnp.bfloat16)
            d1 = d[:, :, starts[1] : starts[2]] + os_[1][y, z].astype(jnp.float32)
            ps[1][core, y, z] = d1.astype(jnp.bfloat16)
            for x in range(4):
                d2 = d[x, :, starts[2] :] + os_[2][x, y, z].astype(jnp.float32)
                ps[2][core, x, y, z] = d2.astype(jnp.bfloat16)
            return carry

        lax.fori_loop(0, 4, own_body, 0)

    rcs, ncs, qs = (rc0, rc1, rc2), (nc0, nc1, nc2), (q0, q1, q2)
    rbs, nbs, tas, ras = (rb0, rb1, rb2), (nb0, nb1, nb2), (ta0, ta1, ta2), (ra0, ra1, ra2)

    def piece_c(k):
        def view(d, half):
            at = place.shifted(AXES[k][2], d)
            return ps[k].at[core, at, pl.ds(2 * half, 2)]

        return view

    def piece_b(k):
        def view(d, half):
            at = place.shifted(AXES[k][1], d)
            return qs[k].at[at, pl.ds(2 * half, 2)]

        return view

    along_c = [
        Scatter(wire, place, AXES[k][2], piece_c(k), rcs[k], ncs[k]) for k in range(3)
    ]
    along_b = [
        Scatter(wire, place, AXES[k][1], piece_b(k), rbs[k], nbs[k]) for k in range(3)
    ]
    slots_a = [[wire.slot() for _ in range(3)] for _ in range(3)]
    for s in along_c:
        s.open()
    for s in along_c:
        s.pass_on(2)
    for k, s in enumerate(along_c):
        s.close()
        at = place.at[AXES[k][2]]

        def sum_c(b, carry):
            v = ps[k][core, at, b].astype(jnp.float32)
            v = v + ncs[k][0, b // 2, b % 2].astype(jnp.float32)
            v = v + ncs[k][1, b // 2, b % 2].astype(jnp.float32)
            qs[k][b] = v.astype(jnp.bfloat16)
            return carry

        lax.fori_loop(0, 4, sum_c, 0)
        along_b[k].open()
    for s in along_b:
        s.pass_on(2)
    for k, s in enumerate(along_b):
        s.close()
        at = place.at[AXES[k][1]]
        for a in range(4):
            v = qs[k][at, a].astype(jnp.float32)
            v = v + nbs[k][0, a // 2, a % 2].astype(jnp.float32)
            v = v + nbs[k][1, a // 2, a % 2].astype(jnp.float32)
            tas[k][a] = v.astype(jnp.bfloat16)
        for j in (2, 1, 3):
            axis = AXES[k][0]
            wire.send(
                slots_a[k][j - 1],
                tas[k].at[place.shifted(axis, j)],
                ras[k].at[j - 1],
                place.device(axis, j),
            )
    for k in range(3):
        axis = AXES[k][0]
        v = tas[k][place.at[axis]].astype(jnp.float32)
        for j in (1, 3, 2):
            wire.recv(slots_a[k][j - 1], ras[k].at[j - 1], place.device(axis, -j))
            v = v + ras[k][j - 1].astype(jnp.float32)
        lo = starts[k]
        v = v + mine_s[:, lo : lo + widths[k]].astype(jnp.float32)
        last[t, :, lo : lo + widths[k]] = v.astype(jnp.bfloat16)
    slots_l = [wire.slot() for _ in range(7)]
    for j in (4, 3, 5, 2, 6, 1, 7):
        to = {"seq": place.s, "tp": lax.rem(t + j, 8)}
        wire.send(slots_l[j - 1], last.at[t], last.at[t], to)
    for y in range(4):
        for c in range(2):
            tt = y * 2 + c
            z, x = place.at["z"], place.at["x"]
            attended_ref[:, tt * cols : tt * cols + widths[0]] = g0[c, z, x, y]
            attended_ref[:, tt * cols + starts[1] : tt * cols + starts[2]] = g1[c, y, z, x]
            attended_ref[:, tt * cols + starts[2] : tt * cols + cols] = g2[c, x, y, z]
    for j in range(1, 8):
        tt = lax.rem(t + 8 - j, 8)
        wire.recv(slots_l[j - 1], last.at[tt], {"seq": place.s, "tp": tt})
    for tt in range(8):
        layer_ref[:, tt * cols : tt * cols + cols] = last[tt]
    wire.drain()


def second_half(attention, x, w_output, w_gate_up, w_down):
    rows, width = x.shape
    cols = width // 8
    ff = w_down.shape[0]
    tiles = cols // 128
    first = -(-2 * tiles // 5)
    widths = (first * 128, first * 128, (tiles - 2 * first) * 128)
    assert rows == 32 and min(widths) > 0
    bf, f32 = jnp.bfloat16, jnp.float32
    vm = pltpu.VMEM

    def each(*shape):
        return [vm(shape + (rows, w), bf) for w in widths]

    count = slots_needed()
    scratch = [
        vm(w_output.shape, bf),
        vm(w_gate_up.shape, bf),
        vm(w_down.shape, bf),
        vm((7, rows, cols), bf),
        vm((7, rows, cols), bf),
        *each(2, 4, 4, 4),
        vm((512, 2 * ff), f32),
        vm((512, 128), f32),
        vm((512, ff), bf),
        *each(2, 4, 4, 4),
        *each(4, 4, 4),
        *each(2, 2, 4),
        *each(2, 2, 2, 4),
        *each(4, 4),
        *each(2, 2),
        *each(2, 2, 2),
        *each(4),
        *each(3),
        vm((rows, cols), bf),
        vm((8, rows, cols), bf),
        pltpu.SemaphoreType.DMA((3,)),
        pltpu.SemaphoreType.DMA((count,)),
        pltpu.SemaphoreType.DMA((count,)),
    ]
    whole = pl.BlockSpec(memory_space=pltpu.VMEM)
    hbm = pl.BlockSpec(memory_space=pl.ANY)
    out = jax.ShapeDtypeStruct((rows, width), bf)
    return pl.pallas_call(
        functools.partial(block_kernel, widths),
        out_shape=[out, out],
        in_specs=[whole, whole, hbm, hbm, hbm],
        out_specs=[whole, whole],
        scratch_shapes=scratch,
        compiler_params=pltpu.CompilerParams(
            collective_id=1, has_side_effects=True, vmem_limit_bytes=60 * 1024 * 1024
        ),
        name="second_half",
    )(attention, x, w_output, w_gate_up, w_down)


def local(
    token_inputs,
    attn_gain,
    w_query,
    key_projection,
    value_projection,
    w_output,
    mlp_gain,
    w_gate,
    w_up,
    w_down,
    key_cache,
    paged_value_cache,
    cache_lengths,
    page_request,
    page_number,
    request_slot,
):
    steps, row_count, width = token_inputs.shape
    seq = lax.axis_size("seq")
    total_rows = row_count * seq
    page_count, kv_local, page_size, head_dim = key_cache.shape
    group = w_query.shape[1] // head_dim
    scale = head_dim ** (-0.5)
    first_row = lax.axis_index("seq") * row_count
    own_rows = first_row + jnp.arange(row_count, dtype=jnp.int32)
    own_match = request_slot[None, :] == own_rows[:, None]
    row_lengths = jnp.sum(jnp.where(own_match, cache_lengths[None, :], 0), axis=1)
    page_live = page_request >= 0
    page_req = jnp.where(page_live, page_request, 0)
    req_match = page_req[:, None] == jnp.arange(total_rows, dtype=jnp.int32)[None, :]
    page_row = jnp.sum(jnp.where(req_match, request_slot[None, :], 0), axis=1)
    page_len = jnp.sum(jnp.where(req_match, cache_lengths[None, :], 0), axis=1)
    valid = jnp.where(page_live, jnp.clip(page_len - page_number * page_size, 0, page_size), 0)

    x = token_inputs.reshape(steps * row_count, width)
    normed = rms_norm(x, attn_gain).astype(jnp.bfloat16)
    position = (jnp.arange(steps, dtype=jnp.int32)[:, None] + row_lengths[None, :]).reshape(-1)
    cosine, sine = rotary_tables(position, head_dim)
    q = jnp.dot(normed, w_query, preferred_element_type=jnp.float32)
    q = rotate(q.reshape(-1, group, head_dim), cosine[:, None], sine[:, None])
    q = q.astype(jnp.bfloat16).reshape(steps, row_count, group, head_dim)
    fresh_k = rotate(
        jnp.dot(normed, key_projection, preferred_element_type=jnp.float32), cosine, sine
    )
    fresh_k = fresh_k.astype(jnp.bfloat16).reshape(steps, row_count, head_dim)
    fresh_v = jnp.dot(normed, value_projection, preferred_element_type=jnp.float32)
    fresh_v = fresh_v.astype(jnp.bfloat16).reshape(steps, row_count, head_dim)
    q = jnp.swapaxes(q, 0, 1).reshape(row_count, steps * group, head_dim)
    all_q = lax.all_gather(q, "seq", axis=0, tiled=True)
    part, lse = paged_attention(
        page_row, valid, all_q, key_cache[:, 0], paged_value_cache[:, 0]
    )
    part = lax.all_to_all(part.reshape(seq, row_count, steps * group, head_dim), "seq", 0, 0)
    lse = lax.all_to_all(lse.reshape(seq, row_count, head_dim), "seq", 0, 0)
    lse = lse[:, :, : steps * group]
    s = jnp.einsum("rqd,jrd->rqj", q, fresh_k, preferred_element_type=jnp.float32) * scale
    allowed = (
        jnp.arange(steps)[None, :] <= (jnp.arange(steps * group) // group)[:, None]
    )
    s = jnp.where(allowed[None], s, masked_low)
    recent_max = jnp.max(s, axis=-1)
    w = jnp.where(allowed[None], jnp.exp(s - recent_max[..., None]), 0.0)
    recent_sum = jnp.sum(w, axis=-1)
    recent_acc = jnp.einsum(
        "rqj,jrd->rqd", w.astype(jnp.bfloat16), fresh_v, preferred_element_type=jnp.float32
    )
    top = jnp.maximum(jnp.max(lse, axis=0), recent_max)
    factor = jnp.exp(lse - top[None])
    fresh_factor = jnp.exp(recent_max - top)
    total = jnp.sum(factor, axis=0) + recent_sum * fresh_factor
    acc = jnp.sum(part.astype(jnp.float32) * factor[..., None], axis=0)
    acc = acc + recent_acc * fresh_factor[..., None]
    attention = (acc / total[..., None]).astype(jnp.bfloat16)
    attention = jnp.swapaxes(attention.reshape(row_count, steps, group * head_dim), 0, 1)
    attention = attention.reshape(steps * row_count, group * head_dim)
    gain = mlp_gain[:, None]
    w_gate_up = jnp.concatenate([w_gate, w_up], axis=1).astype(jnp.float32) * gain
    w_gate_up = w_gate_up.astype(jnp.bfloat16)
    attended, layer_out = second_half(attention, x, w_output, w_gate_up, w_down)
    shape = (steps, row_count, width)
    return attended.reshape(shape), layer_out.reshape(shape)


def solution(mesh):
    in_specs = (
        P(None, "seq", None),
        P(),
        P(None, "tp"),
        P(None, "tp"),
        P(None, "tp"),
        P("tp", None),
        P(),
        P(None, ("seq", "tp")),
        P(None, ("seq", "tp")),
        P(("seq", "tp"), None),
        P("seq", "tp", None, None),
        P("seq", "tp", None, None),
        P(),
        P("seq"),
        P("seq"),
        P(),
    )
    out_specs = (P(None, "seq", None), P(None, "seq", None))
    return jax.shard_map(local, mesh=mesh, in_specs=in_specs, out_specs=out_specs, check_vma=False)
```

```python
import functools

import jax
import jax.numpy as jnp
from jax import lax
from jax.experimental import pallas as pl
from jax.experimental.pallas import tpu as pltpu
from jax.sharding import PartitionSpec as P

STEPS = 4
rope_theta = 100000000.0
norm_eps = 1e-05
masked_low = -1e30


def paged_kernel(
    pages, request_ref, number_ref, slot_ref, length_ref, q_ref, k_ref, v_ref, o_ref, lse_ref, m_s, l_s, acc_s
):
    step = pl.program_id(0)
    scale = k_ref.shape[-1] ** (-0.5)
    length = k_ref.shape[1]

    @pl.when(step == 0)
    def _():
        m_s[...] = jnp.full_like(m_s, masked_low)
        l_s[...] = jnp.zeros_like(l_s)
        acc_s[...] = jnp.zeros_like(acc_s)

    stats = []
    for i in range(pages):
        page = step * pages + i
        request = request_ref[page]
        live_page = request >= 0
        request = jnp.maximum(request, 0)
        row = slot_ref[request]
        valid = jnp.clip(length_ref[request] - number_ref[page] * length, 0, length)
        valid = jnp.where(live_page, valid, 0)
        q = q_ref[(row % 8) // 4, row // 8, row % 4]
        s = (
            lax.dot_general(
                q, k_ref[i], (((1,), (1,)), ((), ())), preferred_element_type=jnp.float32
            )
            * scale
        )
        live = lax.broadcasted_iota(jnp.int32, s.shape, 1) < valid
        s = jnp.where(live, s, masked_low)
        m = jnp.max(s, axis=-1, keepdims=True)
        w = jnp.where(live, jnp.exp(s - m), 0.0)
        l = jnp.sum(w, axis=-1, keepdims=True)
        acc = jnp.dot(w.astype(jnp.bfloat16), v_ref[i], preferred_element_type=jnp.float32)
        stats.append((row, m, l, acc))
    for row, m, l, acc in stats:
        m_old = m_s[row]
        m_new = jnp.maximum(m_old, m)
        a_old = jnp.exp(m_old - m_new)
        a_new = jnp.exp(m - m_new)
        m_s[row] = m_new
        l_s[row] = l_s[row] * a_old + l * a_new
        acc_s[row] = acc_s[row] * a_old + acc * a_new

    @pl.when(step == pl.num_programs(0) - 1)
    def _():
        l = l_s[...]
        safe = jnp.where(l > 0.0, l, 1.0)
        o_ref[...] = (acc_s[...] / safe).astype(o_ref.dtype)
        lse = jnp.where(l > 0.0, m_s[...] + jnp.log(safe), masked_low)
        lse_ref[...] = compact(lse)


def compact(values):
    eye = lax.broadcasted_iota(jnp.int32, values.shape, 1) == lax.broadcasted_iota(
        jnp.int32, values.shape, 2
    )
    return jnp.sum(jnp.where(eye, values, 0.0), axis=1)


def expand(values, count):
    shape = (values.shape[0], count, values.shape[1])
    eye = lax.broadcasted_iota(jnp.int32, shape, 1) == lax.broadcasted_iota(jnp.int32, shape, 2)
    wide = jnp.broadcast_to(values[:, None, :], shape)
    return jnp.sum(jnp.where(eye, wide, 0.0), axis=-1, keepdims=True)


def paged_attention(request, number, slot, lengths, queries, keys, values):
    group, dim = queries.shape[-2:]
    total = slot.shape[0]
    count, _, length, _ = keys.shape
    pages = next(n for n in (6, 4, 3, 2, 1) if count % n == 0)
    paged = pl.BlockSpec((pages, None, length, dim), lambda i, *_: (i, 0, 0, 0))
    return pl.pallas_call(
        functools.partial(paged_kernel, pages),
        grid_spec=pltpu.PrefetchScalarGridSpec(
            num_scalar_prefetch=4,
            grid=(count // pages,),
            in_specs=[
                pl.BlockSpec(queries.shape, lambda i, *_: (0, 0, 0, 0, 0)),
                paged,
                paged,
            ],
            out_specs=[
                pl.BlockSpec((total, group, dim), lambda i, *_: (0, 0, 0)),
                pl.BlockSpec((total, dim), lambda i, *_: (0, 0)),
            ],
            scratch_shapes=[
                pltpu.VMEM((total, group, dim), jnp.float32),
                pltpu.VMEM((total, group, dim), jnp.float32),
                pltpu.VMEM((total, group, dim), jnp.float32),
            ],
        ),
        out_shape=[
            jax.ShapeDtypeStruct((total, group, dim), jnp.bfloat16),
            jax.ShapeDtypeStruct((total, dim), jnp.float32),
        ],
        name="paged_attention",
    )(request, number, slot, lengths, queries, keys, values)


AXES = (("y", "x", "z"), ("x", "z", "y"), ("z", "y", "x"))
MESH = pl.DeviceIdType.MESH


class Place:
    def __init__(self):
        s = lax.axis_index("seq")
        t = lax.axis_index("tp")
        self.at = {"z": s // 4, "x": s % 4, "y": t // 2}
        self.core = t % 2
        self.s = s
        self.t = t

    def shifted(self, axis, by):
        return lax.rem(self.at[axis] + (by + 4), 4)

    def device(self, axis=None, by=0, flip=False):
        at = dict(self.at)
        if axis is not None:
            at[axis] = self.shifted(axis, by)
        core = 1 - self.core if flip else self.core
        return {"seq": at["z"] * 4 + at["x"], "tp": at["y"] * 2 + core}


class Wire:
    def __init__(self, send_sem, recv_sem):
        self.send_sem = send_sem
        self.recv_sem = recv_sem
        self.used = 0
        self.sent = []

    def slot(self):
        self.used += 1
        return self.used - 1

    def send(self, slot, src, dst, device):
        copy = pltpu.make_async_remote_copy(
            src_ref=src,
            dst_ref=dst,
            send_sem=self.send_sem.at[slot],
            recv_sem=self.recv_sem.at[slot],
            device_id=device,
            device_id_type=MESH,
        )
        copy.start()
        self.sent.append(copy)

    def recv(self, slot, dst, device):
        pltpu.make_async_remote_copy(
            src_ref=dst,
            dst_ref=dst,
            send_sem=self.send_sem.at[slot],
            recv_sem=self.recv_sem.at[slot],
            device_id=device,
            device_id_type=MESH,
        ).wait_recv()

    def drain(self):
        for copy in self.sent:
            copy.wait_send()


def greet(place):
    barrier = pltpu.get_barrier_semaphore()
    peers = [{"seq": place.s, "tp": lax.rem(place.t + j, 8)} for j in range(1, 8)]
    peers += [{"seq": seq_peer(place, j)[0], "tp": place.t} for j in SEQ_ORDER]
    for peer in peers:
        pl.semaphore_signal(barrier, inc=1, device_id=peer, device_id_type=MESH)
    return barrier, len(peers)


SEQ_ORDER = tuple(
    sorted(
        ((dz, dx) for dz in range(4) for dx in range(4) if (dz, dx) != (0, 0)),
        key=lambda d: -(min(d[0], 4 - d[0]) + min(d[1], 4 - d[1])),
    )
)


def seq_peer(place, by):
    on = place.shifted("z", by[0]) * 4 + place.shifted("x", by[1])
    back = place.shifted("z", -by[0]) * 4 + place.shifted("x", -by[1])
    return on, back


class Gather:
    def __init__(self, wire, place, axes, buf):
        self.wire, self.place, self.buf = wire, place, buf
        self.a, self.b, self.c = axes
        self.slots_a = [wire.slot() for _ in range(3)]
        self.slots_b = [wire.slot() for _ in range(4)]
        self.slots_c = [[wire.slot() for _ in range(4)] for _ in range(4)]
        self.slots_p = [[wire.slot() for _ in range(4)] for _ in range(4)]

    def group(self, db, dc, core=None):
        place = self.place
        core = place.core if core is None else core
        return self.buf.at[core, place.shifted(self.c, dc), place.shifted(self.b, db)]

    def half(self, db, dc, which):
        place = self.place
        return self.buf.at[
            place.core, place.shifted(self.c, dc), place.shifted(self.b, db), pl.ds(2 * which, 2)
        ]

    def block(self, da):
        place = self.place
        return self.buf.at[
            place.core, place.at[self.c], place.at[self.b], place.shifted(self.a, da)
        ]

    def open(self):
        mine = self.block(0)
        for j in (2, 1, 3):
            self.wire.send(self.slots_a[j - 1], mine, mine, self.place.device(self.a, j))

    def spread(self, db):
        mine = self.group(db, 0)
        slots = self.slots_c[db]
        self.wire.send(slots[0], mine, mine, self.place.device(self.c, 1))
        self.wire.send(slots[1], mine, mine, self.place.device(self.c, -1))
        self.over(db, 0)

    def over(self, db, dc):
        mine = self.group(db, dc)
        self.wire.send(self.slots_p[db][dc], mine, mine, self.place.device(flip=True))

    def line(self):
        for j in (1, 3, 2):
            self.wire.recv(self.slots_a[j - 1], self.block(-j), self.place.device(self.a, -j))
        mine = self.group(0, 0)
        self.wire.send(self.slots_b[0], mine, mine, self.place.device(self.b, 1))
        self.wire.send(self.slots_b[1], mine, mine, self.place.device(self.b, -1))
        self.spread(0)

    def plane_near(self):
        place, wire = self.place, self.wire
        wire.recv(self.slots_b[0], self.group(-1, 0), place.device(self.b, -1))
        part = self.half(-1, 0, 0)
        wire.send(self.slots_b[2], part, part, place.device(self.b, 1))
        wire.recv(self.slots_b[1], self.group(1, 0), place.device(self.b, 1))
        part = self.half(1, 0, 1)
        wire.send(self.slots_b[3], part, part, place.device(self.b, -1))
        self.spread(3)
        self.spread(1)

    def plane_far(self):
        place, wire = self.place, self.wire
        wire.recv(self.slots_b[2], self.half(2, 0, 0), place.device(self.b, -1))
        wire.recv(self.slots_b[3], self.half(2, 0, 1), place.device(self.b, 1))
        self.spread(2)

    def space_near(self, db):
        place, wire = self.place, self.wire
        slots = self.slots_c[db]
        wire.recv(slots[0], self.group(db, -1), place.device(self.c, -1))
        part = self.half(db, -1, 0)
        wire.send(slots[2], part, part, place.device(self.c, 1))
        wire.recv(slots[1], self.group(db, 1), place.device(self.c, 1))
        part = self.half(db, 1, 1)
        wire.send(slots[3], part, part, place.device(self.c, -1))
        self.over(db, 3)
        self.over(db, 1)

    def space_far(self, db):
        place, wire = self.place, self.wire
        slots = self.slots_c[db]
        wire.recv(slots[2], self.half(db, 2, 0), place.device(self.c, -1))
        wire.recv(slots[3], self.half(db, 2, 1), place.device(self.c, 1))
        self.over(db, 2)

    def other_core(self):
        place = self.place
        for db in (0, 3, 1, 2):
            for dc in (0, 3, 1, 2):
                self.wire.recv(
                    self.slots_p[db][dc],
                    self.group(db, dc, 1 - place.core),
                    place.device(flip=True),
                )


def add_into(dst, src, count):
    def body(i, carry):
        total = dst[i].astype(jnp.float32) + src[i].astype(jnp.float32)
        dst[i] = total.astype(dst.dtype)
        return carry

    lax.fori_loop(0, count, body, 0)


class Scatter:
    def __init__(self, wire, place, axis, piece, relay, near):
        self.wire, self.place, self.axis = wire, place, axis
        self.piece, self.relay, self.near = piece, relay, near
        self.slots = [wire.slot() for _ in range(6)]

    def open(self):
        w, p = self.wire, self.place
        up, down = p.device(self.axis, 1), p.device(self.axis, -1)
        w.send(self.slots[0], self.piece(2, 0), self.relay.at[0], up)
        w.send(self.slots[1], self.piece(2, 1), self.relay.at[1], down)
        w.send(self.slots[2], self.piece(1, 1), self.near.at[0, 1], up)
        w.send(self.slots[3], self.piece(-1, 0), self.near.at[1, 0], down)

    def pass_on(self, count):
        w, p = self.wire, self.place
        up, down = p.device(self.axis, 1), p.device(self.axis, -1)
        w.recv(self.slots[0], self.relay.at[0], down)
        add_into(self.piece(1, 0), self.relay.at[0], count)
        w.send(self.slots[4], self.piece(1, 0), self.near.at[0, 0], up)
        w.recv(self.slots[1], self.relay.at[1], up)
        add_into(self.piece(-1, 1), self.relay.at[1], count)
        w.send(self.slots[5], self.piece(-1, 1), self.near.at[1, 1], down)

    def close(self):
        w, p = self.wire, self.place
        up, down = p.device(self.axis, 1), p.device(self.axis, -1)
        w.recv(self.slots[2], self.near.at[0, 1], down)
        w.recv(self.slots[3], self.near.at[1, 0], up)
        w.recv(self.slots[4], self.near.at[0, 0], down)
        w.recv(self.slots[5], self.near.at[1, 1], up)


def slots_needed():
    return 30 + 7 + 3 * (3 + 4 + 16 + 16) + 12 + 3 * (6 + 6 + 3) + 7


def block_kernel(
    widths,
    part_ref,
    lse_ref,
    fresh_ref,
    fresh_lse_ref,
    x_ref,
    gain_ref,
    wo_hbm,
    wg_hbm,
    wu_hbm,
    wd_hbm,
    attended_ref,
    layer_ref,
    wo,
    wgu,
    wd,
    s1,
    r1,
    g0,
    g1,
    g2,
    acc,
    squares,
    act,
    p0,
    p1,
    p2,
    o0,
    o1,
    o2,
    rc0,
    rc1,
    rc2,
    nc0,
    nc1,
    nc2,
    q0,
    q1,
    q2,
    rb0,
    rb1,
    rb2,
    nb0,
    nb1,
    nb2,
    ta0,
    ta1,
    ta2,
    ra0,
    ra1,
    ra2,
    mine_s,
    last,
    parts,
    lses,
    att32,
    load_sem,
    send_sem,
    recv_sem,
):
    place = Place()
    t, core = place.t, place.core
    ff = wd.shape[0]
    cols = sum(widths)
    starts = (0, widths[0], widths[0] + widths[1])
    wire = Wire(send_sem, recv_sem)
    barrier, peers = greet(place)
    weights = (
        (wg_hbm, wgu.at[:, pl.ds(0, ff)]),
        (wu_hbm, wgu.at[:, pl.ds(ff, ff)]),
        (wo_hbm, wo),
        (wd_hbm, wd),
    )
    loads = [
        pltpu.make_async_copy(src, dst, load_sem.at[i]) for i, (src, dst) in enumerate(weights)
    ]
    for load in loads:
        load.start()

    def columns(index, start=0, size=cols):
        return pl.ds(pl.multiple_of(index * cols + start, 128), size)

    slots_e = [[wire.slot() for _ in range(2)] for _ in range(15)]
    pl.semaphore_wait(barrier, peers)
    for n, j in enumerate(SEQ_ORDER):
        to, _ = seq_peer(place, j)
        device = {"seq": to, "tp": t}
        wire.send(slots_e[n][0], part_ref.at[to], parts.at[n], device)
        wire.send(slots_e[n][1], lse_ref.at[to], lses.at[n], device)

    loads[0].wait()
    loads[1].wait()

    def gain_body(n, carry):
        rows = pl.ds(pl.multiple_of(n * 128, 128), 128)
        row = jnp.broadcast_to(gain_ref[pl.ds(n, 1), :], (128, 128))
        eye = lax.broadcasted_iota(jnp.int32, row.shape, 0) == lax.broadcasted_iota(
            jnp.int32, row.shape, 1
        )
        column = jnp.sum(jnp.where(eye, row, 0.0), axis=1, keepdims=True)
        wgu[rows, :] = (wgu[rows, :].astype(jnp.float32) * column).astype(wgu.dtype)
        return carry

    lax.fori_loop(0, wgu.shape[0] // 128, gain_body, 0)

    for n, j in enumerate(SEQ_ORDER):
        _, back = seq_peer(place, j)
        device = {"seq": back, "tp": t}
        wire.recv(slots_e[n][0], parts.at[n], device)
        wire.recv(slots_e[n][1], lses.at[n], device)
    count = part_ref.shape[2]
    sums = [lses[n] for n in range(15)] + [lse_ref[place.s], fresh_lse_ref[...]]
    top = functools.reduce(jnp.maximum, sums)
    sums = [jnp.exp(v - top) for v in sums]
    whole = functools.reduce(jnp.add, sums)
    attention = fresh_ref[...] * expand(sums[16] / whole, count)
    for n in range(15):
        attention += parts[n].astype(jnp.float32) * expand(sums[n] / whole, count)
    attention += part_ref[place.s].astype(jnp.float32) * expand(sums[15] / whole, count)
    att32[...] = attention
    per_step = count // STEPS
    heads = jnp.concatenate(
        [
            jnp.concatenate(
                [att32[:, i * per_step + g, :].astype(jnp.bfloat16) for g in range(per_step)],
                axis=1,
            )
            for i in range(STEPS)
        ],
        axis=0,
    )

    slots1 = [wire.slot() for _ in range(7)]
    loads[2].wait()
    own = None
    for j in (4, 3, 5, 2, 6, 1, 7, 0):
        to = lax.rem(t + j, 8)
        part = jnp.dot(heads, wo[:, columns(to)], preferred_element_type=jnp.float32)
        if j == 0:
            own = part
            break
        s1[j - 1] = part.astype(s1.dtype)
        wire.send(slots1[j - 1], s1.at[j - 1], r1.at[j - 1], {"seq": place.s, "tp": to})
    total = own + x_ref[:, columns(t)].astype(jnp.float32)
    for j in (1, 7, 2, 6, 3, 5, 4):
        wire.recv(slots1[j - 1], r1.at[j - 1], {"seq": place.s, "tp": lax.rem(t + 8 - j, 8)})
        total = total + r1[j - 1].astype(jnp.float32)
    mine = total.astype(jnp.bfloat16)
    mine_s[...] = mine

    gs = (g0, g1, g2)
    gathers = [Gather(wire, place, axes, buf) for axes, buf in zip(AXES, gs)]
    for g, w, start in zip(gathers, widths, starts):
        g.buf[core, place.at[g.c], place.at[g.b], place.at[g.a]] = mine[:, start : start + w]
        g.open()
    for g in gathers:
        g.line()
    for g in gathers:
        g.plane_near()
    for g in gathers:
        g.space_near(0)
    for g in gathers:
        g.plane_far()
    for db in (3, 1, 2):
        for g in gathers:
            g.space_near(db)
    for db in (0, 3, 1, 2):
        for g in gathers:
            g.space_far(db)
    for g in gathers:
        g.other_core()

    acc[...] = jnp.zeros_like(acc)
    squares[...] = jnp.zeros_like(squares)

    def rows_of(k, c, y):
        if k == 0:
            v = gs[0][c, :, :, y]
        elif k == 1:
            v = gs[1][c, y]
        else:
            v = jnp.stack(
                [jnp.stack([gs[2][c, x, y, z] for x in range(4)]) for z in range(4)]
            )
        return v.reshape(512, v.shape[-1])

    def up_body(i, carry):
        c, y = i // 4, i % 4
        tt = y * 2 + c
        for k in range(3):
            v = rows_of(k, c, y)
            w = wgu[columns(tt, starts[k], widths[k]), :]
            acc[...] += jnp.dot(v, w, preferred_element_type=jnp.float32)
            sq = None
            for n in range(widths[k] // 128):
                f = v[:, n * 128 : n * 128 + 128].astype(jnp.float32)
                sq = f * f if sq is None else sq + f * f
            squares[...] += sq
        return carry

    lax.fori_loop(0, 8, up_body, 0)

    def act_body(i, carry):
        rows = pl.ds(pl.multiple_of(i * 128, 128), 128)
        mean = jnp.sum(squares[rows, :], axis=-1, keepdims=True) / (8 * cols)
        r = lax.rsqrt(mean + norm_eps)
        gate = acc[rows, :ff] * r
        up = acc[rows, ff:] * r
        act[rows, :] = (gate / (1.0 + jnp.exp(-gate)) * up).astype(act.dtype)
        return carry

    lax.fori_loop(0, 4, act_body, 0)
    loads[3].wait()

    ps, os_ = (p0, p1, p2), (o0, o1, o2)

    def at_y(k, ref, y):
        return ref.at[:, :, y] if k == 0 else (ref.at[y] if k == 1 else ref.at[:, y])

    def down_rows(tt, z):
        rows = act[pl.ds(pl.multiple_of(z * 128, 128), 128), :]
        return jnp.dot(rows, wd[:, columns(tt)], preferred_element_type=jnp.float32)

    slots_o = [[wire.slot() for _ in range(3)] for _ in range(4)]
    for y in range(4):

        def other_body(z, carry):
            d = down_rows(y * 2 + 1 - core, z).astype(jnp.bfloat16).reshape(4, 32, cols)
            ps[0][1 - core, z, :, y] = d[:, :, : widths[0]]
            ps[1][1 - core, y, z] = d[:, :, starts[1] : starts[2]]
            for x in range(4):
                ps[2][1 - core, x, y, z] = d[x, :, starts[2] :]
            return carry

        lax.fori_loop(0, 4, other_body, 0)
        for k in range(3):
            wire.send(
                slots_o[y][k],
                at_y(k, ps[k].at[1 - core], y),
                at_y(k, os_[k], y),
                place.device(flip=True),
            )
    for y in range(4):
        for k in range(3):
            wire.recv(slots_o[y][k], at_y(k, os_[k], y), place.device(flip=True))

        def own_body(z, carry):
            d = down_rows(y * 2 + core, z).reshape(4, 32, cols)
            d0 = d[:, :, : widths[0]] + os_[0][z, :, y].astype(jnp.float32)
            ps[0][core, z, :, y] = d0.astype(jnp.bfloat16)
            d1 = d[:, :, starts[1] : starts[2]] + os_[1][y, z].astype(jnp.float32)
            ps[1][core, y, z] = d1.astype(jnp.bfloat16)
            for x in range(4):
                d2 = d[x, :, starts[2] :] + os_[2][x, y, z].astype(jnp.float32)
                ps[2][core, x, y, z] = d2.astype(jnp.bfloat16)
            return carry

        lax.fori_loop(0, 4, own_body, 0)

    rcs, ncs, qs = (rc0, rc1, rc2), (nc0, nc1, nc2), (q0, q1, q2)
    rbs, nbs, tas, ras = (rb0, rb1, rb2), (nb0, nb1, nb2), (ta0, ta1, ta2), (ra0, ra1, ra2)

    def piece_c(k):
        def view(d, half):
            at = place.shifted(AXES[k][2], d)
            return ps[k].at[core, at, pl.ds(2 * half, 2)]

        return view

    def piece_b(k):
        def view(d, half):
            at = place.shifted(AXES[k][1], d)
            return qs[k].at[at, pl.ds(2 * half, 2)]

        return view

    along_c = [
        Scatter(wire, place, AXES[k][2], piece_c(k), rcs[k], ncs[k]) for k in range(3)
    ]
    along_b = [
        Scatter(wire, place, AXES[k][1], piece_b(k), rbs[k], nbs[k]) for k in range(3)
    ]
    slots_a = [[wire.slot() for _ in range(3)] for _ in range(3)]
    for s in along_c:
        s.open()
    for s in along_c:
        s.pass_on(2)
    for k, s in enumerate(along_c):
        s.close()
        at = place.at[AXES[k][2]]

        def sum_c(b, carry):
            v = ps[k][core, at, b].astype(jnp.float32)
            v = v + ncs[k][0, b // 2, b % 2].astype(jnp.float32)
            v = v + ncs[k][1, b // 2, b % 2].astype(jnp.float32)
            qs[k][b] = v.astype(jnp.bfloat16)
            return carry

        lax.fori_loop(0, 4, sum_c, 0)
        along_b[k].open()
    for s in along_b:
        s.pass_on(2)
    for k, s in enumerate(along_b):
        s.close()
        at = place.at[AXES[k][1]]
        for a in range(4):
            v = qs[k][at, a].astype(jnp.float32)
            v = v + nbs[k][0, a // 2, a % 2].astype(jnp.float32)
            v = v + nbs[k][1, a // 2, a % 2].astype(jnp.float32)
            tas[k][a] = v.astype(jnp.bfloat16)
        for j in (2, 1, 3):
            axis = AXES[k][0]
            wire.send(
                slots_a[k][j - 1],
                tas[k].at[place.shifted(axis, j)],
                ras[k].at[j - 1],
                place.device(axis, j),
            )
    for k in range(3):
        axis = AXES[k][0]
        v = tas[k][place.at[axis]].astype(jnp.float32)
        for j in (1, 3, 2):
            wire.recv(slots_a[k][j - 1], ras[k].at[j - 1], place.device(axis, -j))
            v = v + ras[k][j - 1].astype(jnp.float32)
        lo = starts[k]
        v = v + mine_s[:, lo : lo + widths[k]].astype(jnp.float32)
        last[t, :, lo : lo + widths[k]] = v.astype(jnp.bfloat16)
    slots_l = [wire.slot() for _ in range(7)]
    for j in (4, 3, 5, 2, 6, 1, 7):
        to = {"seq": place.s, "tp": lax.rem(t + j, 8)}
        wire.send(slots_l[j - 1], last.at[t], last.at[t], to)
    for y in range(4):
        for c in range(2):
            tt = y * 2 + c
            z, x = place.at["z"], place.at["x"]
            attended_ref[:, tt * cols : tt * cols + widths[0]] = g0[c, z, x, y]
            attended_ref[:, tt * cols + starts[1] : tt * cols + starts[2]] = g1[c, y, z, x]
            attended_ref[:, tt * cols + starts[2] : tt * cols + cols] = g2[c, x, y, z]
    for j in range(1, 8):
        tt = lax.rem(t + 8 - j, 8)
        wire.recv(slots_l[j - 1], last.at[tt], {"seq": place.s, "tp": tt})
    for tt in range(8):
        layer_ref[:, tt * cols : tt * cols + cols] = last[tt]
    wire.drain()


def second_half(part, lse, fresh, fresh_lse, x, gain, w_output, w_gate, w_up, w_down):
    rows, width = x.shape
    cols = width // 8
    ff = w_down.shape[0]
    tiles = cols // 128
    first = -(-2 * tiles // 5)
    widths = (first * 128, first * 128, (tiles - 2 * first) * 128)
    assert rows == 32 and min(widths) > 0
    bf, f32 = jnp.bfloat16, jnp.float32
    vm = pltpu.VMEM

    def each(*shape):
        return [vm(shape + (rows, w), bf) for w in widths]

    count = slots_needed()
    scratch = [
        vm(w_output.shape, bf),
        vm((width, 2 * ff), bf),
        vm(w_down.shape, bf),
        vm((7, rows, cols), bf),
        vm((7, rows, cols), bf),
        *each(2, 4, 4, 4),
        vm((512, 2 * ff), f32),
        vm((512, 128), f32),
        vm((512, ff), bf),
        *each(2, 4, 4, 4),
        *each(4, 4, 4),
        *each(2, 2, 4),
        *each(2, 2, 2, 4),
        *each(4, 4),
        *each(2, 2),
        *each(2, 2, 2),
        *each(4),
        *each(3),
        vm((rows, cols), bf),
        vm((8, rows, cols), bf),
        vm((15,) + part.shape[1:], bf),
        vm((15,) + lse.shape[1:], f32),
        vm(part.shape[1:], f32),
        pltpu.SemaphoreType.DMA((4,)),
        pltpu.SemaphoreType.DMA((count,)),
        pltpu.SemaphoreType.DMA((count,)),
    ]
    whole = pl.BlockSpec(memory_space=pltpu.VMEM)
    hbm = pl.BlockSpec(memory_space=pl.ANY)
    out = jax.ShapeDtypeStruct((rows, width), bf)
    return pl.pallas_call(
        functools.partial(block_kernel, widths),
        out_shape=[out, out],
        in_specs=[whole] * 6 + [hbm] * 4,
        out_specs=[whole, whole],
        scratch_shapes=scratch,
        compiler_params=pltpu.CompilerParams(
            collective_id=1, has_side_effects=True, vmem_limit_bytes=60 * 1024 * 1024
        ),
        name="second_half",
    )(part, lse, fresh, fresh_lse, x, gain, w_output, w_gate, w_up, w_down)


class QueryGather:
    def __init__(self, wire, place, axes, buf):
        self.wire, self.place, self.buf = wire, place, buf
        self.a, self.b = axes
        self.slots_a = [wire.slot() for _ in range(3)]
        self.slots_b = [wire.slot() for _ in range(4)]

    def cut(self, b, a):
        return self.buf.at[b, a] if self.b == "z" else self.buf.at[a, b]

    def block(self, da):
        return self.cut(self.place.at[self.b], self.place.shifted(self.a, da))

    def half(self, db, which):
        return self.cut(self.place.shifted(self.b, db), pl.ds(2 * which, 2))

    def group(self, db):
        return self.cut(self.place.shifted(self.b, db), pl.ds(0, 4))

    def open(self):
        mine = self.block(0)
        for j in (2, 1, 3):
            self.wire.send(self.slots_a[j - 1], mine, mine, self.place.device(self.a, j))

    def line(self):
        for j in (1, 3, 2):
            self.wire.recv(self.slots_a[j - 1], self.block(-j), self.place.device(self.a, -j))
        mine = self.group(0)
        self.wire.send(self.slots_b[0], mine, mine, self.place.device(self.b, 1))
        self.wire.send(self.slots_b[1], mine, mine, self.place.device(self.b, -1))

    def near(self):
        place, wire = self.place, self.wire
        wire.recv(self.slots_b[0], self.group(-1), place.device(self.b, -1))
        part = self.half(-1, 0)
        wire.send(self.slots_b[2], part, part, place.device(self.b, 1))
        wire.recv(self.slots_b[1], self.group(1), place.device(self.b, 1))
        part = self.half(1, 1)
        wire.send(self.slots_b[3], part, part, place.device(self.b, -1))

    def far(self):
        place, wire = self.place, self.wire
        wire.recv(self.slots_b[2], self.half(2, 0), place.device(self.b, -1))
        wire.recv(self.slots_b[3], self.half(2, 1), place.device(self.b, 1))


def project_kernel(
    x_ref,
    gain_ref,
    freq_ref,
    slot_ref,
    length_ref,
    wq_hbm,
    wk_hbm,
    wv_hbm,
    q_all,
    fresh_ref,
    fresh_lse_ref,
    wq,
    wk,
    wv,
    q32,
    load_sem,
    send_sem,
    recv_sem,
):
    place = Place()
    wire = Wire(send_sem, recv_sem)
    rows, width = x_ref.shape
    dim = wk.shape[1]
    heads = wq.shape[1] // dim
    steps = STEPS
    own = rows // steps
    barrier = pltpu.get_barrier_semaphore()
    for axis in ("x", "z"):
        for by in (1, 2, 3):
            pl.semaphore_signal(
                barrier, inc=1, device_id=place.device(axis, by), device_id_type=MESH
            )
    chunks = load_sem.shape[0]
    depth = width // chunks
    loads = []
    for i in range(chunks):
        part = pl.ds(i * depth, depth)
        loads.append(
            [
                pltpu.make_async_copy(src.at[part], dst.at[part], load_sem.at[i, n])
                for n, (src, dst) in enumerate(((wq_hbm, wq), (wk_hbm, wk), (wv_hbm, wv)))
            ]
        )
        for load in loads[-1]:
            load.start()
    x = x_ref[...].astype(jnp.float32)
    mean = jnp.mean(x * x, axis=-1, keepdims=True)
    normed = (x * lax.rsqrt(mean + norm_eps) * gain_ref[...]).astype(jnp.bfloat16)

    shape = (own, slot_ref.shape[1])
    mine = place.s * own + lax.broadcasted_iota(jnp.int32, shape, 0)
    length = jnp.where(slot_ref[...] == mine, length_ref[...].astype(jnp.float32), 0.0)
    length = jnp.sum(length, axis=-1, keepdims=True)
    position = jnp.concatenate([length + float(i) for i in range(steps)], axis=0)
    angle = position * freq_ref[...]
    cosine = jnp.cos(angle)
    sine = jnp.sin(angle)
    low = lax.broadcasted_iota(jnp.int32, angle.shape, 1) < dim // 2
    sine = jnp.where(low, -sine, sine)

    def rotate(v):
        return v * cosine + pltpu.roll(v, dim // 2, 1) * sine

    q = k = v = 0.0
    for i in range(chunks):
        for load in loads[i]:
            load.wait()
        lhs = normed[:, i * depth : (i + 1) * depth]
        part = pl.ds(i * depth, depth)
        q = q + jnp.dot(lhs, wq[part, :], preferred_element_type=jnp.float32)
        k = k + jnp.dot(lhs, wk[part, :], preferred_element_type=jnp.float32)
        v = v + jnp.dot(lhs, wv[part, :], preferred_element_type=jnp.float32)
    for g in range(heads):
        turned = rotate(q[:, g * dim : (g + 1) * dim])
        for i in range(steps):
            q32[:, i * heads + g, :] = turned[i * own : (i + 1) * own]
    queries = q32[...].astype(jnp.bfloat16)
    s_at = (place.at["z"], place.at["x"])
    half = own // 2
    for n in range(2):
        q_all[n, s_at[0], s_at[1]] = queries[n * half : (n + 1) * half]
    gathers = [
        QueryGather(wire, place, axes, q_all.at[n])
        for n, axes in enumerate((("x", "z"), ("z", "x")))
    ]
    pl.semaphore_wait(barrier, 6)
    for g in gathers:
        g.open()

    new_k = rotate(k).astype(jnp.bfloat16)
    new_v = v.astype(jnp.bfloat16)
    count = steps * heads
    flat = queries.reshape(own * count, dim)
    s = lax.dot_general(
        flat, new_k, (((1,), (1,)), ((), ())), preferred_element_type=jnp.float32
    ) * (dim**-0.5)
    r = lax.broadcasted_iota(jnp.int32, s.shape, 0)
    c = lax.broadcasted_iota(jnp.int32, s.shape, 1)
    allowed = (r // count == c % own) & (c // own <= (r % count) // heads)
    s = jnp.where(allowed, s, masked_low)
    top = jnp.max(s, axis=-1, keepdims=True)
    w = jnp.where(allowed, jnp.exp(s - top), 0.0)
    total = jnp.sum(w, axis=-1, keepdims=True)
    acc = jnp.dot(w.astype(jnp.bfloat16), new_v, preferred_element_type=jnp.float32)
    fresh_ref[...] = (acc / total).reshape(own, count, dim)
    lse = jnp.broadcast_to(top + jnp.log(total), (own * count, dim))
    fresh_lse_ref[...] = compact(lse.reshape(own, count, dim))

    for g in gathers:
        g.line()
    for g in gathers:
        g.near()
    for g in gathers:
        g.far()
    wire.drain()


def first_half(x, gain, slot, lengths, w_query, w_key, w_value):
    rows, width = x.shape
    dim = w_key.shape[1]
    count = STEPS * w_query.shape[1] // dim
    own = rows // STEPS
    bf, f32, vm = jnp.bfloat16, jnp.float32, pltpu.VMEM
    exponent = jnp.arange(dim // 2, dtype=f32) * (2.0 / dim)
    freq = rope_theta ** (-exponent)
    freq = jnp.concatenate([freq, freq])[None, :]
    whole = pl.BlockSpec(memory_space=pltpu.VMEM)
    hbm = pl.BlockSpec(memory_space=pl.ANY)
    return pl.pallas_call(
        project_kernel,
        out_shape=[
            jax.ShapeDtypeStruct((2, 4, 4, own // 2, count, dim), bf),
            jax.ShapeDtypeStruct((own, count, dim), f32),
            jax.ShapeDtypeStruct((own, dim), f32),
        ],
        in_specs=[whole] * 5 + [hbm] * 3,
        out_specs=[whole] * 3,
        scratch_shapes=[
            vm(w_query.shape, bf),
            vm(w_key.shape, bf),
            vm(w_value.shape, bf),
            vm((own, count, dim), f32),
            pltpu.SemaphoreType.DMA((8, 3)),
            pltpu.SemaphoreType.DMA((14,)),
            pltpu.SemaphoreType.DMA((14,)),
        ],
        compiler_params=pltpu.CompilerParams(
            collective_id=2, has_side_effects=True, vmem_limit_bytes=40 * 1024 * 1024
        ),
        name="first_half",
    )(x, gain[None, :], freq, slot[None, :], lengths[None, :], w_query, w_key, w_value)


def local(
    token_inputs,
    attn_gain,
    w_query,
    key_projection,
    value_projection,
    w_output,
    mlp_gain,
    w_gate,
    w_up,
    w_down,
    key_cache,
    paged_value_cache,
    cache_lengths,
    page_request,
    page_number,
    request_slot,
):
    steps, row_count, width = token_inputs.shape
    x = token_inputs.reshape(steps * row_count, width)
    queries, fresh, fresh_lse = first_half(
        x, attn_gain, request_slot, cache_lengths, w_query, key_projection, value_projection
    )
    count, dim = queries.shape[-2:]
    seq = lax.axis_size("seq")
    queries = queries.reshape(2, seq, row_count // 2, count, dim)
    part, lse = paged_attention(
        page_request,
        page_number,
        request_slot,
        cache_lengths,
        queries,
        key_cache,
        paged_value_cache,
    )
    attended, layer_out = second_half(
        part.reshape(seq, row_count, count, dim),
        lse.reshape(seq, row_count, dim),
        fresh,
        fresh_lse,
        x,
        mlp_gain.reshape(-1, 128),
        w_output,
        w_gate,
        w_up,
        w_down,
    )
    shape = (steps, row_count, width)
    return attended.reshape(shape), layer_out.reshape(shape)


def solution(mesh):
    in_specs = (
        P(None, "seq", None),
        P(),
        P(None, "tp"),
        P(None, "tp"),
        P(None, "tp"),
        P("tp", None),
        P(),
        P(None, ("seq", "tp")),
        P(None, ("seq", "tp")),
        P(("seq", "tp"), None),
        P("seq", "tp", None, None),
        P("seq", "tp", None, None),
        P(),
        P("seq"),
        P("seq"),
        P(),
    )
    out_specs = (P(None, "seq", None), P(None, "seq", None))
    return jax.shard_map(local, mesh=mesh, in_specs=in_specs, out_specs=out_specs, check_vma=False)
```

```python
import functools

import jax
import jax.numpy as jnp
from jax import lax
from jax.experimental import pallas as pl
from jax.experimental.pallas import tpu as pltpu
from jax.sharding import PartitionSpec as P

STEPS = 4
rope_theta = 100000000.0
norm_eps = 1e-05
masked_low = -1e30


def paged_kernel(
    pages, request_ref, number_ref, slot_ref, length_ref, q_ref, k_ref, v_ref, o_ref, lse_ref, m_s, l_s, acc_s
):
    step = pl.program_id(0)
    scale = k_ref.shape[-1] ** (-0.5)
    length = k_ref.shape[1]

    @pl.when(step == 0)
    def _():
        m_s[...] = jnp.full_like(m_s, masked_low)
        l_s[...] = jnp.zeros_like(l_s)
        acc_s[...] = jnp.zeros_like(acc_s)

    stats = []
    for i in range(pages):
        page = step * pages + i
        request = request_ref[page]
        live_page = request >= 0
        request = jnp.maximum(request, 0)
        row = slot_ref[request]
        valid = jnp.clip(length_ref[request] - number_ref[page] * length, 0, length)
        valid = jnp.where(live_page, valid, 0)
        q = q_ref[(row % 8) // 4, row // 8, row % 4]
        s = (
            lax.dot_general(
                q, k_ref[i], (((1,), (1,)), ((), ())), preferred_element_type=jnp.float32
            )
            * scale
        )
        live = lax.broadcasted_iota(jnp.int32, s.shape, 1) < valid
        s = jnp.where(live, s, masked_low)
        m = jnp.max(s, axis=-1, keepdims=True)
        w = jnp.where(live, jnp.exp(s - m), 0.0)
        l = jnp.sum(w, axis=-1, keepdims=True)
        acc = jnp.dot(w.astype(jnp.bfloat16), v_ref[i], preferred_element_type=jnp.float32)
        stats.append((row, m, l, acc))
    for row, m, l, acc in stats:
        m_old = m_s[row]
        m_new = jnp.maximum(m_old, m)
        a_old = jnp.exp(m_old - m_new)
        a_new = jnp.exp(m - m_new)
        m_s[row] = m_new
        l_s[row] = l_s[row] * a_old + l * a_new
        acc_s[row] = acc_s[row] * a_old + acc * a_new

    @pl.when(step == pl.num_programs(0) - 1)
    def _():
        l = l_s[...]
        safe = jnp.where(l > 0.0, l, 1.0)
        o_ref[...] = (acc_s[...] / safe).astype(o_ref.dtype)
        lse = jnp.where(l > 0.0, m_s[...] + jnp.log(safe), masked_low)
        lse_ref[...] = compact(lse)


def compact(values):
    eye = lax.broadcasted_iota(jnp.int32, values.shape, 1) == lax.broadcasted_iota(
        jnp.int32, values.shape, 2
    )
    return jnp.sum(jnp.where(eye, values, 0.0), axis=1)


def expand(values, count):
    shape = (values.shape[0], count, values.shape[1])
    eye = lax.broadcasted_iota(jnp.int32, shape, 1) == lax.broadcasted_iota(jnp.int32, shape, 2)
    wide = jnp.broadcast_to(values[:, None, :], shape)
    return jnp.sum(jnp.where(eye, wide, 0.0), axis=-1, keepdims=True)


def paged_attention(request, number, slot, lengths, queries, keys, values):
    group, dim = queries.shape[-2:]
    total = slot.shape[0]
    count, _, length, _ = keys.shape
    pages = next(n for n in (6, 4, 3, 2, 1) if count % n == 0)
    paged = pl.BlockSpec((pages, None, length, dim), lambda i, *_: (i, 0, 0, 0))
    return pl.pallas_call(
        functools.partial(paged_kernel, pages),
        grid_spec=pltpu.PrefetchScalarGridSpec(
            num_scalar_prefetch=4,
            grid=(count // pages,),
            in_specs=[
                pl.BlockSpec(queries.shape, lambda i, *_: (0, 0, 0, 0, 0)),
                paged,
                paged,
            ],
            out_specs=[
                pl.BlockSpec((total, group, dim), lambda i, *_: (0, 0, 0)),
                pl.BlockSpec((total, dim), lambda i, *_: (0, 0)),
            ],
            scratch_shapes=[
                pltpu.VMEM((total, group, dim), jnp.float32),
                pltpu.VMEM((total, group, dim), jnp.float32),
                pltpu.VMEM((total, group, dim), jnp.float32),
            ],
        ),
        out_shape=[
            jax.ShapeDtypeStruct((total, group, dim), jnp.bfloat16),
            jax.ShapeDtypeStruct((total, dim), jnp.float32),
        ],
        name="paged_attention",
    )(request, number, slot, lengths, queries, keys, values)


AXES = (("y", "x", "z"), ("x", "z", "y"), ("z", "y", "x"))
MESH = pl.DeviceIdType.MESH


class Place:
    def __init__(self):
        s = lax.axis_index("seq")
        t = lax.axis_index("tp")
        self.at = {"z": s // 4, "x": s % 4, "y": t // 2}
        self.core = t % 2
        self.s = s
        self.t = t

    def shifted(self, axis, by):
        return lax.rem(self.at[axis] + (by + 4), 4)

    def device(self, axis=None, by=0, flip=False):
        at = dict(self.at)
        if axis is not None:
            at[axis] = self.shifted(axis, by)
        core = 1 - self.core if flip else self.core
        return {"seq": at["z"] * 4 + at["x"], "tp": at["y"] * 2 + core}


class Wire:
    def __init__(self, send_sem, recv_sem):
        self.send_sem = send_sem
        self.recv_sem = recv_sem
        self.used = 0
        self.sent = []

    def slot(self):
        self.used += 1
        return self.used - 1

    def send(self, slot, src, dst, device):
        copy = pltpu.make_async_remote_copy(
            src_ref=src,
            dst_ref=dst,
            send_sem=self.send_sem.at[slot],
            recv_sem=self.recv_sem.at[slot],
            device_id=device,
            device_id_type=MESH,
        )
        copy.start()
        self.sent.append(copy)

    def recv(self, slot, dst, device):
        pltpu.make_async_remote_copy(
            src_ref=dst,
            dst_ref=dst,
            send_sem=self.send_sem.at[slot],
            recv_sem=self.recv_sem.at[slot],
            device_id=device,
            device_id_type=MESH,
        ).wait_recv()

    def drain(self):
        for copy in self.sent:
            copy.wait_send()


def greet(place):
    barrier = pltpu.get_barrier_semaphore()
    peers = [{"seq": place.s, "tp": lax.rem(place.t + j, 8)} for j in range(1, 8)]
    peers += [{"seq": seq_peer(place, j)[0], "tp": place.t} for j in SEQ_ORDER]
    for peer in peers:
        pl.semaphore_signal(barrier, inc=1, device_id=peer, device_id_type=MESH)
    return barrier, len(peers)


SEQ_ORDER = tuple(
    sorted(
        ((dz, dx) for dz in range(4) for dx in range(4) if (dz, dx) != (0, 0)),
        key=lambda d: -(min(d[0], 4 - d[0]) + min(d[1], 4 - d[1])),
    )
)


def seq_peer(place, by):
    on = place.shifted("z", by[0]) * 4 + place.shifted("x", by[1])
    back = place.shifted("z", -by[0]) * 4 + place.shifted("x", -by[1])
    return on, back


class Gather:
    def __init__(self, wire, place, axes, buf):
        self.wire, self.place, self.buf = wire, place, buf
        self.a, self.b, self.c = axes
        self.slots_a = [wire.slot() for _ in range(3)]
        self.slots_b = [wire.slot() for _ in range(3)]
        self.slots_c = [[wire.slot() for _ in range(4)] for _ in range(4)]
        self.slots_p = [[wire.slot() for _ in range(4)] for _ in range(4)]

    def group(self, db, dc, core=None):
        place = self.place
        core = place.core if core is None else core
        return self.buf.at[core, place.shifted(self.c, dc), place.shifted(self.b, db)]

    def half(self, db, dc, which):
        place = self.place
        return self.buf.at[
            place.core, place.shifted(self.c, dc), place.shifted(self.b, db), pl.ds(2 * which, 2)
        ]

    def block(self, da):
        place = self.place
        return self.buf.at[
            place.core, place.at[self.c], place.at[self.b], place.shifted(self.a, da)
        ]

    def open(self):
        mine = self.block(0)
        for j in (2, 1, 3):
            self.wire.send(self.slots_a[j - 1], mine, mine, self.place.device(self.a, j))

    def spread(self, db):
        mine = self.group(db, 0)
        slots = self.slots_c[db]
        self.wire.send(slots[0], mine, mine, self.place.device(self.c, 1))
        self.wire.send(slots[1], mine, mine, self.place.device(self.c, -1))
        self.over(db, 0)

    def over(self, db, dc):
        mine = self.group(db, dc)
        self.wire.send(self.slots_p[db][dc], mine, mine, self.place.device(flip=True))

    def line(self):
        for j in (1, 3, 2):
            self.wire.recv(self.slots_a[j - 1], self.block(-j), self.place.device(self.a, -j))
        mine = self.group(0, 0)
        for j in (2, 1, 3):
            self.wire.send(self.slots_b[j - 1], mine, mine, self.place.device(self.b, j))
        self.spread(0)

    def plane(self, j):
        self.wire.recv(self.slots_b[j - 1], self.group(-j, 0), self.place.device(self.b, -j))
        self.spread(4 - j)

    def space_near(self, db):
        place, wire = self.place, self.wire
        slots = self.slots_c[db]
        wire.recv(slots[0], self.group(db, -1), place.device(self.c, -1))
        part = self.half(db, -1, 0)
        wire.send(slots[2], part, part, place.device(self.c, 1))
        wire.recv(slots[1], self.group(db, 1), place.device(self.c, 1))
        part = self.half(db, 1, 1)
        wire.send(slots[3], part, part, place.device(self.c, -1))
        self.over(db, 3)
        self.over(db, 1)

    def space_far(self, db):
        place, wire = self.place, self.wire
        slots = self.slots_c[db]
        wire.recv(slots[2], self.half(db, 2, 0), place.device(self.c, -1))
        wire.recv(slots[3], self.half(db, 2, 1), place.device(self.c, 1))
        self.over(db, 2)

    def other_core(self):
        place = self.place
        for db in (0, 3, 1, 2):
            for dc in (0, 3, 1, 2):
                self.wire.recv(
                    self.slots_p[db][dc],
                    self.group(db, dc, 1 - place.core),
                    place.device(flip=True),
                )


def add_into(dst, src, count):
    def body(i, carry):
        total = dst[i].astype(jnp.float32) + src[i].astype(jnp.float32)
        dst[i] = total.astype(dst.dtype)
        return carry

    lax.fori_loop(0, count, body, 0)


class Scatter:
    def __init__(self, wire, place, axis, piece, relay, near):
        self.wire, self.place, self.axis = wire, place, axis
        self.piece, self.relay, self.near = piece, relay, near
        self.slots = [wire.slot() for _ in range(6)]

    def open(self):
        w, p = self.wire, self.place
        up, down = p.device(self.axis, 1), p.device(self.axis, -1)
        w.send(self.slots[0], self.piece(2, 0), self.relay.at[0], up)
        w.send(self.slots[1], self.piece(2, 1), self.relay.at[1], down)
        w.send(self.slots[2], self.piece(1, 1), self.near.at[0, 1], up)
        w.send(self.slots[3], self.piece(-1, 0), self.near.at[1, 0], down)

    def pass_on(self, count):
        w, p = self.wire, self.place
        up, down = p.device(self.axis, 1), p.device(self.axis, -1)
        w.recv(self.slots[0], self.relay.at[0], down)
        add_into(self.piece(1, 0), self.relay.at[0], count)
        w.send(self.slots[4], self.piece(1, 0), self.near.at[0, 0], up)
        w.recv(self.slots[1], self.relay.at[1], up)
        add_into(self.piece(-1, 1), self.relay.at[1], count)
        w.send(self.slots[5], self.piece(-1, 1), self.near.at[1, 1], down)

    def close(self):
        w, p = self.wire, self.place
        up, down = p.device(self.axis, 1), p.device(self.axis, -1)
        w.recv(self.slots[2], self.near.at[0, 1], down)
        w.recv(self.slots[3], self.near.at[1, 0], up)
        w.recv(self.slots[4], self.near.at[0, 0], down)
        w.recv(self.slots[5], self.near.at[1, 1], up)


def slots_needed():
    return 30 + 7 + 3 * (3 + 3 + 16 + 16) + 12 + 3 * (6 + 3 + 3) + 7


def block_kernel(
    widths,
    part_ref,
    lse_ref,
    fresh_ref,
    fresh_lse_ref,
    x_ref,
    gain_ref,
    wo_hbm,
    wg_hbm,
    wu_hbm,
    wd_hbm,
    attended_ref,
    layer_ref,
    wo,
    wgu,
    wd,
    s1,
    r1,
    g0,
    g1,
    g2,
    acc,
    squares,
    act,
    p0,
    p1,
    p2,
    o0,
    o1,
    o2,
    rc0,
    rc1,
    rc2,
    nc0,
    nc1,
    nc2,
    q0,
    q1,
    q2,
    nb0,
    nb1,
    nb2,
    ta0,
    ta1,
    ta2,
    ra0,
    ra1,
    ra2,
    mine_s,
    last,
    parts,
    lses,
    att32,
    load_sem,
    send_sem,
    recv_sem,
):
    place = Place()
    t, core = place.t, place.core
    ff = wd.shape[0]
    cols = sum(widths)
    starts = (0, widths[0], widths[0] + widths[1])
    wire = Wire(send_sem, recv_sem)
    barrier, peers = greet(place)
    weights = (
        (wg_hbm, wgu.at[:, pl.ds(0, ff)]),
        (wu_hbm, wgu.at[:, pl.ds(ff, ff)]),
        (wo_hbm, wo),
        (wd_hbm, wd),
    )
    loads = [
        pltpu.make_async_copy(src, dst, load_sem.at[i]) for i, (src, dst) in enumerate(weights)
    ]
    for load in loads:
        load.start()

    def columns(index, start=0, size=cols):
        return pl.ds(pl.multiple_of(index * cols + start, 128), size)

    slots_e = [[wire.slot() for _ in range(2)] for _ in range(15)]
    pl.semaphore_wait(barrier, peers)
    for n, j in enumerate(SEQ_ORDER):
        to, _ = seq_peer(place, j)
        device = {"seq": to, "tp": t}
        wire.send(slots_e[n][0], part_ref.at[to], parts.at[n], device)
        wire.send(slots_e[n][1], lse_ref.at[to], lses.at[n], device)

    loads[0].wait()
    loads[1].wait()

    def gain_body(n, carry):
        rows = pl.ds(pl.multiple_of(n * 128, 128), 128)
        row = jnp.broadcast_to(gain_ref[pl.ds(n, 1), :], (128, 128))
        eye = lax.broadcasted_iota(jnp.int32, row.shape, 0) == lax.broadcasted_iota(
            jnp.int32, row.shape, 1
        )
        column = jnp.sum(jnp.where(eye, row, 0.0), axis=1, keepdims=True)
        wgu[rows, :] = (wgu[rows, :].astype(jnp.float32) * column).astype(wgu.dtype)
        return carry

    lax.fori_loop(0, wgu.shape[0] // 128, gain_body, 0)

    for n, j in enumerate(SEQ_ORDER):
        _, back = seq_peer(place, j)
        device = {"seq": back, "tp": t}
        wire.recv(slots_e[n][0], parts.at[n], device)
        wire.recv(slots_e[n][1], lses.at[n], device)
    count = part_ref.shape[2]
    sums = [lses[n] for n in range(15)] + [lse_ref[place.s], fresh_lse_ref[...]]
    top = functools.reduce(jnp.maximum, sums)
    sums = [jnp.exp(v - top) for v in sums]
    whole = functools.reduce(jnp.add, sums)
    attention = fresh_ref[...] * expand(sums[16] / whole, count)
    for n in range(15):
        attention += parts[n].astype(jnp.float32) * expand(sums[n] / whole, count)
    attention += part_ref[place.s].astype(jnp.float32) * expand(sums[15] / whole, count)
    att32[...] = attention
    per_step = count // STEPS
    heads = jnp.concatenate(
        [
            jnp.concatenate(
                [att32[:, i * per_step + g, :].astype(jnp.bfloat16) for g in range(per_step)],
                axis=1,
            )
            for i in range(STEPS)
        ],
        axis=0,
    )

    slots1 = [wire.slot() for _ in range(7)]
    loads[2].wait()
    own = None
    for j in (4, 3, 5, 2, 6, 1, 7, 0):
        to = lax.rem(t + j, 8)
        part = jnp.dot(heads, wo[:, columns(to)], preferred_element_type=jnp.float32)
        if j == 0:
            own = part
            break
        s1[j - 1] = part.astype(s1.dtype)
        wire.send(slots1[j - 1], s1.at[j - 1], r1.at[j - 1], {"seq": place.s, "tp": to})
    total = own + x_ref[:, columns(t)].astype(jnp.float32)
    for j in (1, 7, 2, 6, 3, 5, 4):
        wire.recv(slots1[j - 1], r1.at[j - 1], {"seq": place.s, "tp": lax.rem(t + 8 - j, 8)})
        total = total + r1[j - 1].astype(jnp.float32)
    mine = total.astype(jnp.bfloat16)
    mine_s[...] = mine

    gs = (g0, g1, g2)
    gathers = [Gather(wire, place, axes, buf) for axes, buf in zip(AXES, gs)]
    for g, w, start in zip(gathers, widths, starts):
        g.buf[core, place.at[g.c], place.at[g.b], place.at[g.a]] = mine[:, start : start + w]
        g.open()
    for g in gathers:
        g.line()
    for j in (1, 3, 2):
        for g in gathers:
            g.plane(j)
    for db in (0, 3, 1, 2):
        for g in gathers:
            g.space_near(db)
    for db in (0, 3, 1, 2):
        for g in gathers:
            g.space_far(db)
    for g in gathers:
        g.other_core()

    acc[...] = jnp.zeros_like(acc)
    squares[...] = jnp.zeros_like(squares)

    def rows_of(k, c, y):
        if k == 0:
            v = gs[0][c, :, :, y]
        elif k == 1:
            v = gs[1][c, y]
        else:
            v = jnp.stack(
                [jnp.stack([gs[2][c, x, y, z] for x in range(4)]) for z in range(4)]
            )
        return v.reshape(512, v.shape[-1])

    def up_body(i, carry):
        c, y = i // 4, i % 4
        tt = y * 2 + c
        for k in range(3):
            v = rows_of(k, c, y)
            w = wgu[columns(tt, starts[k], widths[k]), :]
            acc[...] += jnp.dot(v, w, preferred_element_type=jnp.float32)
            sq = None
            for n in range(widths[k] // 128):
                f = v[:, n * 128 : n * 128 + 128].astype(jnp.float32)
                sq = f * f if sq is None else sq + f * f
            squares[...] += sq
        return carry

    lax.fori_loop(0, 8, up_body, 0)

    def act_body(i, carry):
        rows = pl.ds(pl.multiple_of(i * 128, 128), 128)
        mean = jnp.sum(squares[rows, :], axis=-1, keepdims=True) / (8 * cols)
        r = lax.rsqrt(mean + norm_eps)
        gate = acc[rows, :ff] * r
        up = acc[rows, ff:] * r
        act[rows, :] = (gate / (1.0 + jnp.exp(-gate)) * up).astype(act.dtype)
        return carry

    lax.fori_loop(0, 4, act_body, 0)
    loads[3].wait()

    ps, os_ = (p0, p1, p2), (o0, o1, o2)

    def at_y(k, ref, y):
        return ref.at[:, :, y] if k == 0 else (ref.at[y] if k == 1 else ref.at[:, y])

    def down_rows(tt, z):
        rows = act[pl.ds(pl.multiple_of(z * 128, 128), 128), :]
        return jnp.dot(rows, wd[:, columns(tt)], preferred_element_type=jnp.float32)

    slots_o = [[wire.slot() for _ in range(3)] for _ in range(4)]
    for y in range(4):

        def other_body(z, carry):
            d = down_rows(y * 2 + 1 - core, z).astype(jnp.bfloat16).reshape(4, 32, cols)
            ps[0][1 - core, z, :, y] = d[:, :, : widths[0]]
            ps[1][1 - core, y, z] = d[:, :, starts[1] : starts[2]]
            for x in range(4):
                ps[2][1 - core, x, y, z] = d[x, :, starts[2] :]
            return carry

        lax.fori_loop(0, 4, other_body, 0)
        for k in range(3):
            wire.send(
                slots_o[y][k],
                at_y(k, ps[k].at[1 - core], y),
                at_y(k, os_[k], y),
                place.device(flip=True),
            )
    for y in range(4):
        for k in range(3):
            wire.recv(slots_o[y][k], at_y(k, os_[k], y), place.device(flip=True))

        def own_body(z, carry):
            d = down_rows(y * 2 + core, z).reshape(4, 32, cols)
            d0 = d[:, :, : widths[0]] + os_[0][z, :, y].astype(jnp.float32)
            ps[0][core, z, :, y] = d0.astype(jnp.bfloat16)
            d1 = d[:, :, starts[1] : starts[2]] + os_[1][y, z].astype(jnp.float32)
            ps[1][core, y, z] = d1.astype(jnp.bfloat16)
            for x in range(4):
                d2 = d[x, :, starts[2] :] + os_[2][x, y, z].astype(jnp.float32)
                ps[2][core, x, y, z] = d2.astype(jnp.bfloat16)
            return carry

        lax.fori_loop(0, 4, own_body, 0)

    rcs, ncs, qs = (rc0, rc1, rc2), (nc0, nc1, nc2), (q0, q1, q2)
    nbs, tas, ras = (nb0, nb1, nb2), (ta0, ta1, ta2), (ra0, ra1, ra2)

    def piece_c(k):
        def view(d, half):
            at = place.shifted(AXES[k][2], d)
            return ps[k].at[core, at, pl.ds(2 * half, 2)]

        return view

    along_c = [
        Scatter(wire, place, AXES[k][2], piece_c(k), rcs[k], ncs[k]) for k in range(3)
    ]
    slots_b = [[wire.slot() for _ in range(3)] for _ in range(3)]
    slots_a = [[wire.slot() for _ in range(3)] for _ in range(3)]
    for s in along_c:
        s.open()
    for s in along_c:
        s.pass_on(2)
    for k, s in enumerate(along_c):
        s.close()
        at = place.at[AXES[k][2]]

        def sum_c(b, carry):
            v = ps[k][core, at, b].astype(jnp.float32)
            v = v + ncs[k][0, b // 2, b % 2].astype(jnp.float32)
            v = v + ncs[k][1, b // 2, b % 2].astype(jnp.float32)
            qs[k][b] = v.astype(jnp.bfloat16)
            return carry

        lax.fori_loop(0, 4, sum_c, 0)
        axis = AXES[k][1]
        for j in (2, 1, 3):
            wire.send(
                slots_b[k][j - 1],
                qs[k].at[place.shifted(axis, j)],
                nbs[k].at[j - 1],
                place.device(axis, j),
            )
    for k in range(3):
        axis = AXES[k][1]
        at = place.at[axis]
        for j in (1, 3, 2):
            wire.recv(slots_b[k][j - 1], nbs[k].at[j - 1], place.device(axis, -j))
        for a in range(4):
            v = qs[k][at, a].astype(jnp.float32)
            for j in range(3):
                v = v + nbs[k][j, a].astype(jnp.float32)
            tas[k][a] = v.astype(jnp.bfloat16)
        for j in (2, 1, 3):
            axis = AXES[k][0]
            wire.send(
                slots_a[k][j - 1],
                tas[k].at[place.shifted(axis, j)],
                ras[k].at[j - 1],
                place.device(axis, j),
            )
    for k in range(3):
        axis = AXES[k][0]
        v = tas[k][place.at[axis]].astype(jnp.float32)
        for j in (1, 3, 2):
            wire.recv(slots_a[k][j - 1], ras[k].at[j - 1], place.device(axis, -j))
            v = v + ras[k][j - 1].astype(jnp.float32)
        lo = starts[k]
        v = v + mine_s[:, lo : lo + widths[k]].astype(jnp.float32)
        last[t, :, lo : lo + widths[k]] = v.astype(jnp.bfloat16)
    slots_l = [wire.slot() for _ in range(7)]
    for j in (4, 3, 5, 2, 6, 1, 7):
        to = {"seq": place.s, "tp": lax.rem(t + j, 8)}
        wire.send(slots_l[j - 1], last.at[t], last.at[t], to)
    for y in range(4):
        for c in range(2):
            tt = y * 2 + c
            z, x = place.at["z"], place.at["x"]
            attended_ref[:, tt * cols : tt * cols + widths[0]] = g0[c, z, x, y]
            attended_ref[:, tt * cols + starts[1] : tt * cols + starts[2]] = g1[c, y, z, x]
            attended_ref[:, tt * cols + starts[2] : tt * cols + cols] = g2[c, x, y, z]
    for j in range(1, 8):
        tt = lax.rem(t + 8 - j, 8)
        wire.recv(slots_l[j - 1], last.at[tt], {"seq": place.s, "tp": tt})
    for tt in range(8):
        layer_ref[:, tt * cols : tt * cols + cols] = last[tt]
    wire.drain()


def second_half(part, lse, fresh, fresh_lse, x, gain, w_output, w_gate, w_up, w_down):
    rows, width = x.shape
    cols = width // 8
    ff = w_down.shape[0]
    tiles = cols // 128
    first = -(-2 * tiles // 5)
    widths = (first * 128, first * 128, (tiles - 2 * first) * 128)
    assert rows == 32 and min(widths) > 0
    bf, f32 = jnp.bfloat16, jnp.float32
    vm = pltpu.VMEM

    def each(*shape):
        return [vm(shape + (rows, w), bf) for w in widths]

    count = slots_needed()
    scratch = [
        vm(w_output.shape, bf),
        vm((width, 2 * ff), bf),
        vm(w_down.shape, bf),
        vm((7, rows, cols), bf),
        vm((7, rows, cols), bf),
        *each(2, 4, 4, 4),
        vm((512, 2 * ff), f32),
        vm((512, 128), f32),
        vm((512, ff), bf),
        *each(2, 4, 4, 4),
        *each(4, 4, 4),
        *each(2, 2, 4),
        *each(2, 2, 2, 4),
        *each(4, 4),
        *each(3, 4),
        *each(4),
        *each(3),
        vm((rows, cols), bf),
        vm((8, rows, cols), bf),
        vm((15,) + part.shape[1:], bf),
        vm((15,) + lse.shape[1:], f32),
        vm(part.shape[1:], f32),
        pltpu.SemaphoreType.DMA((4,)),
        pltpu.SemaphoreType.DMA((count,)),
        pltpu.SemaphoreType.DMA((count,)),
    ]
    whole = pl.BlockSpec(memory_space=pltpu.VMEM)
    hbm = pl.BlockSpec(memory_space=pl.ANY)
    out = jax.ShapeDtypeStruct((rows, width), bf)
    return pl.pallas_call(
        functools.partial(block_kernel, widths),
        out_shape=[out, out],
        in_specs=[whole] * 6 + [hbm] * 4,
        out_specs=[whole, whole],
        scratch_shapes=scratch,
        compiler_params=pltpu.CompilerParams(
            collective_id=1, has_side_effects=True, vmem_limit_bytes=63 * 1024 * 1024
        ),
        name="second_half",
    )(part, lse, fresh, fresh_lse, x, gain, w_output, w_gate, w_up, w_down)


class QueryGather:
    def __init__(self, wire, place, axes, buf):
        self.wire, self.place, self.buf = wire, place, buf
        self.a, self.b = axes
        self.slots_a = [wire.slot() for _ in range(3)]
        self.slots_b = [wire.slot() for _ in range(4)]

    def cut(self, b, a):
        return self.buf.at[b, a] if self.b == "z" else self.buf.at[a, b]

    def block(self, da):
        return self.cut(self.place.at[self.b], self.place.shifted(self.a, da))

    def half(self, db, which):
        return self.cut(self.place.shifted(self.b, db), pl.ds(2 * which, 2))

    def group(self, db):
        return self.cut(self.place.shifted(self.b, db), pl.ds(0, 4))

    def open(self):
        mine = self.block(0)
        for j in (2, 1, 3):
            self.wire.send(self.slots_a[j - 1], mine, mine, self.place.device(self.a, j))

    def line(self):
        for j in (1, 3, 2):
            self.wire.recv(self.slots_a[j - 1], self.block(-j), self.place.device(self.a, -j))
        mine = self.group(0)
        self.wire.send(self.slots_b[0], mine, mine, self.place.device(self.b, 1))
        self.wire.send(self.slots_b[1], mine, mine, self.place.device(self.b, -1))

    def near(self):
        place, wire = self.place, self.wire
        wire.recv(self.slots_b[0], self.group(-1), place.device(self.b, -1))
        part = self.half(-1, 0)
        wire.send(self.slots_b[2], part, part, place.device(self.b, 1))
        wire.recv(self.slots_b[1], self.group(1), place.device(self.b, 1))
        part = self.half(1, 1)
        wire.send(self.slots_b[3], part, part, place.device(self.b, -1))

    def far(self):
        place, wire = self.place, self.wire
        wire.recv(self.slots_b[2], self.half(2, 0), place.device(self.b, -1))
        wire.recv(self.slots_b[3], self.half(2, 1), place.device(self.b, 1))


def project_kernel(
    x_ref,
    gain_ref,
    freq_ref,
    slot_ref,
    length_ref,
    wq_hbm,
    wk_hbm,
    wv_hbm,
    q_all,
    fresh_ref,
    fresh_lse_ref,
    wq,
    wk,
    wv,
    q32,
    load_sem,
    send_sem,
    recv_sem,
):
    place = Place()
    wire = Wire(send_sem, recv_sem)
    rows, width = x_ref.shape
    dim = wk.shape[1]
    heads = wq.shape[1] // dim
    steps = STEPS
    own = rows // steps
    barrier = pltpu.get_barrier_semaphore()
    for axis in ("x", "z"):
        for by in (1, 2, 3):
            pl.semaphore_signal(
                barrier, inc=1, device_id=place.device(axis, by), device_id_type=MESH
            )
    chunks = load_sem.shape[0]
    depth = width // chunks
    loads = []
    for i in range(chunks):
        part = pl.ds(i * depth, depth)
        loads.append(
            [
                pltpu.make_async_copy(src.at[part], dst.at[part], load_sem.at[i, n])
                for n, (src, dst) in enumerate(((wq_hbm, wq), (wk_hbm, wk), (wv_hbm, wv)))
            ]
        )
        for load in loads[-1]:
            load.start()
    x = x_ref[...].astype(jnp.float32)
    mean = jnp.mean(x * x, axis=-1, keepdims=True)
    normed = (x * lax.rsqrt(mean + norm_eps) * gain_ref[...]).astype(jnp.bfloat16)

    shape = (own, slot_ref.shape[1])
    mine = place.s * own + lax.broadcasted_iota(jnp.int32, shape, 0)
    length = jnp.where(slot_ref[...] == mine, length_ref[...].astype(jnp.float32), 0.0)
    length = jnp.sum(length, axis=-1, keepdims=True)
    position = jnp.concatenate([length + float(i) for i in range(steps)], axis=0)
    angle = position * freq_ref[...]
    cosine = jnp.cos(angle)
    sine = jnp.sin(angle)
    low = lax.broadcasted_iota(jnp.int32, angle.shape, 1) < dim // 2
    sine = jnp.where(low, -sine, sine)

    def rotate(v):
        return v * cosine + pltpu.roll(v, dim // 2, 1) * sine

    q = k = v = 0.0
    for i in range(chunks):
        for load in loads[i]:
            load.wait()
        lhs = normed[:, i * depth : (i + 1) * depth]
        part = pl.ds(i * depth, depth)
        q = q + jnp.dot(lhs, wq[part, :], preferred_element_type=jnp.float32)
        k = k + jnp.dot(lhs, wk[part, :], preferred_element_type=jnp.float32)
        v = v + jnp.dot(lhs, wv[part, :], preferred_element_type=jnp.float32)
    for g in range(heads):
        turned = rotate(q[:, g * dim : (g + 1) * dim])
        for i in range(steps):
            q32[:, i * heads + g, :] = turned[i * own : (i + 1) * own]
    queries = q32[...].astype(jnp.bfloat16)
    s_at = (place.at["z"], place.at["x"])
    half = own // 2
    for n in range(2):
        q_all[n, s_at[0], s_at[1]] = queries[n * half : (n + 1) * half]
    gathers = [
        QueryGather(wire, place, axes, q_all.at[n])
        for n, axes in enumerate((("x", "z"), ("z", "x")))
    ]
    pl.semaphore_wait(barrier, 6)
    for g in gathers:
        g.open()

    new_k = rotate(k).astype(jnp.bfloat16)
    new_v = v.astype(jnp.bfloat16)
    count = steps * heads
    flat = queries.reshape(own * count, dim)
    s = lax.dot_general(
        flat, new_k, (((1,), (1,)), ((), ())), preferred_element_type=jnp.float32
    ) * (dim**-0.5)
    r = lax.broadcasted_iota(jnp.int32, s.shape, 0)
    c = lax.broadcasted_iota(jnp.int32, s.shape, 1)
    allowed = (r // count == c % own) & (c // own <= (r % count) // heads)
    s = jnp.where(allowed, s, masked_low)
    top = jnp.max(s, axis=-1, keepdims=True)
    w = jnp.where(allowed, jnp.exp(s - top), 0.0)
    total = jnp.sum(w, axis=-1, keepdims=True)
    acc = jnp.dot(w.astype(jnp.bfloat16), new_v, preferred_element_type=jnp.float32)
    fresh_ref[...] = (acc / total).reshape(own, count, dim)
    lse = jnp.broadcast_to(top + jnp.log(total), (own * count, dim))
    fresh_lse_ref[...] = compact(lse.reshape(own, count, dim))

    for g in gathers:
        g.line()
    for g in gathers:
        g.near()
    for g in gathers:
        g.far()
    wire.drain()


def first_half(x, gain, slot, lengths, w_query, w_key, w_value):
    rows, width = x.shape
    dim = w_key.shape[1]
    count = STEPS * w_query.shape[1] // dim
    own = rows // STEPS
    bf, f32, vm = jnp.bfloat16, jnp.float32, pltpu.VMEM
    exponent = jnp.arange(dim // 2, dtype=f32) * (2.0 / dim)
    freq = rope_theta ** (-exponent)
    freq = jnp.concatenate([freq, freq])[None, :]
    whole = pl.BlockSpec(memory_space=pltpu.VMEM)
    hbm = pl.BlockSpec(memory_space=pl.ANY)
    return pl.pallas_call(
        project_kernel,
        out_shape=[
            jax.ShapeDtypeStruct((2, 4, 4, own // 2, count, dim), bf),
            jax.ShapeDtypeStruct((own, count, dim), f32),
            jax.ShapeDtypeStruct((own, dim), f32),
        ],
        in_specs=[whole] * 5 + [hbm] * 3,
        out_specs=[whole] * 3,
        scratch_shapes=[
            vm(w_query.shape, bf),
            vm(w_key.shape, bf),
            vm(w_value.shape, bf),
            vm((own, count, dim), f32),
            pltpu.SemaphoreType.DMA((8, 3)),
            pltpu.SemaphoreType.DMA((14,)),
            pltpu.SemaphoreType.DMA((14,)),
        ],
        compiler_params=pltpu.CompilerParams(
            collective_id=2, has_side_effects=True, vmem_limit_bytes=63 * 1024 * 1024
        ),
        name="first_half",
    )(x, gain[None, :], freq, slot[None, :], lengths[None, :], w_query, w_key, w_value)


def local(
    token_inputs,
    attn_gain,
    w_query,
    key_projection,
    value_projection,
    w_output,
    mlp_gain,
    w_gate,
    w_up,
    w_down,
    key_cache,
    paged_value_cache,
    cache_lengths,
    page_request,
    page_number,
    request_slot,
):
    steps, row_count, width = token_inputs.shape
    x = token_inputs.reshape(steps * row_count, width)
    queries, fresh, fresh_lse = first_half(
        x, attn_gain, request_slot, cache_lengths, w_query, key_projection, value_projection
    )
    count, dim = queries.shape[-2:]
    seq = lax.axis_size("seq")
    queries = queries.reshape(2, seq, row_count // 2, count, dim)
    part, lse = paged_attention(
        page_request,
        page_number,
        request_slot,
        cache_lengths,
        queries,
        key_cache,
        paged_value_cache,
    )
    attended, layer_out = second_half(
        part.reshape(seq, row_count, count, dim),
        lse.reshape(seq, row_count, dim),
        fresh,
        fresh_lse,
        x,
        mlp_gain.reshape(-1, 128),
        w_output,
        w_gate,
        w_up,
        w_down,
    )
    shape = (steps, row_count, width)
    return attended.reshape(shape), layer_out.reshape(shape)


def solution(mesh):
    in_specs = (
        P(None, "seq", None),
        P(),
        P(None, "tp"),
        P(None, "tp"),
        P(None, "tp"),
        P("tp", None),
        P(),
        P(None, ("seq", "tp")),
        P(None, ("seq", "tp")),
        P(("seq", "tp"), None),
        P("seq", "tp", None, None),
        P("seq", "tp", None, None),
        P(),
        P("seq"),
        P("seq"),
        P(),
    )
    out_specs = (P(None, "seq", None), P(None, "seq", None))
    return jax.shard_map(local, mesh=mesh, in_specs=in_specs, out_specs=out_specs, check_vma=False)
```

```python
import functools

import jax
import jax.numpy as jnp
from jax import lax
from jax.experimental import pallas as pl
from jax.experimental.pallas import tpu as pltpu
from jax.sharding import PartitionSpec as P

STEPS = 4
rope_theta = 100000000.0
norm_eps = 1e-05
masked_low = -1e30


def paged_kernel(
    pages, request_ref, number_ref, slot_ref, length_ref, q_ref, k_ref, v_ref, o_ref, lse_ref, m_s, l_s, acc_s
):
    step = pl.program_id(0)
    scale = k_ref.shape[-1] ** (-0.5)
    length = k_ref.shape[1]

    @pl.when(step == 0)
    def _():
        m_s[...] = jnp.full_like(m_s, masked_low)
        l_s[...] = jnp.zeros_like(l_s)
        acc_s[...] = jnp.zeros_like(acc_s)

    stats = []
    for i in range(pages):
        page = step * pages + i
        request = request_ref[page]
        live_page = request >= 0
        request = jnp.maximum(request, 0)
        row = slot_ref[request]
        valid = jnp.clip(length_ref[request] - number_ref[page] * length, 0, length)
        valid = jnp.where(live_page, valid, 0)
        q = q_ref[(row % 8) // 4, row // 8, row % 4]
        s = (
            lax.dot_general(
                q, k_ref[i], (((1,), (1,)), ((), ())), preferred_element_type=jnp.float32
            )
            * scale
        )
        live = lax.broadcasted_iota(jnp.int32, s.shape, 1) < valid
        s = jnp.where(live, s, masked_low)
        m = jnp.max(s, axis=-1, keepdims=True)
        w = jnp.where(live, jnp.exp(s - m), 0.0)
        l = jnp.sum(w, axis=-1, keepdims=True)
        acc = jnp.dot(w.astype(jnp.bfloat16), v_ref[i], preferred_element_type=jnp.float32)
        stats.append((row, m, l, acc))
    for row, m, l, acc in stats:
        m_old = m_s[row]
        m_new = jnp.maximum(m_old, m)
        a_old = jnp.exp(m_old - m_new)
        a_new = jnp.exp(m - m_new)
        m_s[row] = m_new
        l_s[row] = l_s[row] * a_old + l * a_new
        acc_s[row] = acc_s[row] * a_old + acc * a_new

    @pl.when(step == pl.num_programs(0) - 1)
    def _():
        o_ref[...] = acc_s[...].astype(o_ref.dtype)
        lse_ref[...] = compact(m_s[...], l_s[...])


def compact(tops, sums):
    row = lax.broadcasted_iota(jnp.int32, tops.shape, 1)
    lane = lax.broadcasted_iota(jnp.int32, tops.shape, 2)
    count = tops.shape[1]
    picked = jnp.where(lane == row, tops, jnp.where(lane == row + count, sums, 0.0))
    return jnp.sum(picked, axis=1)


def expand(values, count):
    shape = (values.shape[0], count, values.shape[1])
    eye = lax.broadcasted_iota(jnp.int32, shape, 1) == lax.broadcasted_iota(jnp.int32, shape, 2)
    wide = jnp.broadcast_to(values[:, None, :], shape)
    return jnp.sum(jnp.where(eye, wide, 0.0), axis=-1, keepdims=True)


def paged_attention(request, number, slot, lengths, queries, keys, values):
    group, dim = queries.shape[-2:]
    total = slot.shape[0]
    count, _, length, _ = keys.shape
    pages = next(n for n in (12, 9, 6, 4, 3, 2, 1) if count % n == 0)
    paged = pl.BlockSpec((pages, None, length, dim), lambda i, *_: (i, 0, 0, 0))
    return pl.pallas_call(
        functools.partial(paged_kernel, pages),
        grid_spec=pltpu.PrefetchScalarGridSpec(
            num_scalar_prefetch=4,
            grid=(count // pages,),
            in_specs=[
                pl.BlockSpec(queries.shape, lambda i, *_: (0, 0, 0, 0, 0)),
                paged,
                paged,
            ],
            out_specs=[
                pl.BlockSpec((total, group, dim), lambda i, *_: (0, 0, 0)),
                pl.BlockSpec((total, dim), lambda i, *_: (0, 0)),
            ],
            scratch_shapes=[
                pltpu.VMEM((total, group, dim), jnp.float32),
                pltpu.VMEM((total, group, dim), jnp.float32),
                pltpu.VMEM((total, group, dim), jnp.float32),
            ],
        ),
        out_shape=[
            jax.ShapeDtypeStruct((total, group, dim), jnp.bfloat16),
            jax.ShapeDtypeStruct((total, dim), jnp.float32),
        ],
        name="paged_attention",
    )(request, number, slot, lengths, queries, keys, values)


AXES = (("y", "x", "z"), ("x", "z", "y"), ("z", "y", "x"))
MESH = pl.DeviceIdType.MESH


class Place:
    def __init__(self):
        s = lax.axis_index("seq")
        t = lax.axis_index("tp")
        self.at = {"z": s // 4, "x": s % 4, "y": t // 2}
        self.core = t % 2
        self.s = s
        self.t = t

    def shifted(self, axis, by):
        return lax.rem(self.at[axis] + (by + 4), 4)

    def device(self, axis=None, by=0, flip=False):
        at = dict(self.at)
        if axis is not None:
            at[axis] = self.shifted(axis, by)
        core = 1 - self.core if flip else self.core
        return {"seq": at["z"] * 4 + at["x"], "tp": at["y"] * 2 + core}


class Wire:
    def __init__(self, send_sem, recv_sem):
        self.send_sem = send_sem
        self.recv_sem = recv_sem
        self.used = 0
        self.sent = []

    def slot(self):
        self.used += 1
        return self.used - 1

    def send(self, slot, src, dst, device):
        copy = pltpu.make_async_remote_copy(
            src_ref=src,
            dst_ref=dst,
            send_sem=self.send_sem.at[slot],
            recv_sem=self.recv_sem.at[slot],
            device_id=device,
            device_id_type=MESH,
        )
        copy.start()
        self.sent.append(copy)

    def recv(self, slot, dst, device):
        pltpu.make_async_remote_copy(
            src_ref=dst,
            dst_ref=dst,
            send_sem=self.send_sem.at[slot],
            recv_sem=self.recv_sem.at[slot],
            device_id=device,
            device_id_type=MESH,
        ).wait_recv()

    def drain(self):
        for copy in self.sent:
            copy.wait_send()


def greet(place):
    barrier = pltpu.get_barrier_semaphore()
    peers = [{"seq": place.s, "tp": lax.rem(place.t + j, 8)} for j in range(1, 8)]
    peers += [{"seq": seq_peer(place, j)[0], "tp": place.t} for j in SEQ_ORDER]
    for peer in peers:
        pl.semaphore_signal(barrier, inc=1, device_id=peer, device_id_type=MESH)
    return barrier, len(peers)


SEQ_ORDER = tuple(
    sorted(
        ((dz, dx) for dz in range(4) for dx in range(4) if (dz, dx) != (0, 0)),
        key=lambda d: -(min(d[0], 4 - d[0]) + min(d[1], 4 - d[1])),
    )
)


def seq_peer(place, by):
    on = place.shifted("z", by[0]) * 4 + place.shifted("x", by[1])
    back = place.shifted("z", -by[0]) * 4 + place.shifted("x", -by[1])
    return on, back


class Gather:
    def __init__(self, wire, place, axes, buf):
        self.wire, self.place, self.buf = wire, place, buf
        self.a, self.b, self.c = axes
        self.slots_a = [wire.slot() for _ in range(3)]
        self.slots_b = [wire.slot() for _ in range(3)]
        self.slots_c = [[wire.slot() for _ in range(4)] for _ in range(4)]
        self.slots_p = [[wire.slot() for _ in range(4)] for _ in range(4)]

    def group(self, db, dc, core=None):
        place = self.place
        core = place.core if core is None else core
        return self.buf.at[core, place.shifted(self.c, dc), place.shifted(self.b, db)]

    def half(self, db, dc, which):
        place = self.place
        return self.buf.at[
            place.core, place.shifted(self.c, dc), place.shifted(self.b, db), pl.ds(2 * which, 2)
        ]

    def block(self, da):
        place = self.place
        return self.buf.at[
            place.core, place.at[self.c], place.at[self.b], place.shifted(self.a, da)
        ]

    def open(self):
        mine = self.block(0)
        for j in (2, 1, 3):
            self.wire.send(self.slots_a[j - 1], mine, mine, self.place.device(self.a, j))

    def spread(self, db):
        mine = self.group(db, 0)
        slots = self.slots_c[db]
        self.wire.send(slots[0], mine, mine, self.place.device(self.c, 1))
        self.wire.send(slots[1], mine, mine, self.place.device(self.c, -1))
        self.over(db, 0)

    def over(self, db, dc):
        mine = self.group(db, dc)
        self.wire.send(self.slots_p[db][dc], mine, mine, self.place.device(flip=True))

    def line(self):
        for j in (1, 3, 2):
            self.wire.recv(self.slots_a[j - 1], self.block(-j), self.place.device(self.a, -j))
        mine = self.group(0, 0)
        for j in (2, 1, 3):
            self.wire.send(self.slots_b[j - 1], mine, mine, self.place.device(self.b, j))
        self.spread(0)

    def plane(self, j):
        self.wire.recv(self.slots_b[j - 1], self.group(-j, 0), self.place.device(self.b, -j))
        self.spread(4 - j)

    def space_near(self, db):
        place, wire = self.place, self.wire
        slots = self.slots_c[db]
        wire.recv(slots[0], self.group(db, -1), place.device(self.c, -1))
        part = self.half(db, -1, 0)
        wire.send(slots[2], part, part, place.device(self.c, 1))
        wire.recv(slots[1], self.group(db, 1), place.device(self.c, 1))
        part = self.half(db, 1, 1)
        wire.send(slots[3], part, part, place.device(self.c, -1))
        self.over(db, 3)
        self.over(db, 1)

    def space_far(self, db):
        place, wire = self.place, self.wire
        slots = self.slots_c[db]
        wire.recv(slots[2], self.half(db, 2, 0), place.device(self.c, -1))
        wire.recv(slots[3], self.half(db, 2, 1), place.device(self.c, 1))
        self.over(db, 2)

    def other_core(self):
        place = self.place
        for db in (0, 3, 1, 2):
            for dc in (0, 3, 1, 2):
                self.wire.recv(
                    self.slots_p[db][dc],
                    self.group(db, dc, 1 - place.core),
                    place.device(flip=True),
                )


def add_into(dst, src, count):
    def body(i, carry):
        total = dst[i].astype(jnp.float32) + src[i].astype(jnp.float32)
        dst[i] = total.astype(dst.dtype)
        return carry

    lax.fori_loop(0, count, body, 0)


class Scatter:
    def __init__(self, wire, place, axis, piece, relay, near):
        self.wire, self.place, self.axis = wire, place, axis
        self.piece, self.relay, self.near = piece, relay, near
        self.slots = [wire.slot() for _ in range(6)]

    def open(self):
        w, p = self.wire, self.place
        up, down = p.device(self.axis, 1), p.device(self.axis, -1)
        w.send(self.slots[0], self.piece(2, 0), self.relay.at[0], up)
        w.send(self.slots[1], self.piece(2, 1), self.relay.at[1], down)
        w.send(self.slots[2], self.piece(1, 1), self.near.at[0, 1], up)
        w.send(self.slots[3], self.piece(-1, 0), self.near.at[1, 0], down)

    def pass_on(self, count):
        w, p = self.wire, self.place
        up, down = p.device(self.axis, 1), p.device(self.axis, -1)
        w.recv(self.slots[0], self.relay.at[0], down)
        add_into(self.piece(1, 0), self.relay.at[0], count)
        w.send(self.slots[4], self.piece(1, 0), self.near.at[0, 0], up)
        w.recv(self.slots[1], self.relay.at[1], up)
        add_into(self.piece(-1, 1), self.relay.at[1], count)
        w.send(self.slots[5], self.piece(-1, 1), self.near.at[1, 1], down)

    def close(self):
        w, p = self.wire, self.place
        up, down = p.device(self.axis, 1), p.device(self.axis, -1)
        w.recv(self.slots[2], self.near.at[0, 1], down)
        w.recv(self.slots[3], self.near.at[1, 0], up)
        w.recv(self.slots[4], self.near.at[0, 0], down)
        w.recv(self.slots[5], self.near.at[1, 1], up)


def slots_needed():
    return 30 + 7 + 3 * (3 + 3 + 16 + 16) + 12 + 3 * (6 + 3 + 3) + 7


def block_kernel(
    widths,
    part_ref,
    lse_ref,
    fresh_ref,
    fresh_lse_ref,
    x_ref,
    gain_ref,
    wo_hbm,
    wg_hbm,
    wu_hbm,
    wd_hbm,
    attended_ref,
    layer_ref,
    wo,
    wgu,
    wd,
    s1,
    r1,
    g0,
    g1,
    g2,
    acc,
    squares,
    act,
    p0,
    p1,
    p2,
    o0,
    o1,
    o2,
    rc0,
    rc1,
    rc2,
    nc0,
    nc1,
    nc2,
    q0,
    q1,
    q2,
    nb0,
    nb1,
    nb2,
    ta0,
    ta1,
    ta2,
    ra0,
    ra1,
    ra2,
    mine_s,
    last,
    parts,
    lses,
    att32,
    load_sem,
    send_sem,
    recv_sem,
):
    place = Place()
    t, core = place.t, place.core
    ff = wd.shape[0]
    cols = sum(widths)
    starts = (0, widths[0], widths[0] + widths[1])
    wire = Wire(send_sem, recv_sem)
    barrier, peers = greet(place)
    weights = (
        (wg_hbm, wgu.at[:, pl.ds(0, ff)]),
        (wu_hbm, wgu.at[:, pl.ds(ff, ff)]),
        (wo_hbm, wo),
        (wd_hbm, wd),
    )
    loads = [
        pltpu.make_async_copy(src, dst, load_sem.at[i]) for i, (src, dst) in enumerate(weights)
    ]
    for load in loads:
        load.start()

    def columns(index, start=0, size=cols):
        return pl.ds(pl.multiple_of(index * cols + start, 128), size)

    slots_e = [[wire.slot() for _ in range(2)] for _ in range(15)]
    pl.semaphore_wait(barrier, peers)
    for n, j in enumerate(SEQ_ORDER):
        to, _ = seq_peer(place, j)
        device = {"seq": to, "tp": t}
        wire.send(slots_e[n][0], part_ref.at[to], parts.at[n], device)
        wire.send(slots_e[n][1], lse_ref.at[to], lses.at[n], device)

    loads[0].wait()
    loads[1].wait()

    def gain_body(n, carry):
        rows = pl.ds(pl.multiple_of(n * 128, 128), 128)
        row = jnp.broadcast_to(gain_ref[pl.ds(n, 1), :], (128, 128))
        eye = lax.broadcasted_iota(jnp.int32, row.shape, 0) == lax.broadcasted_iota(
            jnp.int32, row.shape, 1
        )
        column = jnp.sum(jnp.where(eye, row, 0.0), axis=1, keepdims=True)
        wgu[rows, :] = (wgu[rows, :].astype(jnp.float32) * column).astype(wgu.dtype)
        return carry

    lax.fori_loop(0, wgu.shape[0] // 128, gain_body, 0)

    for n, j in enumerate(SEQ_ORDER):
        _, back = seq_peer(place, j)
        device = {"seq": back, "tp": t}
        wire.recv(slots_e[n][0], parts.at[n], device)
        wire.recv(slots_e[n][1], lses.at[n], device)
    count = part_ref.shape[2]
    sums = [lses[n] for n in range(15)] + [lse_ref[place.s], fresh_lse_ref[...]]
    top = functools.reduce(jnp.maximum, sums)
    shares = [jnp.exp(v - top) for v in sums]
    totals = [pltpu.roll(v, v.shape[1] - count, 1) for v in sums]
    whole = functools.reduce(jnp.add, [w * v for w, v in zip(shares, totals)])
    used = lax.broadcasted_iota(jnp.int32, top.shape, 1) < count
    shares = [jnp.where(used, w / jnp.where(used, whole, 1.0), 0.0) for w in shares]
    attention = fresh_ref[...] * expand(shares[16], count)
    for n in range(15):
        attention += parts[n].astype(jnp.float32) * expand(shares[n], count)
    attention += part_ref[place.s].astype(jnp.float32) * expand(shares[15], count)
    att32[...] = attention
    per_step = count // STEPS
    heads = jnp.concatenate(
        [
            jnp.concatenate(
                [att32[:, i * per_step + g, :].astype(jnp.bfloat16) for g in range(per_step)],
                axis=1,
            )
            for i in range(STEPS)
        ],
        axis=0,
    )

    slots1 = [wire.slot() for _ in range(7)]
    loads[2].wait()
    own = None
    for j in (4, 3, 5, 2, 6, 1, 7, 0):
        to = lax.rem(t + j, 8)
        part = jnp.dot(heads, wo[:, columns(to)], preferred_element_type=jnp.float32)
        if j == 0:
            own = part
            break
        s1[j - 1] = part.astype(s1.dtype)
        wire.send(slots1[j - 1], s1.at[j - 1], r1.at[j - 1], {"seq": place.s, "tp": to})
    total = own + x_ref[:, columns(t)].astype(jnp.float32)
    for j in (1, 7, 2, 6, 3, 5, 4):
        wire.recv(slots1[j - 1], r1.at[j - 1], {"seq": place.s, "tp": lax.rem(t + 8 - j, 8)})
        total = total + r1[j - 1].astype(jnp.float32)
    mine = total.astype(jnp.bfloat16)
    mine_s[...] = mine

    gs = (g0, g1, g2)
    gathers = [Gather(wire, place, axes, buf) for axes, buf in zip(AXES, gs)]
    for g, w, start in zip(gathers, widths, starts):
        g.buf[core, place.at[g.c], place.at[g.b], place.at[g.a]] = mine[:, start : start + w]
        g.open()
    for g in gathers:
        g.line()
    for j in (1, 3, 2):
        for g in gathers:
            g.plane(j)
    for db in (0, 3, 1, 2):
        for g in gathers:
            g.space_near(db)
    for db in (0, 3, 1, 2):
        for g in gathers:
            g.space_far(db)
    for g in gathers:
        g.other_core()

    acc[...] = jnp.zeros_like(acc)
    squares[...] = jnp.zeros_like(squares)

    def rows_of(k, c, y):
        if k == 0:
            v = gs[0][c, :, :, y]
        elif k == 1:
            v = gs[1][c, y]
        else:
            v = jnp.stack(
                [jnp.stack([gs[2][c, x, y, z] for x in range(4)]) for z in range(4)]
            )
        return v.reshape(512, v.shape[-1])

    def up_body(i, carry):
        c, y = i // 4, i % 4
        tt = y * 2 + c
        for k in range(3):
            v = rows_of(k, c, y)
            w = wgu[columns(tt, starts[k], widths[k]), :]
            acc[...] += jnp.dot(v, w, preferred_element_type=jnp.float32)
            sq = None
            for n in range(widths[k] // 128):
                f = v[:, n * 128 : n * 128 + 128].astype(jnp.float32)
                sq = f * f if sq is None else sq + f * f
            squares[...] += sq
        return carry

    lax.fori_loop(0, 8, up_body, 0)

    def act_body(i, carry):
        rows = pl.ds(pl.multiple_of(i * 128, 128), 128)
        mean = jnp.sum(squares[rows, :], axis=-1, keepdims=True) / (8 * cols)
        r = lax.rsqrt(mean + norm_eps)
        gate = acc[rows, :ff] * r
        up = acc[rows, ff:] * r
        act[rows, :] = (gate / (1.0 + jnp.exp(-gate)) * up).astype(act.dtype)
        return carry

    lax.fori_loop(0, 4, act_body, 0)
    loads[3].wait()

    ps, os_ = (p0, p1, p2), (o0, o1, o2)

    def at_y(k, ref, y):
        return ref.at[:, :, y] if k == 0 else (ref.at[y] if k == 1 else ref.at[:, y])

    def down_rows(tt, z):
        rows = act[pl.ds(pl.multiple_of(z * 128, 128), 128), :]
        return jnp.dot(rows, wd[:, columns(tt)], preferred_element_type=jnp.float32)

    slots_o = [[wire.slot() for _ in range(3)] for _ in range(4)]
    for y in range(4):

        def other_body(z, carry):
            d = down_rows(y * 2 + 1 - core, z).astype(jnp.bfloat16).reshape(4, 32, cols)
            ps[0][1 - core, z, :, y] = d[:, :, : widths[0]]
            ps[1][1 - core, y, z] = d[:, :, starts[1] : starts[2]]
            for x in range(4):
                ps[2][1 - core, x, y, z] = d[x, :, starts[2] :]
            return carry

        lax.fori_loop(0, 4, other_body, 0)
        for k in range(3):
            wire.send(
                slots_o[y][k],
                at_y(k, ps[k].at[1 - core], y),
                at_y(k, os_[k], y),
                place.device(flip=True),
            )
    for y in range(4):
        for k in range(3):
            wire.recv(slots_o[y][k], at_y(k, os_[k], y), place.device(flip=True))

        def own_body(z, carry):
            d = down_rows(y * 2 + core, z).reshape(4, 32, cols)
            d0 = d[:, :, : widths[0]] + os_[0][z, :, y].astype(jnp.float32)
            ps[0][core, z, :, y] = d0.astype(jnp.bfloat16)
            d1 = d[:, :, starts[1] : starts[2]] + os_[1][y, z].astype(jnp.float32)
            ps[1][core, y, z] = d1.astype(jnp.bfloat16)
            for x in range(4):
                d2 = d[x, :, starts[2] :] + os_[2][x, y, z].astype(jnp.float32)
                ps[2][core, x, y, z] = d2.astype(jnp.bfloat16)
            return carry

        lax.fori_loop(0, 4, own_body, 0)

    rcs, ncs, qs = (rc0, rc1, rc2), (nc0, nc1, nc2), (q0, q1, q2)
    nbs, tas, ras = (nb0, nb1, nb2), (ta0, ta1, ta2), (ra0, ra1, ra2)

    def piece_c(k):
        def view(d, half):
            at = place.shifted(AXES[k][2], d)
            return ps[k].at[core, at, pl.ds(2 * half, 2)]

        return view

    along_c = [
        Scatter(wire, place, AXES[k][2], piece_c(k), rcs[k], ncs[k]) for k in range(3)
    ]
    slots_b = [[wire.slot() for _ in range(3)] for _ in range(3)]
    slots_a = [[wire.slot() for _ in range(3)] for _ in range(3)]
    for s in along_c:
        s.open()
    for s in along_c:
        s.pass_on(2)
    for k, s in enumerate(along_c):
        s.close()
        at = place.at[AXES[k][2]]

        def sum_c(b, carry):
            v = ps[k][core, at, b].astype(jnp.float32)
            v = v + ncs[k][0, b // 2, b % 2].astype(jnp.float32)
            v = v + ncs[k][1, b // 2, b % 2].astype(jnp.float32)
            qs[k][b] = v.astype(jnp.bfloat16)
            return carry

        lax.fori_loop(0, 4, sum_c, 0)
        axis = AXES[k][1]
        for j in (2, 1, 3):
            wire.send(
                slots_b[k][j - 1],
                qs[k].at[place.shifted(axis, j)],
                nbs[k].at[j - 1],
                place.device(axis, j),
            )
    for k in range(3):
        axis = AXES[k][1]
        at = place.at[axis]
        for j in (1, 3, 2):
            wire.recv(slots_b[k][j - 1], nbs[k].at[j - 1], place.device(axis, -j))
        for a in range(4):
            v = qs[k][at, a].astype(jnp.float32)
            for j in range(3):
                v = v + nbs[k][j, a].astype(jnp.float32)
            tas[k][a] = v.astype(jnp.bfloat16)
        for j in (2, 1, 3):
            axis = AXES[k][0]
            wire.send(
                slots_a[k][j - 1],
                tas[k].at[place.shifted(axis, j)],
                ras[k].at[j - 1],
                place.device(axis, j),
            )
    for k in range(3):
        axis = AXES[k][0]
        v = tas[k][place.at[axis]].astype(jnp.float32)
        for j in (1, 3, 2):
            wire.recv(slots_a[k][j - 1], ras[k].at[j - 1], place.device(axis, -j))
            v = v + ras[k][j - 1].astype(jnp.float32)
        lo = starts[k]
        v = v + mine_s[:, lo : lo + widths[k]].astype(jnp.float32)
        last[t, :, lo : lo + widths[k]] = v.astype(jnp.bfloat16)
    slots_l = [wire.slot() for _ in range(7)]
    for j in (4, 3, 5, 2, 6, 1, 7):
        to = {"seq": place.s, "tp": lax.rem(t + j, 8)}
        wire.send(slots_l[j - 1], last.at[t], last.at[t], to)
    for y in range(4):
        for c in range(2):
            tt = y * 2 + c
            z, x = place.at["z"], place.at["x"]
            attended_ref[:, tt * cols : tt * cols + widths[0]] = g0[c, z, x, y]
            attended_ref[:, tt * cols + starts[1] : tt * cols + starts[2]] = g1[c, y, z, x]
            attended_ref[:, tt * cols + starts[2] : tt * cols + cols] = g2[c, x, y, z]
    for j in range(1, 8):
        tt = lax.rem(t + 8 - j, 8)
        wire.recv(slots_l[j - 1], last.at[tt], {"seq": place.s, "tp": tt})
    for tt in range(8):
        layer_ref[:, tt * cols : tt * cols + cols] = last[tt]
    wire.drain()


def second_half(part, lse, fresh, fresh_lse, x, gain, w_output, w_gate, w_up, w_down):
    rows, width = x.shape
    cols = width // 8
    ff = w_down.shape[0]
    tiles = cols // 128
    first = -(-2 * tiles // 5)
    widths = (first * 128, first * 128, (tiles - 2 * first) * 128)
    assert rows == 32 and min(widths) > 0
    bf, f32 = jnp.bfloat16, jnp.float32
    vm = pltpu.VMEM

    def each(*shape):
        return [vm(shape + (rows, w), bf) for w in widths]

    count = slots_needed()
    scratch = [
        vm(w_output.shape, bf),
        vm((width, 2 * ff), bf),
        vm(w_down.shape, bf),
        vm((7, rows, cols), bf),
        vm((7, rows, cols), bf),
        *each(2, 4, 4, 4),
        vm((512, 2 * ff), f32),
        vm((512, 128), f32),
        vm((512, ff), bf),
        *each(2, 4, 4, 4),
        *each(4, 4, 4),
        *each(2, 2, 4),
        *each(2, 2, 2, 4),
        *each(4, 4),
        *each(3, 4),
        *each(4),
        *each(3),
        vm((rows, cols), bf),
        vm((8, rows, cols), bf),
        vm((15,) + part.shape[1:], bf),
        vm((15,) + lse.shape[1:], f32),
        vm(part.shape[1:], f32),
        pltpu.SemaphoreType.DMA((4,)),
        pltpu.SemaphoreType.DMA((count,)),
        pltpu.SemaphoreType.DMA((count,)),
    ]
    whole = pl.BlockSpec(memory_space=pltpu.VMEM)
    hbm = pl.BlockSpec(memory_space=pl.ANY)
    out = jax.ShapeDtypeStruct((rows, width), bf)
    return pl.pallas_call(
        functools.partial(block_kernel, widths),
        out_shape=[out, out],
        in_specs=[whole] * 6 + [hbm] * 4,
        out_specs=[whole, whole],
        scratch_shapes=scratch,
        compiler_params=pltpu.CompilerParams(
            collective_id=1, has_side_effects=True, vmem_limit_bytes=63 * 1024 * 1024
        ),
        name="second_half",
    )(part, lse, fresh, fresh_lse, x, gain, w_output, w_gate, w_up, w_down)


class QueryGather:
    def __init__(self, wire, place, axes, buf):
        self.wire, self.place, self.buf = wire, place, buf
        self.a, self.b = axes
        self.slots_a = [wire.slot() for _ in range(3)]
        self.slots_b = [wire.slot() for _ in range(3)]

    def cut(self, b, a):
        return self.buf.at[b, a] if self.b == "z" else self.buf.at[a, b]

    def block(self, da):
        return self.cut(self.place.at[self.b], self.place.shifted(self.a, da))

    def group(self, db):
        return self.cut(self.place.shifted(self.b, db), pl.ds(0, 4))

    def open(self):
        mine = self.block(0)
        for j in (2, 1, 3):
            self.wire.send(self.slots_a[j - 1], mine, mine, self.place.device(self.a, j))

    def line(self):
        for j in (1, 3, 2):
            self.wire.recv(self.slots_a[j - 1], self.block(-j), self.place.device(self.a, -j))
        mine = self.group(0)
        for j in (2, 1, 3):
            self.wire.send(self.slots_b[j - 1], mine, mine, self.place.device(self.b, j))

    def plane(self):
        for j in (1, 3, 2):
            self.wire.recv(self.slots_b[j - 1], self.group(-j), self.place.device(self.b, -j))


def project_kernel(
    x_ref,
    gain_ref,
    freq_ref,
    slot_ref,
    length_ref,
    wq_hbm,
    wk_hbm,
    wv_hbm,
    q_all,
    fresh_ref,
    fresh_lse_ref,
    wq,
    wk,
    wv,
    q32,
    load_sem,
    send_sem,
    recv_sem,
):
    place = Place()
    wire = Wire(send_sem, recv_sem)
    rows, width = x_ref.shape
    dim = wk.shape[1]
    heads = wq.shape[1] // dim
    steps = STEPS
    own = rows // steps
    barrier = pltpu.get_barrier_semaphore()
    for axis in ("x", "z"):
        for by in (1, 2, 3):
            pl.semaphore_signal(
                barrier, inc=1, device_id=place.device(axis, by), device_id_type=MESH
            )
    chunks = load_sem.shape[0]
    depth = width // chunks
    loads = []
    for i in range(chunks):
        part = pl.ds(i * depth, depth)
        loads.append(
            [
                pltpu.make_async_copy(src.at[part], dst.at[part], load_sem.at[i, n])
                for n, (src, dst) in enumerate(((wq_hbm, wq), (wk_hbm, wk), (wv_hbm, wv)))
            ]
        )
        for load in loads[-1]:
            load.start()
    x = x_ref[...].astype(jnp.float32)
    mean = jnp.mean(x * x, axis=-1, keepdims=True)
    normed = (x * lax.rsqrt(mean + norm_eps) * gain_ref[...]).astype(jnp.bfloat16)

    shape = (own, slot_ref.shape[1])
    mine = place.s * own + lax.broadcasted_iota(jnp.int32, shape, 0)
    length = jnp.where(slot_ref[...] == mine, length_ref[...].astype(jnp.float32), 0.0)
    length = jnp.sum(length, axis=-1, keepdims=True)
    position = jnp.concatenate([length + float(i) for i in range(steps)], axis=0)
    angle = position * freq_ref[...]
    cosine = jnp.cos(angle)
    sine = jnp.sin(angle)
    low = lax.broadcasted_iota(jnp.int32, angle.shape, 1) < dim // 2
    sine = jnp.where(low, -sine, sine)

    def rotate(v):
        return v * cosine + pltpu.roll(v, dim // 2, 1) * sine

    q = k = v = 0.0
    for i in range(chunks):
        for load in loads[i]:
            load.wait()
        lhs = normed[:, i * depth : (i + 1) * depth]
        part = pl.ds(i * depth, depth)
        q = q + jnp.dot(lhs, wq[part, :], preferred_element_type=jnp.float32)
        k = k + jnp.dot(lhs, wk[part, :], preferred_element_type=jnp.float32)
        v = v + jnp.dot(lhs, wv[part, :], preferred_element_type=jnp.float32)
    for g in range(heads):
        turned = rotate(q[:, g * dim : (g + 1) * dim])
        for i in range(steps):
            q32[:, i * heads + g, :] = turned[i * own : (i + 1) * own]
    queries = q32[...].astype(jnp.bfloat16)
    s_at = (place.at["z"], place.at["x"])
    half = own // 2
    for n in range(2):
        q_all[n, s_at[0], s_at[1]] = queries[n * half : (n + 1) * half]
    gathers = [
        QueryGather(wire, place, axes, q_all.at[n])
        for n, axes in enumerate((("x", "z"), ("z", "x")))
    ]
    pl.semaphore_wait(barrier, 6)
    for g in gathers:
        g.open()

    new_k = rotate(k).astype(jnp.bfloat16)
    new_v = v.astype(jnp.bfloat16)
    count = steps * heads
    flat = queries.reshape(own * count, dim)
    s = lax.dot_general(
        flat, new_k, (((1,), (1,)), ((), ())), preferred_element_type=jnp.float32
    ) * (dim**-0.5)
    r = lax.broadcasted_iota(jnp.int32, s.shape, 0)
    c = lax.broadcasted_iota(jnp.int32, s.shape, 1)
    allowed = (r // count == c % own) & (c // own <= (r % count) // heads)
    s = jnp.where(allowed, s, masked_low)
    top = jnp.max(s, axis=-1, keepdims=True)
    w = jnp.where(allowed, jnp.exp(s - top), 0.0)
    total = jnp.sum(w, axis=-1, keepdims=True)
    acc = jnp.dot(w.astype(jnp.bfloat16), new_v, preferred_element_type=jnp.float32)
    fresh_ref[...] = acc.reshape(own, count, dim)
    shape = (own, count, dim)
    fresh_lse_ref[...] = compact(
        jnp.broadcast_to(top, (own * count, dim)).reshape(shape),
        jnp.broadcast_to(total, (own * count, dim)).reshape(shape),
    )

    for g in gathers:
        g.line()
    for g in gathers:
        g.plane()
    wire.drain()


def first_half(x, gain, slot, lengths, w_query, w_key, w_value):
    rows, width = x.shape
    dim = w_key.shape[1]
    count = STEPS * w_query.shape[1] // dim
    own = rows // STEPS
    bf, f32, vm = jnp.bfloat16, jnp.float32, pltpu.VMEM
    exponent = jnp.arange(dim // 2, dtype=f32) * (2.0 / dim)
    freq = rope_theta ** (-exponent)
    freq = jnp.concatenate([freq, freq])[None, :]
    whole = pl.BlockSpec(memory_space=pltpu.VMEM)
    hbm = pl.BlockSpec(memory_space=pl.ANY)
    return pl.pallas_call(
        project_kernel,
        out_shape=[
            jax.ShapeDtypeStruct((2, 4, 4, own // 2, count, dim), bf),
            jax.ShapeDtypeStruct((own, count, dim), f32),
            jax.ShapeDtypeStruct((own, dim), f32),
        ],
        in_specs=[whole] * 5 + [hbm] * 3,
        out_specs=[whole] * 3,
        scratch_shapes=[
            vm(w_query.shape, bf),
            vm(w_key.shape, bf),
            vm(w_value.shape, bf),
            vm((own, count, dim), f32),
            pltpu.SemaphoreType.DMA((8, 3)),
            pltpu.SemaphoreType.DMA((12,)),
            pltpu.SemaphoreType.DMA((12,)),
        ],
        compiler_params=pltpu.CompilerParams(
            collective_id=2, has_side_effects=True, vmem_limit_bytes=63 * 1024 * 1024
        ),
        name="first_half",
    )(x, gain[None, :], freq, slot[None, :], lengths[None, :], w_query, w_key, w_value)


def finish_kernel(a_ref, b_ref, c_ref, d_ref):
    c_ref[...] = a_ref[...].reshape(c_ref.shape)
    d_ref[...] = b_ref[...].reshape(d_ref.shape)


def finish(attended, layer_out, shape):
    out = jax.ShapeDtypeStruct(shape, attended.dtype)
    return pl.pallas_call(finish_kernel, out_shape=[out, out], name="finish")(attended, layer_out)


def local(
    token_inputs,
    attn_gain,
    w_query,
    key_projection,
    value_projection,
    w_output,
    mlp_gain,
    w_gate,
    w_up,
    w_down,
    key_cache,
    paged_value_cache,
    cache_lengths,
    page_request,
    page_number,
    request_slot,
):
    steps, row_count, width = token_inputs.shape
    x = token_inputs.reshape(steps * row_count, width)
    queries, fresh, fresh_lse = first_half(
        x, attn_gain, request_slot, cache_lengths, w_query, key_projection, value_projection
    )
    count, dim = queries.shape[-2:]
    seq = lax.axis_size("seq")
    queries = queries.reshape(2, seq, row_count // 2, count, dim)
    part, lse = paged_attention(
        page_request,
        page_number,
        request_slot,
        cache_lengths,
        queries,
        key_cache,
        paged_value_cache,
    )
    attended, layer_out = second_half(
        part.reshape(seq, row_count, count, dim),
        lse.reshape(seq, row_count, dim),
        fresh,
        fresh_lse,
        x,
        mlp_gain.reshape(-1, 128),
        w_output,
        w_gate,
        w_up,
        w_down,
    )
    shape = (steps, row_count, width)
    return tuple(finish(attended, layer_out, shape))


def solution(mesh):
    in_specs = (
        P(None, "seq", None),
        P(),
        P(None, "tp"),
        P(None, "tp"),
        P(None, "tp"),
        P("tp", None),
        P(),
        P(None, ("seq", "tp")),
        P(None, ("seq", "tp")),
        P(("seq", "tp"), None),
        P("seq", "tp", None, None),
        P("seq", "tp", None, None),
        P(),
        P("seq"),
        P("seq"),
        P(),
    )
    out_specs = (P(None, "seq", None), P(None, "seq", None))
    return jax.shard_map(local, mesh=mesh, in_specs=in_specs, out_specs=out_specs, check_vma=False)
```

```python
import functools

import jax
import jax.numpy as jnp
from jax import lax
from jax.experimental import pallas as pl
from jax.experimental.pallas import tpu as pltpu
from jax.sharding import PartitionSpec as P

STEPS = 4
rope_theta = 100000000.0
norm_eps = 1e-05
masked_low = -1e30


def paged_kernel(
    pages, request_ref, number_ref, slot_ref, length_ref, q_ref, k_ref, v_ref, o_ref, lse_ref, m_s, l_s, acc_s
):
    step = pl.program_id(0)
    scale = k_ref.shape[-1] ** (-0.5)
    length = k_ref.shape[1]

    @pl.when(step == 0)
    def _():
        m_s[...] = jnp.full_like(m_s, masked_low)
        l_s[...] = jnp.zeros_like(l_s)
        acc_s[...] = jnp.zeros_like(acc_s)

    stats = []
    for i in range(pages):
        page = step * pages + i
        request = request_ref[page]
        live_page = request >= 0
        request = jnp.maximum(request, 0)
        row = slot_ref[request]
        valid = jnp.clip(length_ref[request] - number_ref[page] * length, 0, length)
        valid = jnp.where(live_page, valid, 0)
        q = q_ref[(row % 8) // 4, row // 8, row % 4]
        s = (
            lax.dot_general(
                q, k_ref[i], (((1,), (1,)), ((), ())), preferred_element_type=jnp.float32
            )
            * scale
        )
        live = lax.broadcasted_iota(jnp.int32, s.shape, 1) < valid
        s = jnp.where(live, s, masked_low)
        m = jnp.max(s, axis=-1, keepdims=True)
        w = jnp.where(live, jnp.exp(s - m), 0.0)
        l = jnp.sum(w, axis=-1, keepdims=True)
        acc = jnp.dot(w.astype(jnp.bfloat16), v_ref[i], preferred_element_type=jnp.float32)
        stats.append((row, m, l, acc))
    for row, m, l, acc in stats:
        m_old = m_s[row]
        m_new = jnp.maximum(m_old, m)
        a_old = jnp.exp(m_old - m_new)
        a_new = jnp.exp(m - m_new)
        m_s[row] = m_new
        l_s[row] = l_s[row] * a_old + l * a_new
        acc_s[row] = acc_s[row] * a_old + acc * a_new

    @pl.when(step == pl.num_programs(0) - 1)
    def _():
        o_ref[...] = acc_s[...].astype(o_ref.dtype)
        lse_ref[...] = compact(m_s[...], l_s[...])


def compact(tops, sums):
    row = lax.broadcasted_iota(jnp.int32, tops.shape, 1)
    lane = lax.broadcasted_iota(jnp.int32, tops.shape, 2)
    count = tops.shape[1]
    picked = jnp.where(lane == row, tops, jnp.where(lane == row + count, sums, 0.0))
    return jnp.sum(picked, axis=1)


def expand(values, count):
    shape = (values.shape[0], count, values.shape[1])
    eye = lax.broadcasted_iota(jnp.int32, shape, 1) == lax.broadcasted_iota(jnp.int32, shape, 2)
    wide = jnp.broadcast_to(values[:, None, :], shape)
    return jnp.sum(jnp.where(eye, wide, 0.0), axis=-1, keepdims=True)


def paged_attention(request, number, slot, lengths, queries, keys, values):
    group, dim = queries.shape[-2:]
    total = slot.shape[0]
    count, _, length, _ = keys.shape
    pages = next(n for n in (12, 9, 6, 4, 3, 2, 1) if count % n == 0)
    paged = pl.BlockSpec((pages, None, length, dim), lambda i, *_: (i, 0, 0, 0))
    return pl.pallas_call(
        functools.partial(paged_kernel, pages),
        grid_spec=pltpu.PrefetchScalarGridSpec(
            num_scalar_prefetch=4,
            grid=(count // pages,),
            in_specs=[
                pl.BlockSpec(queries.shape, lambda i, *_: (0, 0, 0, 0, 0)),
                paged,
                paged,
            ],
            out_specs=[
                pl.BlockSpec((total, group, dim), lambda i, *_: (0, 0, 0)),
                pl.BlockSpec((total, dim), lambda i, *_: (0, 0)),
            ],
            scratch_shapes=[
                pltpu.VMEM((total, group, dim), jnp.float32),
                pltpu.VMEM((total, group, dim), jnp.float32),
                pltpu.VMEM((total, group, dim), jnp.float32),
            ],
        ),
        out_shape=[
            jax.ShapeDtypeStruct((total, group, dim), jnp.bfloat16),
            jax.ShapeDtypeStruct((total, dim), jnp.float32),
        ],
        name="paged_attention",
    )(request, number, slot, lengths, queries, keys, values)


AXES = (("y", "x", "z"), ("x", "z", "y"), ("z", "y", "x"))
MESH = pl.DeviceIdType.MESH


class Place:
    def __init__(self):
        s = lax.axis_index("seq")
        t = lax.axis_index("tp")
        self.at = {"z": s // 4, "x": s % 4, "y": t // 2}
        self.core = t % 2
        self.s = s
        self.t = t

    def shifted(self, axis, by):
        return lax.rem(self.at[axis] + (by + 4), 4)

    def device(self, axis=None, by=0, flip=False):
        at = dict(self.at)
        if axis is not None:
            at[axis] = self.shifted(axis, by)
        core = 1 - self.core if flip else self.core
        return {"seq": at["z"] * 4 + at["x"], "tp": at["y"] * 2 + core}


class Wire:
    def __init__(self, send_sem, recv_sem):
        self.send_sem = send_sem
        self.recv_sem = recv_sem
        self.used = 0
        self.sent = []

    def slot(self):
        self.used += 1
        return self.used - 1

    def send(self, slot, src, dst, device):
        copy = pltpu.make_async_remote_copy(
            src_ref=src,
            dst_ref=dst,
            send_sem=self.send_sem.at[slot],
            recv_sem=self.recv_sem.at[slot],
            device_id=device,
            device_id_type=MESH,
        )
        copy.start()
        self.sent.append(copy)

    def recv(self, slot, dst, device):
        pltpu.make_async_remote_copy(
            src_ref=dst,
            dst_ref=dst,
            send_sem=self.send_sem.at[slot],
            recv_sem=self.recv_sem.at[slot],
            device_id=device,
            device_id_type=MESH,
        ).wait_recv()

    def drain(self):
        for copy in self.sent:
            copy.wait_send()


def greet(place):
    barrier = pltpu.get_barrier_semaphore()
    peers = [{"seq": place.s, "tp": lax.rem(place.t + j, 8)} for j in range(1, 8)]
    peers += [{"seq": seq_peer(place, j)[0], "tp": place.t} for j in SEQ_ORDER]
    for peer in peers:
        pl.semaphore_signal(barrier, inc=1, device_id=peer, device_id_type=MESH)
    return barrier, len(peers)


SEQ_ORDER = tuple(
    sorted(
        ((dz, dx) for dz in range(4) for dx in range(4) if (dz, dx) != (0, 0)),
        key=lambda d: -(min(d[0], 4 - d[0]) + min(d[1], 4 - d[1])),
    )
)


def seq_peer(place, by):
    on = place.shifted("z", by[0]) * 4 + place.shifted("x", by[1])
    back = place.shifted("z", -by[0]) * 4 + place.shifted("x", -by[1])
    return on, back


class Gather:
    def __init__(self, wire, place, axes, buf):
        self.wire, self.place, self.buf = wire, place, buf
        self.a, self.b, self.c = axes
        self.slots_a = [wire.slot() for _ in range(3)]
        self.slots_b = [wire.slot() for _ in range(3)]
        self.slots_c = [[wire.slot() for _ in range(4)] for _ in range(4)]
        self.slots_p = [[wire.slot() for _ in range(4)] for _ in range(4)]

    def group(self, db, dc, core=None):
        place = self.place
        core = place.core if core is None else core
        return self.buf.at[core, place.shifted(self.c, dc), place.shifted(self.b, db)]

    def half(self, db, dc, which):
        place = self.place
        return self.buf.at[
            place.core, place.shifted(self.c, dc), place.shifted(self.b, db), pl.ds(2 * which, 2)
        ]

    def block(self, da):
        place = self.place
        return self.buf.at[
            place.core, place.at[self.c], place.at[self.b], place.shifted(self.a, da)
        ]

    def open(self):
        mine = self.block(0)
        for j in (2, 1, 3):
            self.wire.send(self.slots_a[j - 1], mine, mine, self.place.device(self.a, j))

    def spread(self, db):
        mine = self.group(db, 0)
        slots = self.slots_c[db]
        self.wire.send(slots[0], mine, mine, self.place.device(self.c, 1))
        self.wire.send(slots[1], mine, mine, self.place.device(self.c, -1))
        self.over(db, 0)

    def over(self, db, dc):
        mine = self.group(db, dc)
        self.wire.send(self.slots_p[db][dc], mine, mine, self.place.device(flip=True))

    def line(self):
        for j in (1, 3, 2):
            self.wire.recv(self.slots_a[j - 1], self.block(-j), self.place.device(self.a, -j))
        mine = self.group(0, 0)
        for j in (2, 1, 3):
            self.wire.send(self.slots_b[j - 1], mine, mine, self.place.device(self.b, j))
        self.spread(0)

    def plane(self, j):
        self.wire.recv(self.slots_b[j - 1], self.group(-j, 0), self.place.device(self.b, -j))
        self.spread(4 - j)

    def space_near(self, db):
        place, wire = self.place, self.wire
        slots = self.slots_c[db]
        wire.recv(slots[0], self.group(db, -1), place.device(self.c, -1))
        part = self.half(db, -1, 0)
        wire.send(slots[2], part, part, place.device(self.c, 1))
        wire.recv(slots[1], self.group(db, 1), place.device(self.c, 1))
        part = self.half(db, 1, 1)
        wire.send(slots[3], part, part, place.device(self.c, -1))
        self.over(db, 3)
        self.over(db, 1)

    def space_far(self, db):
        place, wire = self.place, self.wire
        slots = self.slots_c[db]
        wire.recv(slots[2], self.half(db, 2, 0), place.device(self.c, -1))
        wire.recv(slots[3], self.half(db, 2, 1), place.device(self.c, 1))
        self.over(db, 2)

    def other_core(self, dc):
        place = self.place
        for db in (0, 3, 1, 2):
            self.wire.recv(
                self.slots_p[db][dc], self.group(db, dc, 1 - place.core), place.device(flip=True)
            )


def add_into(dst, src, count):
    def body(i, carry):
        total = dst[i].astype(jnp.float32) + src[i].astype(jnp.float32)
        dst[i] = total.astype(dst.dtype)
        return carry

    lax.fori_loop(0, count, body, 0)


class Scatter:
    def __init__(self, wire, place, axis, piece, relay, near):
        self.wire, self.place, self.axis = wire, place, axis
        self.piece, self.relay, self.near = piece, relay, near
        self.slots = [wire.slot() for _ in range(6)]

    def open(self):
        w, p = self.wire, self.place
        up, down = p.device(self.axis, 1), p.device(self.axis, -1)
        w.send(self.slots[0], self.piece(2, 0), self.relay.at[0], up)
        w.send(self.slots[1], self.piece(2, 1), self.relay.at[1], down)
        w.send(self.slots[2], self.piece(1, 1), self.near.at[0, 1], up)
        w.send(self.slots[3], self.piece(-1, 0), self.near.at[1, 0], down)

    def pass_on(self, count):
        w, p = self.wire, self.place
        up, down = p.device(self.axis, 1), p.device(self.axis, -1)
        w.recv(self.slots[0], self.relay.at[0], down)
        add_into(self.piece(1, 0), self.relay.at[0], count)
        w.send(self.slots[4], self.piece(1, 0), self.near.at[0, 0], up)
        w.recv(self.slots[1], self.relay.at[1], up)
        add_into(self.piece(-1, 1), self.relay.at[1], count)
        w.send(self.slots[5], self.piece(-1, 1), self.near.at[1, 1], down)

    def close(self):
        w, p = self.wire, self.place
        up, down = p.device(self.axis, 1), p.device(self.axis, -1)
        w.recv(self.slots[2], self.near.at[0, 1], down)
        w.recv(self.slots[3], self.near.at[1, 0], up)
        w.recv(self.slots[4], self.near.at[0, 0], down)
        w.recv(self.slots[5], self.near.at[1, 1], up)


def slots_needed():
    return 30 + 7 + 3 * (3 + 3 + 16 + 16) + 12 + 3 * (6 + 3 + 3) + 7


def block_kernel(
    widths,
    part_ref,
    lse_ref,
    fresh_ref,
    fresh_lse_ref,
    x_ref,
    gain_ref,
    wo_hbm,
    wg_hbm,
    wu_hbm,
    wd_hbm,
    attended_ref,
    layer_ref,
    wo,
    wgu,
    wd,
    s1,
    r1,
    g0,
    g1,
    g2,
    acc,
    squares,
    act,
    p0,
    p1,
    p2,
    o0,
    o1,
    o2,
    rc0,
    rc1,
    rc2,
    nc0,
    nc1,
    nc2,
    q0,
    q1,
    q2,
    nb0,
    nb1,
    nb2,
    ta0,
    ta1,
    ta2,
    ra0,
    ra1,
    ra2,
    mine_s,
    last,
    parts,
    lses,
    att32,
    load_sem,
    send_sem,
    recv_sem,
):
    place = Place()
    t, core = place.t, place.core
    ff = wd.shape[0]
    cols = sum(widths)
    starts = (0, widths[0], widths[0] + widths[1])
    wire = Wire(send_sem, recv_sem)
    barrier, peers = greet(place)
    weights = (
        (wg_hbm, wgu.at[:, pl.ds(0, ff)]),
        (wu_hbm, wgu.at[:, pl.ds(ff, ff)]),
        (wo_hbm, wo),
        (wd_hbm, wd),
    )
    loads = [
        pltpu.make_async_copy(src, dst, load_sem.at[i]) for i, (src, dst) in enumerate(weights)
    ]
    for load in loads:
        load.start()

    def columns(index, start=0, size=cols):
        return pl.ds(pl.multiple_of(index * cols + start, 128), size)

    slots_e = [[wire.slot() for _ in range(2)] for _ in range(15)]
    pl.semaphore_wait(barrier, peers)
    for n, j in enumerate(SEQ_ORDER):
        to, _ = seq_peer(place, j)
        device = {"seq": to, "tp": t}
        wire.send(slots_e[n][0], part_ref.at[to], parts.at[n], device)
        wire.send(slots_e[n][1], lse_ref.at[to], lses.at[n], device)

    loads[0].wait()
    loads[1].wait()

    def gain_body(n, carry):
        rows = pl.ds(pl.multiple_of(n * 128, 128), 128)
        row = jnp.broadcast_to(gain_ref[pl.ds(n, 1), :], (128, 128))
        eye = lax.broadcasted_iota(jnp.int32, row.shape, 0) == lax.broadcasted_iota(
            jnp.int32, row.shape, 1
        )
        column = jnp.sum(jnp.where(eye, row, 0.0), axis=1, keepdims=True)
        wgu[rows, :] = (wgu[rows, :].astype(jnp.float32) * column).astype(wgu.dtype)
        return carry

    lax.fori_loop(0, wgu.shape[0] // 128, gain_body, 0)

    for n, j in enumerate(SEQ_ORDER):
        _, back = seq_peer(place, j)
        device = {"seq": back, "tp": t}
        wire.recv(slots_e[n][0], parts.at[n], device)
        wire.recv(slots_e[n][1], lses.at[n], device)
    count = part_ref.shape[2]
    sums = [lses[n] for n in range(15)] + [lse_ref[place.s], fresh_lse_ref[...]]
    top = functools.reduce(jnp.maximum, sums)
    shares = [jnp.exp(v - top) for v in sums]
    totals = [pltpu.roll(v, v.shape[1] - count, 1) for v in sums]
    whole = functools.reduce(jnp.add, [w * v for w, v in zip(shares, totals)])
    used = lax.broadcasted_iota(jnp.int32, top.shape, 1) < count
    shares = [jnp.where(used, w / jnp.where(used, whole, 1.0), 0.0) for w in shares]
    attention = fresh_ref[...] * expand(shares[16], count)
    for n in range(15):
        attention += parts[n].astype(jnp.float32) * expand(shares[n], count)
    attention += part_ref[place.s].astype(jnp.float32) * expand(shares[15], count)
    att32[...] = attention
    per_step = count // STEPS
    heads = jnp.concatenate(
        [
            jnp.concatenate(
                [att32[:, i * per_step + g, :].astype(jnp.bfloat16) for g in range(per_step)],
                axis=1,
            )
            for i in range(STEPS)
        ],
        axis=0,
    )

    slots1 = [wire.slot() for _ in range(7)]
    loads[2].wait()
    own = None
    for j in (4, 3, 5, 2, 6, 1, 7, 0):
        to = lax.rem(t + j, 8)
        part = jnp.dot(heads, wo[:, columns(to)], preferred_element_type=jnp.float32)
        if j == 0:
            own = part
            break
        s1[j - 1] = part.astype(s1.dtype)
        wire.send(slots1[j - 1], s1.at[j - 1], r1.at[j - 1], {"seq": place.s, "tp": to})
    total = own + x_ref[:, columns(t)].astype(jnp.float32)
    for j in (1, 7, 2, 6, 3, 5, 4):
        wire.recv(slots1[j - 1], r1.at[j - 1], {"seq": place.s, "tp": lax.rem(t + 8 - j, 8)})
        total = total + r1[j - 1].astype(jnp.float32)
    mine = total.astype(jnp.bfloat16)
    mine_s[...] = mine

    gs = (g0, g1, g2)
    gathers = [Gather(wire, place, axes, buf) for axes, buf in zip(AXES, gs)]
    for g, w, start in zip(gathers, widths, starts):
        g.buf[core, place.at[g.c], place.at[g.b], place.at[g.a]] = mine[:, start : start + w]
        g.open()
    for g in gathers:
        g.line()
    for j in (1, 3, 2):
        for g in gathers:
            g.plane(j)

    acc[...] = jnp.zeros_like(acc)
    squares[...] = jnp.zeros_like(squares)

    def squared(v):
        total = None
        for n in range(v.shape[-1] // 128):
            f = v[:, n * 128 : n * 128 + 128].astype(jnp.float32)
            total = f * f if total is None else total + f * f
        return total

    def product(v, w):
        return jnp.dot(v, w, preferred_element_type=jnp.float32)

    def use_slab(dc, c):
        z, y1, x = place.shifted("z", dc), place.shifted("y", dc), place.shifted("x", dc)

        def first_body(y, carry):
            v = g0[c, z, :, y].reshape(128, widths[0])
            d = product(v, wgu[columns(y * 2 + c, 0, widths[0]), :])
            acc[z] += d.reshape(4, 32, 2 * ff)
            squares[z] += squared(v).reshape(4, 32, 128)
            return carry

        lax.fori_loop(0, 4, first_body, 0)

        def middle_body(i, carry):
            v = g1[c, y1, i].reshape(128, widths[1])
            d = product(v, wgu[columns(y1 * 2 + c, starts[1], widths[1]), :])
            acc[i] += d.reshape(4, 32, 2 * ff)
            squares[i] += squared(v).reshape(4, 32, 128)
            return carry

        lax.fori_loop(0, 4, middle_body, 0)

        def last_body(i, carry):
            vs = [g2[c, x, i * 2 + n].reshape(128, widths[2]) for n in range(2)]
            ws = [
                wgu[columns((i * 2 + n) * 2 + c, starts[2], widths[2]), :] for n in range(2)
            ]
            v = jnp.concatenate(vs, axis=1)
            d = product(v, jnp.concatenate(ws, axis=0))
            acc[:, x] += d.reshape(4, 32, 2 * ff)
            squares[:, x] += squared(v).reshape(4, 32, 128)
            return carry

        lax.fori_loop(0, 2, last_body, 0)

    use_slab(0, core)
    for db in (0, 3, 1, 2):
        for g in gathers:
            g.space_near(db)
    use_slab(3, core)
    use_slab(1, core)
    for g in gathers:
        g.other_core(0)
    use_slab(0, 1 - core)
    for db in (0, 3, 1, 2):
        for g in gathers:
            g.space_far(db)
    for dc in (3, 1):
        for g in gathers:
            g.other_core(dc)
        use_slab(dc, 1 - core)
    use_slab(2, core)
    for g in gathers:
        g.other_core(2)
    use_slab(2, 1 - core)

    def act_body(i, carry):
        rows = pl.ds(pl.multiple_of(i * 128, 128), 128)
        mean = jnp.sum(squares[i].reshape(128, 128), axis=-1, keepdims=True) / (8 * cols)
        r = lax.rsqrt(mean + norm_eps)
        both = acc[i].reshape(128, 2 * ff) * r
        gate = both[:, :ff]
        up = both[:, ff:]
        act[rows, :] = (gate / (1.0 + jnp.exp(-gate)) * up).astype(act.dtype)
        return carry

    lax.fori_loop(0, 4, act_body, 0)
    loads[3].wait()

    ps, os_ = (p0, p1, p2), (o0, o1, o2)

    def at_y(k, ref, y):
        return ref.at[:, :, y] if k == 0 else (ref.at[y] if k == 1 else ref.at[:, y])

    def down_rows(tt, z):
        rows = act[pl.ds(pl.multiple_of(z * 128, 128), 128), :]
        return jnp.dot(rows, wd[:, columns(tt)], preferred_element_type=jnp.float32)

    slots_o = [[wire.slot() for _ in range(3)] for _ in range(4)]
    for y in range(4):

        def other_body(z, carry):
            d = down_rows(y * 2 + 1 - core, z).astype(jnp.bfloat16).reshape(4, 32, cols)
            ps[0][1 - core, z, :, y] = d[:, :, : widths[0]]
            ps[1][1 - core, y, z] = d[:, :, starts[1] : starts[2]]
            for x in range(4):
                ps[2][1 - core, x, y, z] = d[x, :, starts[2] :]
            return carry

        lax.fori_loop(0, 4, other_body, 0)
        for k in range(3):
            wire.send(
                slots_o[y][k],
                at_y(k, ps[k].at[1 - core], y),
                at_y(k, os_[k], y),
                place.device(flip=True),
            )
    for y in range(4):
        for k in range(3):
            wire.recv(slots_o[y][k], at_y(k, os_[k], y), place.device(flip=True))

        def own_body(z, carry):
            d = down_rows(y * 2 + core, z).reshape(4, 32, cols)
            d0 = d[:, :, : widths[0]] + os_[0][z, :, y].astype(jnp.float32)
            ps[0][core, z, :, y] = d0.astype(jnp.bfloat16)
            d1 = d[:, :, starts[1] : starts[2]] + os_[1][y, z].astype(jnp.float32)
            ps[1][core, y, z] = d1.astype(jnp.bfloat16)
            for x in range(4):
                d2 = d[x, :, starts[2] :] + os_[2][x, y, z].astype(jnp.float32)
                ps[2][core, x, y, z] = d2.astype(jnp.bfloat16)
            return carry

        lax.fori_loop(0, 4, own_body, 0)

    rcs, ncs, qs = (rc0, rc1, rc2), (nc0, nc1, nc2), (q0, q1, q2)
    nbs, tas, ras = (nb0, nb1, nb2), (ta0, ta1, ta2), (ra0, ra1, ra2)

    def piece_c(k):
        def view(d, half):
            at = place.shifted(AXES[k][2], d)
            return ps[k].at[core, at, pl.ds(2 * half, 2)]

        return view

    along_c = [
        Scatter(wire, place, AXES[k][2], piece_c(k), rcs[k], ncs[k]) for k in range(3)
    ]
    slots_b = [[wire.slot() for _ in range(3)] for _ in range(3)]
    slots_a = [[wire.slot() for _ in range(3)] for _ in range(3)]
    for s in along_c:
        s.open()
    for s in along_c:
        s.pass_on(2)
    for k, s in enumerate(along_c):
        s.close()
        at = place.at[AXES[k][2]]

        def sum_c(b, carry):
            v = ps[k][core, at, b].astype(jnp.float32)
            v = v + ncs[k][0, b // 2, b % 2].astype(jnp.float32)
            v = v + ncs[k][1, b // 2, b % 2].astype(jnp.float32)
            qs[k][b] = v.astype(jnp.bfloat16)
            return carry

        lax.fori_loop(0, 4, sum_c, 0)
        axis = AXES[k][1]
        for j in (2, 1, 3):
            wire.send(
                slots_b[k][j - 1],
                qs[k].at[place.shifted(axis, j)],
                nbs[k].at[j - 1],
                place.device(axis, j),
            )
    for k in range(3):
        axis = AXES[k][1]
        at = place.at[axis]
        for j in (1, 3, 2):
            wire.recv(slots_b[k][j - 1], nbs[k].at[j - 1], place.device(axis, -j))
        for a in range(4):
            v = qs[k][at, a].astype(jnp.float32)
            for j in range(3):
                v = v + nbs[k][j, a].astype(jnp.float32)
            tas[k][a] = v.astype(jnp.bfloat16)
        for j in (2, 1, 3):
            axis = AXES[k][0]
            wire.send(
                slots_a[k][j - 1],
                tas[k].at[place.shifted(axis, j)],
                ras[k].at[j - 1],
                place.device(axis, j),
            )
    for k in range(3):
        axis = AXES[k][0]
        v = tas[k][place.at[axis]].astype(jnp.float32)
        for j in (1, 3, 2):
            wire.recv(slots_a[k][j - 1], ras[k].at[j - 1], place.device(axis, -j))
            v = v + ras[k][j - 1].astype(jnp.float32)
        lo = starts[k]
        v = v + mine_s[:, lo : lo + widths[k]].astype(jnp.float32)
        last[t, :, lo : lo + widths[k]] = v.astype(jnp.bfloat16)
    slots_l = [wire.slot() for _ in range(7)]
    for j in (4, 3, 5, 2, 6, 1, 7):
        to = {"seq": place.s, "tp": lax.rem(t + j, 8)}
        wire.send(slots_l[j - 1], last.at[t], last.at[t], to)
    for y in range(4):
        for c in range(2):
            tt = y * 2 + c
            z, x = place.at["z"], place.at["x"]
            attended_ref[:, tt * cols : tt * cols + widths[0]] = g0[c, z, x, y]
            attended_ref[:, tt * cols + starts[1] : tt * cols + starts[2]] = g1[c, y, z, x]
            attended_ref[:, tt * cols + starts[2] : tt * cols + cols] = g2[c, x, y, z]
    for j in range(1, 8):
        tt = lax.rem(t + 8 - j, 8)
        wire.recv(slots_l[j - 1], last.at[tt], {"seq": place.s, "tp": tt})
    for tt in range(8):
        layer_ref[:, tt * cols : tt * cols + cols] = last[tt]
    wire.drain()


def second_half(part, lse, fresh, fresh_lse, x, gain, w_output, w_gate, w_up, w_down):
    rows, width = x.shape
    cols = width // 8
    ff = w_down.shape[0]
    tiles = cols // 128
    first = -(-2 * tiles // 5)
    widths = (first * 128, first * 128, (tiles - 2 * first) * 128)
    assert rows == 32 and min(widths) > 0
    bf, f32 = jnp.bfloat16, jnp.float32
    vm = pltpu.VMEM

    def each(*shape):
        return [vm(shape + (rows, w), bf) for w in widths]

    count = slots_needed()
    scratch = [
        vm(w_output.shape, bf),
        vm((width, 2 * ff), bf),
        vm(w_down.shape, bf),
        vm((7, rows, cols), bf),
        vm((7, rows, cols), bf),
        *each(2, 4, 4, 4),
        vm((4, 4, 32, 2 * ff), f32),
        vm((4, 4, 32, 128), f32),
        vm((512, ff), bf),
        *each(2, 4, 4, 4),
        *each(4, 4, 4),
        *each(2, 2, 4),
        *each(2, 2, 2, 4),
        *each(4, 4),
        *each(3, 4),
        *each(4),
        *each(3),
        vm((rows, cols), bf),
        vm((8, rows, cols), bf),
        vm((15,) + part.shape[1:], bf),
        vm((15,) + lse.shape[1:], f32),
        vm(part.shape[1:], f32),
        pltpu.SemaphoreType.DMA((4,)),
        pltpu.SemaphoreType.DMA((count,)),
        pltpu.SemaphoreType.DMA((count,)),
    ]
    whole = pl.BlockSpec(memory_space=pltpu.VMEM)
    hbm = pl.BlockSpec(memory_space=pl.ANY)
    out = jax.ShapeDtypeStruct((rows, width), bf)
    return pl.pallas_call(
        functools.partial(block_kernel, widths),
        out_shape=[out, out],
        in_specs=[whole] * 6 + [hbm] * 4,
        out_specs=[whole, whole],
        scratch_shapes=scratch,
        compiler_params=pltpu.CompilerParams(
            collective_id=1, has_side_effects=True, vmem_limit_bytes=63 * 1024 * 1024
        ),
        name="second_half",
    )(part, lse, fresh, fresh_lse, x, gain, w_output, w_gate, w_up, w_down)


class QueryGather:
    def __init__(self, wire, place, axes, buf):
        self.wire, self.place, self.buf = wire, place, buf
        self.a, self.b = axes
        self.slots_a = [wire.slot() for _ in range(3)]
        self.slots_b = [wire.slot() for _ in range(3)]

    def cut(self, b, a):
        return self.buf.at[b, a] if self.b == "z" else self.buf.at[a, b]

    def block(self, da):
        return self.cut(self.place.at[self.b], self.place.shifted(self.a, da))

    def group(self, db):
        return self.cut(self.place.shifted(self.b, db), pl.ds(0, 4))

    def open(self):
        mine = self.block(0)
        for j in (2, 1, 3):
            self.wire.send(self.slots_a[j - 1], mine, mine, self.place.device(self.a, j))

    def line(self):
        for j in (1, 3, 2):
            self.wire.recv(self.slots_a[j - 1], self.block(-j), self.place.device(self.a, -j))
        mine = self.group(0)
        for j in (2, 1, 3):
            self.wire.send(self.slots_b[j - 1], mine, mine, self.place.device(self.b, j))

    def plane(self):
        for j in (1, 3, 2):
            self.wire.recv(self.slots_b[j - 1], self.group(-j), self.place.device(self.b, -j))


def project_kernel(
    x_ref,
    gain_ref,
    freq_ref,
    slot_ref,
    length_ref,
    wq_hbm,
    wk_hbm,
    wv_hbm,
    q_all,
    fresh_ref,
    fresh_lse_ref,
    wq,
    wk,
    wv,
    q32,
    load_sem,
    send_sem,
    recv_sem,
):
    place = Place()
    wire = Wire(send_sem, recv_sem)
    rows, width = x_ref.shape
    dim = wk.shape[1]
    heads = wq.shape[1] // dim
    steps = STEPS
    own = rows // steps
    barrier = pltpu.get_barrier_semaphore()
    for axis in ("x", "z"):
        for by in (1, 2, 3):
            pl.semaphore_signal(
                barrier, inc=1, device_id=place.device(axis, by), device_id_type=MESH
            )
    chunks = load_sem.shape[0]
    depth = width // chunks
    loads = []
    for i in range(chunks):
        part = pl.ds(i * depth, depth)
        loads.append(
            [
                pltpu.make_async_copy(src.at[part], dst.at[part], load_sem.at[i, n])
                for n, (src, dst) in enumerate(((wq_hbm, wq), (wk_hbm, wk), (wv_hbm, wv)))
            ]
        )
        for load in loads[-1]:
            load.start()
    x = x_ref[...].astype(jnp.float32)
    mean = jnp.mean(x * x, axis=-1, keepdims=True)
    normed = (x * lax.rsqrt(mean + norm_eps) * gain_ref[...]).astype(jnp.bfloat16)

    shape = (own, slot_ref.shape[1])
    mine = place.s * own + lax.broadcasted_iota(jnp.int32, shape, 0)
    length = jnp.where(slot_ref[...] == mine, length_ref[...].astype(jnp.float32), 0.0)
    length = jnp.sum(length, axis=-1, keepdims=True)
    position = jnp.concatenate([length + float(i) for i in range(steps)], axis=0)
    angle = position * freq_ref[...]
    cosine = jnp.cos(angle)
    sine = jnp.sin(angle)
    low = lax.broadcasted_iota(jnp.int32, angle.shape, 1) < dim // 2
    sine = jnp.where(low, -sine, sine)

    def rotate(v):
        return v * cosine + pltpu.roll(v, dim // 2, 1) * sine

    q = k = v = 0.0
    for i in range(chunks):
        for load in loads[i]:
            load.wait()
        lhs = normed[:, i * depth : (i + 1) * depth]
        part = pl.ds(i * depth, depth)
        q = q + jnp.dot(lhs, wq[part, :], preferred_element_type=jnp.float32)
        k = k + jnp.dot(lhs, wk[part, :], preferred_element_type=jnp.float32)
        v = v + jnp.dot(lhs, wv[part, :], preferred_element_type=jnp.float32)
    for g in range(heads):
        turned = rotate(q[:, g * dim : (g + 1) * dim])
        for i in range(steps):
            q32[:, i * heads + g, :] = turned[i * own : (i + 1) * own]
    queries = q32[...].astype(jnp.bfloat16)
    s_at = (place.at["z"], place.at["x"])
    half = own // 2
    for n in range(2):
        q_all[n, s_at[0], s_at[1]] = queries[n * half : (n + 1) * half]
    gathers = [
        QueryGather(wire, place, axes, q_all.at[n])
        for n, axes in enumerate((("x", "z"), ("z", "x")))
    ]
    pl.semaphore_wait(barrier, 6)
    for g in gathers:
        g.open()

    new_k = rotate(k).astype(jnp.bfloat16)
    new_v = v.astype(jnp.bfloat16)
    count = steps * heads
    flat = queries.reshape(own * count, dim)
    s = lax.dot_general(
        flat, new_k, (((1,), (1,)), ((), ())), preferred_element_type=jnp.float32
    ) * (dim**-0.5)
    r = lax.broadcasted_iota(jnp.int32, s.shape, 0)
    c = lax.broadcasted_iota(jnp.int32, s.shape, 1)
    allowed = (r // count == c % own) & (c // own <= (r % count) // heads)
    s = jnp.where(allowed, s, masked_low)
    top = jnp.max(s, axis=-1, keepdims=True)
    w = jnp.where(allowed, jnp.exp(s - top), 0.0)
    total = jnp.sum(w, axis=-1, keepdims=True)
    acc = jnp.dot(w.astype(jnp.bfloat16), new_v, preferred_element_type=jnp.float32)
    fresh_ref[...] = acc.reshape(own, count, dim)
    shape = (own, count, dim)
    fresh_lse_ref[...] = compact(
        jnp.broadcast_to(top, (own * count, dim)).reshape(shape),
        jnp.broadcast_to(total, (own * count, dim)).reshape(shape),
    )

    for g in gathers:
        g.line()
    for g in gathers:
        g.plane()
    wire.drain()


def first_half(x, gain, slot, lengths, w_query, w_key, w_value):
    rows, width = x.shape
    dim = w_key.shape[1]
    count = STEPS * w_query.shape[1] // dim
    own = rows // STEPS
    bf, f32, vm = jnp.bfloat16, jnp.float32, pltpu.VMEM
    exponent = jnp.arange(dim // 2, dtype=f32) * (2.0 / dim)
    freq = rope_theta ** (-exponent)
    freq = jnp.concatenate([freq, freq])[None, :]
    whole = pl.BlockSpec(memory_space=pltpu.VMEM)
    hbm = pl.BlockSpec(memory_space=pl.ANY)
    return pl.pallas_call(
        project_kernel,
        out_shape=[
            jax.ShapeDtypeStruct((2, 4, 4, own // 2, count, dim), bf),
            jax.ShapeDtypeStruct((own, count, dim), f32),
            jax.ShapeDtypeStruct((own, dim), f32),
        ],
        in_specs=[whole] * 5 + [hbm] * 3,
        out_specs=[whole] * 3,
        scratch_shapes=[
            vm(w_query.shape, bf),
            vm(w_key.shape, bf),
            vm(w_value.shape, bf),
            vm((own, count, dim), f32),
            pltpu.SemaphoreType.DMA((8, 3)),
            pltpu.SemaphoreType.DMA((12,)),
            pltpu.SemaphoreType.DMA((12,)),
        ],
        compiler_params=pltpu.CompilerParams(
            collective_id=2, has_side_effects=True, vmem_limit_bytes=63 * 1024 * 1024
        ),
        name="first_half",
    )(x, gain[None, :], freq, slot[None, :], lengths[None, :], w_query, w_key, w_value)


def finish_kernel(a_ref, b_ref, c_ref, d_ref):
    c_ref[...] = a_ref[...].reshape(c_ref.shape)
    d_ref[...] = b_ref[...].reshape(d_ref.shape)


def finish(attended, layer_out, shape):
    out = jax.ShapeDtypeStruct(shape, attended.dtype)
    return pl.pallas_call(finish_kernel, out_shape=[out, out], name="finish")(attended, layer_out)


def local(
    token_inputs,
    attn_gain,
    w_query,
    key_projection,
    value_projection,
    w_output,
    mlp_gain,
    w_gate,
    w_up,
    w_down,
    key_cache,
    paged_value_cache,
    cache_lengths,
    page_request,
    page_number,
    request_slot,
):
    steps, row_count, width = token_inputs.shape
    x = token_inputs.reshape(steps * row_count, width)
    queries, fresh, fresh_lse = first_half(
        x, attn_gain, request_slot, cache_lengths, w_query, key_projection, value_projection
    )
    count, dim = queries.shape[-2:]
    seq = lax.axis_size("seq")
    queries = queries.reshape(2, seq, row_count // 2, count, dim)
    part, lse = paged_attention(
        page_request,
        page_number,
        request_slot,
        cache_lengths,
        queries,
        key_cache,
        paged_value_cache,
    )
    attended, layer_out = second_half(
        part.reshape(seq, row_count, count, dim),
        lse.reshape(seq, row_count, dim),
        fresh,
        fresh_lse,
        x,
        mlp_gain.reshape(-1, 128),
        w_output,
        w_gate,
        w_up,
        w_down,
    )
    shape = (steps, row_count, width)
    return tuple(finish(attended, layer_out, shape))


def solution(mesh):
    in_specs = (
        P(None, "seq", None),
        P(),
        P(None, "tp"),
        P(None, "tp"),
        P(None, "tp"),
        P("tp", None),
        P(),
        P(None, ("seq", "tp")),
        P(None, ("seq", "tp")),
        P(("seq", "tp"), None),
        P("seq", "tp", None, None),
        P("seq", "tp", None, None),
        P(),
        P("seq"),
        P("seq"),
        P(),
    )
    out_specs = (P(None, "seq", None), P(None, "seq", None))
    return jax.shard_map(local, mesh=mesh, in_specs=in_specs, out_specs=out_specs, check_vma=False)
```

```python
import functools

import jax
import jax.numpy as jnp
from jax import lax
from jax.experimental import pallas as pl
from jax.experimental.pallas import tpu as pltpu
from jax.sharding import PartitionSpec as P

STEPS = 4
rope_theta = 100000000.0
norm_eps = 1e-05
masked_low = -1e30


def paged_kernel(
    pages, request_ref, number_ref, slot_ref, length_ref, q_ref, k_ref, v_ref, o_ref, lse_ref, m_s, l_s, acc_s
):
    step = pl.program_id(0)
    scale = k_ref.shape[-1] ** (-0.5)
    length = k_ref.shape[1]

    @pl.when(step == 0)
    def _():
        m_s[...] = jnp.full_like(m_s, masked_low)
        l_s[...] = jnp.zeros_like(l_s)
        acc_s[...] = jnp.zeros_like(acc_s)

    stats = []
    for i in range(pages):
        page = step * pages + i
        request = request_ref[page]
        live_page = request >= 0
        request = jnp.maximum(request, 0)
        row = slot_ref[request]
        valid = jnp.clip(length_ref[request] - number_ref[page] * length, 0, length)
        valid = jnp.where(live_page, valid, 0)
        q = q_ref[(row % 8) // 4, row // 8, row % 4]
        s = (
            lax.dot_general(
                q, k_ref[i], (((1,), (1,)), ((), ())), preferred_element_type=jnp.float32
            )
            * scale
        )
        live = lax.broadcasted_iota(jnp.int32, s.shape, 1) < valid
        s = jnp.where(live, s, masked_low)
        m = jnp.max(s, axis=-1, keepdims=True)
        w = jnp.where(live, jnp.exp(s - m), 0.0)
        l = jnp.sum(w, axis=-1, keepdims=True)
        acc = jnp.dot(w.astype(jnp.bfloat16), v_ref[i], preferred_element_type=jnp.float32)
        stats.append((row, m, l, acc))
    for row, m, l, acc in stats:
        m_old = m_s[row]
        m_new = jnp.maximum(m_old, m)
        a_old = jnp.exp(m_old - m_new)
        a_new = jnp.exp(m - m_new)
        m_s[row] = m_new
        l_s[row] = l_s[row] * a_old + l * a_new
        acc_s[row] = acc_s[row] * a_old + acc * a_new

    @pl.when(step == pl.num_programs(0) - 1)
    def _():
        o_ref[...] = acc_s[...].astype(o_ref.dtype)
        lse_ref[...] = compact(m_s[...], l_s[...])


def compact(tops, sums):
    row = lax.broadcasted_iota(jnp.int32, tops.shape, 1)
    lane = lax.broadcasted_iota(jnp.int32, tops.shape, 2)
    count = tops.shape[1]
    picked = jnp.where(lane == row, tops, jnp.where(lane == row + count, sums, 0.0))
    return jnp.sum(picked, axis=1)


def expand(values, count):
    shape = (values.shape[0], count, values.shape[1])
    eye = lax.broadcasted_iota(jnp.int32, shape, 1) == lax.broadcasted_iota(jnp.int32, shape, 2)
    wide = jnp.broadcast_to(values[:, None, :], shape)
    return jnp.sum(jnp.where(eye, wide, 0.0), axis=-1, keepdims=True)


def paged_attention(request, number, slot, lengths, queries, keys, values):
    group, dim = queries.shape[-2:]
    total = slot.shape[0]
    count, _, length, _ = keys.shape
    pages = next(n for n in (12, 9, 6, 4, 3, 2, 1) if count % n == 0)
    paged = pl.BlockSpec((pages, None, length, dim), lambda i, *_: (i, 0, 0, 0))
    return pl.pallas_call(
        functools.partial(paged_kernel, pages),
        grid_spec=pltpu.PrefetchScalarGridSpec(
            num_scalar_prefetch=4,
            grid=(count // pages,),
            in_specs=[
                pl.BlockSpec(queries.shape, lambda i, *_: (0, 0, 0, 0, 0)),
                paged,
                paged,
            ],
            out_specs=[
                pl.BlockSpec((total, group, dim), lambda i, *_: (0, 0, 0)),
                pl.BlockSpec((total, dim), lambda i, *_: (0, 0)),
            ],
            scratch_shapes=[
                pltpu.VMEM((total, group, dim), jnp.float32),
                pltpu.VMEM((total, group, dim), jnp.float32),
                pltpu.VMEM((total, group, dim), jnp.float32),
            ],
        ),
        out_shape=[
            jax.ShapeDtypeStruct((total, group, dim), jnp.bfloat16),
            jax.ShapeDtypeStruct((total, dim), jnp.float32),
        ],
        name="paged_attention",
    )(request, number, slot, lengths, queries, keys, values)


AXES = (("y", "x", "z"), ("x", "z", "y"), ("z", "y", "x"))
MESH = pl.DeviceIdType.MESH


class Place:
    def __init__(self):
        s = lax.axis_index("seq")
        t = lax.axis_index("tp")
        self.at = {"z": s // 4, "x": s % 4, "y": t // 2}
        self.core = t % 2
        self.s = s
        self.t = t

    def shifted(self, axis, by):
        return lax.rem(self.at[axis] + (by + 4), 4)

    def device(self, axis=None, by=0, flip=False):
        at = dict(self.at)
        if axis is not None:
            at[axis] = self.shifted(axis, by)
        core = 1 - self.core if flip else self.core
        return {"seq": at["z"] * 4 + at["x"], "tp": at["y"] * 2 + core}


class Wire:
    def __init__(self, send_sem, recv_sem):
        self.send_sem = send_sem
        self.recv_sem = recv_sem
        self.used = 0
        self.sent = []

    def slot(self):
        self.used += 1
        return self.used - 1

    def send(self, slot, src, dst, device):
        copy = pltpu.make_async_remote_copy(
            src_ref=src,
            dst_ref=dst,
            send_sem=self.send_sem.at[slot],
            recv_sem=self.recv_sem.at[slot],
            device_id=device,
            device_id_type=MESH,
        )
        copy.start()
        self.sent.append(copy)

    def recv(self, slot, dst, device):
        pltpu.make_async_remote_copy(
            src_ref=dst,
            dst_ref=dst,
            send_sem=self.send_sem.at[slot],
            recv_sem=self.recv_sem.at[slot],
            device_id=device,
            device_id_type=MESH,
        ).wait_recv()

    def drain(self):
        for copy in self.sent:
            copy.wait_send()


def greet(place):
    barrier = pltpu.get_barrier_semaphore()
    peers = [{"seq": place.s, "tp": lax.rem(place.t + j, 8)} for j in range(1, 8)]
    peers += [{"seq": seq_peer(place, j)[0], "tp": place.t} for j in SEQ_ORDER]
    for peer in peers:
        pl.semaphore_signal(barrier, inc=1, device_id=peer, device_id_type=MESH)
    return barrier, len(peers)


SEQ_ORDER = tuple(
    sorted(
        ((dz, dx) for dz in range(4) for dx in range(4) if (dz, dx) != (0, 0)),
        key=lambda d: -(min(d[0], 4 - d[0]) + min(d[1], 4 - d[1])),
    )
)


def seq_peer(place, by):
    on = place.shifted("z", by[0]) * 4 + place.shifted("x", by[1])
    back = place.shifted("z", -by[0]) * 4 + place.shifted("x", -by[1])
    return on, back


class Gather:
    def __init__(self, wire, place, axes, buf):
        self.wire, self.place, self.buf = wire, place, buf
        self.a, self.b, self.c = axes
        self.slots_a = [wire.slot() for _ in range(3)]
        self.slots_b = [wire.slot() for _ in range(3)]
        self.slots_c = [[wire.slot() for _ in range(4)] for _ in range(4)]
        self.slots_p = [[wire.slot() for _ in range(4)] for _ in range(4)]

    def group(self, db, dc, core=None):
        place = self.place
        core = place.core if core is None else core
        return self.buf.at[core, place.shifted(self.c, dc), place.shifted(self.b, db)]

    def half(self, db, dc, which):
        place = self.place
        return self.buf.at[
            place.core, place.shifted(self.c, dc), place.shifted(self.b, db), pl.ds(2 * which, 2)
        ]

    def block(self, da):
        place = self.place
        return self.buf.at[
            place.core, place.at[self.c], place.at[self.b], place.shifted(self.a, da)
        ]

    def open(self):
        mine = self.block(0)
        for j in (2, 1, 3):
            self.wire.send(self.slots_a[j - 1], mine, mine, self.place.device(self.a, j))

    def spread(self, db):
        mine = self.group(db, 0)
        slots = self.slots_c[db]
        self.wire.send(slots[0], mine, mine, self.place.device(self.c, 1))
        self.wire.send(slots[1], mine, mine, self.place.device(self.c, -1))
        self.over(db, 0)

    def over(self, db, dc):
        mine = self.group(db, dc)
        self.wire.send(self.slots_p[db][dc], mine, mine, self.place.device(flip=True))

    def line(self):
        for j in (1, 3, 2):
            self.wire.recv(self.slots_a[j - 1], self.block(-j), self.place.device(self.a, -j))
        mine = self.group(0, 0)
        for j in (2, 1, 3):
            self.wire.send(self.slots_b[j - 1], mine, mine, self.place.device(self.b, j))
        self.spread(0)

    def plane(self, j):
        self.wire.recv(self.slots_b[j - 1], self.group(-j, 0), self.place.device(self.b, -j))
        self.spread(4 - j)

    def space_near(self, db):
        place, wire = self.place, self.wire
        slots = self.slots_c[db]
        wire.recv(slots[0], self.group(db, -1), place.device(self.c, -1))
        part = self.half(db, -1, 0)
        wire.send(slots[2], part, part, place.device(self.c, 1))
        wire.recv(slots[1], self.group(db, 1), place.device(self.c, 1))
        part = self.half(db, 1, 1)
        wire.send(slots[3], part, part, place.device(self.c, -1))
        self.over(db, 3)
        self.over(db, 1)

    def space_far(self, db):
        place, wire = self.place, self.wire
        slots = self.slots_c[db]
        wire.recv(slots[2], self.half(db, 2, 0), place.device(self.c, -1))
        wire.recv(slots[3], self.half(db, 2, 1), place.device(self.c, 1))
        self.over(db, 2)

    def other_core(self, dc):
        place = self.place
        for db in (0, 3, 1, 2):
            self.wire.recv(
                self.slots_p[db][dc], self.group(db, dc, 1 - place.core), place.device(flip=True)
            )


def add_into(dst, src, count):
    def body(i, carry):
        total = dst[i].astype(jnp.float32) + src[i].astype(jnp.float32)
        dst[i] = total.astype(dst.dtype)
        return carry

    lax.fori_loop(0, count, body, 0)


class Scatter:
    def __init__(self, wire, place, axis, piece, relay, near):
        self.wire, self.place, self.axis = wire, place, axis
        self.piece, self.relay, self.near = piece, relay, near
        self.slots = [wire.slot() for _ in range(6)]

    def open(self):
        w, p = self.wire, self.place
        up, down = p.device(self.axis, 1), p.device(self.axis, -1)
        w.send(self.slots[0], self.piece(2, 0), self.relay.at[0], up)
        w.send(self.slots[1], self.piece(2, 1), self.relay.at[1], down)
        w.send(self.slots[2], self.piece(1, 1), self.near.at[0, 1], up)
        w.send(self.slots[3], self.piece(-1, 0), self.near.at[1, 0], down)

    def pass_on(self, count):
        w, p = self.wire, self.place
        up, down = p.device(self.axis, 1), p.device(self.axis, -1)
        w.recv(self.slots[0], self.relay.at[0], down)
        add_into(self.piece(1, 0), self.relay.at[0], count)
        w.send(self.slots[4], self.piece(1, 0), self.near.at[0, 0], up)
        w.recv(self.slots[1], self.relay.at[1], up)
        add_into(self.piece(-1, 1), self.relay.at[1], count)
        w.send(self.slots[5], self.piece(-1, 1), self.near.at[1, 1], down)

    def close(self):
        w, p = self.wire, self.place
        up, down = p.device(self.axis, 1), p.device(self.axis, -1)
        w.recv(self.slots[2], self.near.at[0, 1], down)
        w.recv(self.slots[3], self.near.at[1, 0], up)
        w.recv(self.slots[4], self.near.at[0, 0], down)
        w.recv(self.slots[5], self.near.at[1, 1], up)


def slots_needed():
    return 30 + 7 + 3 * (3 + 3 + 16 + 16) + 12 + 3 * (6 + 3 + 3) + 7


def block_kernel(
    widths,
    part_ref,
    lse_ref,
    fresh_ref,
    fresh_lse_ref,
    x_ref,
    gain_ref,
    wo_hbm,
    wg_hbm,
    wu_hbm,
    wd_hbm,
    attended_ref,
    layer_ref,
    wo,
    wgu,
    wd,
    s1,
    r1,
    g0,
    g1,
    g2,
    acc,
    squares,
    act,
    p0,
    p1,
    p2,
    o0,
    o1,
    o2,
    rc0,
    rc1,
    rc2,
    nc0,
    nc1,
    nc2,
    q0,
    q1,
    q2,
    nb0,
    nb1,
    nb2,
    ta0,
    ta1,
    ta2,
    ra0,
    ra1,
    ra2,
    mine_s,
    last,
    parts,
    lses,
    att32,
    load_sem,
    send_sem,
    recv_sem,
):
    place = Place()
    t, core = place.t, place.core
    ff = wd.shape[0]
    cols = sum(widths)
    starts = (0, widths[0], widths[0] + widths[1])
    wire = Wire(send_sem, recv_sem)
    barrier, peers = greet(place)
    weights = (
        (wg_hbm, wgu.at[:, pl.ds(0, ff)]),
        (wu_hbm, wgu.at[:, pl.ds(ff, ff)]),
        (wo_hbm, wo),
        (wd_hbm, wd),
    )
    loads = [
        pltpu.make_async_copy(src, dst, load_sem.at[i]) for i, (src, dst) in enumerate(weights)
    ]
    for load in loads:
        load.start()

    def columns(index, start=0, size=cols):
        return pl.ds(pl.multiple_of(index * cols + start, 128), size)

    slots_e = [[wire.slot() for _ in range(2)] for _ in range(15)]
    pl.semaphore_wait(barrier, peers)
    for n, j in enumerate(SEQ_ORDER):
        to, _ = seq_peer(place, j)
        device = {"seq": to, "tp": t}
        wire.send(slots_e[n][0], part_ref.at[to], parts.at[n], device)
        wire.send(slots_e[n][1], lse_ref.at[to], lses.at[n], device)

    loads[0].wait()
    loads[1].wait()

    def gain_body(n, carry):
        rows = pl.ds(pl.multiple_of(n * 128, 128), 128)
        row = jnp.broadcast_to(gain_ref[pl.ds(n, 1), :], (128, 128))
        eye = lax.broadcasted_iota(jnp.int32, row.shape, 0) == lax.broadcasted_iota(
            jnp.int32, row.shape, 1
        )
        column = jnp.sum(jnp.where(eye, row, 0.0), axis=1, keepdims=True)
        wgu[rows, :] = (wgu[rows, :].astype(jnp.float32) * column).astype(wgu.dtype)
        return carry

    lax.fori_loop(0, wgu.shape[0] // 128, gain_body, 0)

    for n, j in enumerate(SEQ_ORDER):
        _, back = seq_peer(place, j)
        device = {"seq": back, "tp": t}
        wire.recv(slots_e[n][0], parts.at[n], device)
        wire.recv(slots_e[n][1], lses.at[n], device)
    count = part_ref.shape[2]
    sums = [lses[n] for n in range(15)] + [lse_ref[place.s], fresh_lse_ref[...]]
    top = functools.reduce(jnp.maximum, sums)
    shares = [jnp.exp(v - top) for v in sums]
    totals = [pltpu.roll(v, v.shape[1] - count, 1) for v in sums]
    whole = functools.reduce(jnp.add, [w * v for w, v in zip(shares, totals)])
    used = lax.broadcasted_iota(jnp.int32, top.shape, 1) < count
    shares = [jnp.where(used, w / jnp.where(used, whole, 1.0), 0.0) for w in shares]
    attention = fresh_ref[...] * expand(shares[16], count)
    for n in range(15):
        attention += parts[n].astype(jnp.float32) * expand(shares[n], count)
    attention += part_ref[place.s].astype(jnp.float32) * expand(shares[15], count)
    att32[...] = attention
    per_step = count // STEPS
    heads = jnp.concatenate(
        [
            jnp.concatenate(
                [att32[:, i * per_step + g, :].astype(jnp.bfloat16) for g in range(per_step)],
                axis=1,
            )
            for i in range(STEPS)
        ],
        axis=0,
    )

    slots1 = [wire.slot() for _ in range(7)]
    loads[2].wait()
    own = None
    for j in (4, 3, 5, 2, 6, 1, 7, 0):
        to = lax.rem(t + j, 8)
        part = jnp.dot(heads, wo[:, columns(to)], preferred_element_type=jnp.float32)
        if j == 0:
            own = part
            break
        s1[j - 1] = part.astype(s1.dtype)
        wire.send(slots1[j - 1], s1.at[j - 1], r1.at[j - 1], {"seq": place.s, "tp": to})
    total = own + x_ref[:, columns(t)].astype(jnp.float32)
    for j in (1, 7, 2, 6, 3, 5, 4):
        wire.recv(slots1[j - 1], r1.at[j - 1], {"seq": place.s, "tp": lax.rem(t + 8 - j, 8)})
        total = total + r1[j - 1].astype(jnp.float32)
    mine = total.astype(jnp.bfloat16)
    mine_s[...] = mine

    gs = (g0, g1, g2)
    gathers = [Gather(wire, place, axes, buf) for axes, buf in zip(AXES, gs)]
    for g, w, start in zip(gathers, widths, starts):
        g.buf[core, place.at[g.c], place.at[g.b], place.at[g.a]] = mine[:, start : start + w]
        g.open()
    for g in gathers:
        g.line()
    for j in (1, 3, 2):
        for g in gathers:
            g.plane(j)

    acc[...] = jnp.zeros_like(acc)
    squares[...] = jnp.zeros_like(squares)

    def squared(v):
        total = None
        for n in range(v.shape[-1] // 128):
            f = v[:, n * 128 : n * 128 + 128].astype(jnp.float32)
            total = f * f if total is None else total + f * f
        return total

    def product(v, w):
        return jnp.dot(v, w, preferred_element_type=jnp.float32)

    def take(v, w):
        acc[...] += product(v, w).reshape(acc.shape)
        squares[...] += squared(v).reshape(squares.shape)

    def use_slab(dc, c):
        y = place.shifted("y", dc)
        v = g1[c, y].reshape(512, widths[1])
        take(v, wgu[columns(y * 2 + c, starts[1], widths[1]), :])

    use_slab(0, core)
    for db in (0, 3, 1, 2):
        for g in gathers:
            g.space_near(db)
    use_slab(3, core)
    use_slab(1, core)
    gathers[1].other_core(0)
    use_slab(0, 1 - core)
    for db in (0, 3, 1, 2):
        for g in (gathers[2], gathers[1], gathers[0]):
            g.space_far(db)
    for dc in (3, 1):
        gathers[1].other_core(dc)
        use_slab(dc, 1 - core)
    use_slab(2, core)
    gathers[1].other_core(2)
    use_slab(2, 1 - core)
    for dc in range(4):
        gathers[2].other_core(dc)

    def last_body(i, carry):
        c, half = i // 2, i % 2
        vs = []
        ws = []
        for n in range(2):
            y = half * 2 + n
            v = jnp.stack([jnp.stack([g2[c, x, y, z] for x in range(4)]) for z in range(4)])
            vs.append(v.reshape(512, widths[2]))
            ws.append(wgu[columns(y * 2 + c, starts[2], widths[2]), :])
        take(jnp.concatenate(vs, axis=1), jnp.concatenate(ws, axis=0))
        return carry

    lax.fori_loop(0, 4, last_body, 0)
    for dc in range(4):
        gathers[0].other_core(dc)

    def first_body(i, carry):
        c, y = i // 4, i % 4
        v = g0[c, :, :, y].reshape(512, widths[0])
        take(v, wgu[columns(y * 2 + c, 0, widths[0]), :])
        return carry

    lax.fori_loop(0, 8, first_body, 0)

    def act_body(i, carry):
        rows = pl.ds(pl.multiple_of(i * 128, 128), 128)
        mean = jnp.sum(squares[i].reshape(128, 128), axis=-1, keepdims=True) / (8 * cols)
        r = lax.rsqrt(mean + norm_eps)
        both = acc[i].reshape(128, 2 * ff) * r
        gate = both[:, :ff]
        up = both[:, ff:]
        act[rows, :] = (gate / (1.0 + jnp.exp(-gate)) * up).astype(act.dtype)
        return carry

    lax.fori_loop(0, 4, act_body, 0)
    loads[3].wait()

    ps, os_ = (p0, p1, p2), (o0, o1, o2)

    def at_y(k, ref, y):
        return ref.at[:, :, y] if k == 0 else (ref.at[y] if k == 1 else ref.at[:, y])

    def down_rows(tt, z):
        rows = act[pl.ds(pl.multiple_of(z * 128, 128), 128), :]
        return jnp.dot(rows, wd[:, columns(tt)], preferred_element_type=jnp.float32)

    slots_o = [[wire.slot() for _ in range(3)] for _ in range(4)]
    for y in range(4):

        def other_body(z, carry):
            d = down_rows(y * 2 + 1 - core, z).astype(jnp.bfloat16).reshape(4, 32, cols)
            ps[0][1 - core, z, :, y] = d[:, :, : widths[0]]
            ps[1][1 - core, y, z] = d[:, :, starts[1] : starts[2]]
            for x in range(4):
                ps[2][1 - core, x, y, z] = d[x, :, starts[2] :]
            return carry

        lax.fori_loop(0, 4, other_body, 0)
        for k in range(3):
            wire.send(
                slots_o[y][k],
                at_y(k, ps[k].at[1 - core], y),
                at_y(k, os_[k], y),
                place.device(flip=True),
            )
    for y in range(4):
        for k in range(3):
            wire.recv(slots_o[y][k], at_y(k, os_[k], y), place.device(flip=True))

        def own_body(z, carry):
            d = down_rows(y * 2 + core, z).reshape(4, 32, cols)
            d0 = d[:, :, : widths[0]] + os_[0][z, :, y].astype(jnp.float32)
            ps[0][core, z, :, y] = d0.astype(jnp.bfloat16)
            d1 = d[:, :, starts[1] : starts[2]] + os_[1][y, z].astype(jnp.float32)
            ps[1][core, y, z] = d1.astype(jnp.bfloat16)
            for x in range(4):
                d2 = d[x, :, starts[2] :] + os_[2][x, y, z].astype(jnp.float32)
                ps[2][core, x, y, z] = d2.astype(jnp.bfloat16)
            return carry

        lax.fori_loop(0, 4, own_body, 0)

    rcs, ncs, qs = (rc0, rc1, rc2), (nc0, nc1, nc2), (q0, q1, q2)
    nbs, tas, ras = (nb0, nb1, nb2), (ta0, ta1, ta2), (ra0, ra1, ra2)

    def piece_c(k):
        def view(d, half):
            at = place.shifted(AXES[k][2], d)
            return ps[k].at[core, at, pl.ds(2 * half, 2)]

        return view

    along_c = [
        Scatter(wire, place, AXES[k][2], piece_c(k), rcs[k], ncs[k]) for k in range(3)
    ]
    slots_b = [[wire.slot() for _ in range(3)] for _ in range(3)]
    slots_a = [[wire.slot() for _ in range(3)] for _ in range(3)]
    for s in along_c:
        s.open()
    for s in along_c:
        s.pass_on(2)
    for k, s in enumerate(along_c):
        s.close()
        at = place.at[AXES[k][2]]

        def sum_c(b, carry):
            v = ps[k][core, at, b].astype(jnp.float32)
            v = v + ncs[k][0, b // 2, b % 2].astype(jnp.float32)
            v = v + ncs[k][1, b // 2, b % 2].astype(jnp.float32)
            qs[k][b] = v.astype(jnp.bfloat16)
            return carry

        lax.fori_loop(0, 4, sum_c, 0)
        axis = AXES[k][1]
        for j in (2, 1, 3):
            wire.send(
                slots_b[k][j - 1],
                qs[k].at[place.shifted(axis, j)],
                nbs[k].at[j - 1],
                place.device(axis, j),
            )
    for k in range(3):
        axis = AXES[k][1]
        at = place.at[axis]
        for j in (1, 3, 2):
            wire.recv(slots_b[k][j - 1], nbs[k].at[j - 1], place.device(axis, -j))
        for a in range(4):
            v = qs[k][at, a].astype(jnp.float32)
            for j in range(3):
                v = v + nbs[k][j, a].astype(jnp.float32)
            tas[k][a] = v.astype(jnp.bfloat16)
        for j in (2, 1, 3):
            axis = AXES[k][0]
            wire.send(
                slots_a[k][j - 1],
                tas[k].at[place.shifted(axis, j)],
                ras[k].at[j - 1],
                place.device(axis, j),
            )
    for k in range(3):
        axis = AXES[k][0]
        v = tas[k][place.at[axis]].astype(jnp.float32)
        for j in (1, 3, 2):
            wire.recv(slots_a[k][j - 1], ras[k].at[j - 1], place.device(axis, -j))
            v = v + ras[k][j - 1].astype(jnp.float32)
        lo = starts[k]
        v = v + mine_s[:, lo : lo + widths[k]].astype(jnp.float32)
        last[t, :, lo : lo + widths[k]] = v.astype(jnp.bfloat16)
    slots_l = [wire.slot() for _ in range(7)]
    for j in (4, 3, 5, 2, 6, 1, 7):
        to = {"seq": place.s, "tp": lax.rem(t + j, 8)}
        wire.send(slots_l[j - 1], last.at[t], last.at[t], to)
    for y in range(4):
        for c in range(2):
            tt = y * 2 + c
            z, x = place.at["z"], place.at["x"]
            attended_ref[:, tt * cols : tt * cols + widths[0]] = g0[c, z, x, y]
            attended_ref[:, tt * cols + starts[1] : tt * cols + starts[2]] = g1[c, y, z, x]
            attended_ref[:, tt * cols + starts[2] : tt * cols + cols] = g2[c, x, y, z]
    for j in range(1, 8):
        tt = lax.rem(t + 8 - j, 8)
        wire.recv(slots_l[j - 1], last.at[tt], {"seq": place.s, "tp": tt})
    for tt in range(8):
        layer_ref[:, tt * cols : tt * cols + cols] = last[tt]
    wire.drain()


def second_half(part, lse, fresh, fresh_lse, x, gain, w_output, w_gate, w_up, w_down):
    rows, width = x.shape
    cols = width // 8
    ff = w_down.shape[0]
    tiles = cols // 128
    first = -(-2 * tiles // 5)
    widths = (first * 128, first * 128, (tiles - 2 * first) * 128)
    assert rows == 32 and min(widths) > 0
    bf, f32 = jnp.bfloat16, jnp.float32
    vm = pltpu.VMEM

    def each(*shape):
        return [vm(shape + (rows, w), bf) for w in widths]

    count = slots_needed()
    scratch = [
        vm(w_output.shape, bf),
        vm((width, 2 * ff), bf),
        vm(w_down.shape, bf),
        vm((7, rows, cols), bf),
        vm((7, rows, cols), bf),
        *each(2, 4, 4, 4),
        vm((4, 4, 32, 2 * ff), f32),
        vm((4, 4, 32, 128), f32),
        vm((512, ff), bf),
        *each(2, 4, 4, 4),
        *each(4, 4, 4),
        *each(2, 2, 4),
        *each(2, 2, 2, 4),
        *each(4, 4),
        *each(3, 4),
        *each(4),
        *each(3),
        vm((rows, cols), bf),
        vm((8, rows, cols), bf),
        vm((15,) + part.shape[1:], bf),
        vm((15,) + lse.shape[1:], f32),
        vm(part.shape[1:], f32),
        pltpu.SemaphoreType.DMA((4,)),
        pltpu.SemaphoreType.DMA((count,)),
        pltpu.SemaphoreType.DMA((count,)),
    ]
    whole = pl.BlockSpec(memory_space=pltpu.VMEM)
    hbm = pl.BlockSpec(memory_space=pl.ANY)
    out = jax.ShapeDtypeStruct((rows, width), bf)
    return pl.pallas_call(
        functools.partial(block_kernel, widths),
        out_shape=[out, out],
        in_specs=[whole] * 6 + [hbm] * 4,
        out_specs=[whole, whole],
        scratch_shapes=scratch,
        compiler_params=pltpu.CompilerParams(
            collective_id=1, has_side_effects=True, vmem_limit_bytes=63 * 1024 * 1024
        ),
        name="second_half",
    )(part, lse, fresh, fresh_lse, x, gain, w_output, w_gate, w_up, w_down)


class QueryGather:
    def __init__(self, wire, place, axes, buf):
        self.wire, self.place, self.buf = wire, place, buf
        self.a, self.b = axes
        self.slots_a = [wire.slot() for _ in range(3)]
        self.slots_b = [wire.slot() for _ in range(3)]

    def cut(self, b, a):
        return self.buf.at[b, a] if self.b == "z" else self.buf.at[a, b]

    def block(self, da):
        return self.cut(self.place.at[self.b], self.place.shifted(self.a, da))

    def group(self, db):
        return self.cut(self.place.shifted(self.b, db), pl.ds(0, 4))

    def open(self):
        mine = self.block(0)
        for j in (2, 1, 3):
            self.wire.send(self.slots_a[j - 1], mine, mine, self.place.device(self.a, j))

    def line(self):
        for j in (1, 3, 2):
            self.wire.recv(self.slots_a[j - 1], self.block(-j), self.place.device(self.a, -j))
        mine = self.group(0)
        for j in (2, 1, 3):
            self.wire.send(self.slots_b[j - 1], mine, mine, self.place.device(self.b, j))

    def plane(self):
        for j in (1, 3, 2):
            self.wire.recv(self.slots_b[j - 1], self.group(-j), self.place.device(self.b, -j))


def project_kernel(
    x_ref,
    gain_ref,
    freq_ref,
    slot_ref,
    length_ref,
    wq_hbm,
    wk_hbm,
    wv_hbm,
    q_all,
    fresh_ref,
    fresh_lse_ref,
    wq,
    wk,
    wv,
    q32,
    load_sem,
    send_sem,
    recv_sem,
):
    place = Place()
    wire = Wire(send_sem, recv_sem)
    rows, width = x_ref.shape
    dim = wk.shape[1]
    heads = wq.shape[1] // dim
    steps = STEPS
    own = rows // steps
    barrier = pltpu.get_barrier_semaphore()
    for axis in ("x", "z"):
        for by in (1, 2, 3):
            pl.semaphore_signal(
                barrier, inc=1, device_id=place.device(axis, by), device_id_type=MESH
            )
    chunks = load_sem.shape[0]
    depth = width // chunks
    loads = []
    for i in range(chunks):
        part = pl.ds(i * depth, depth)
        loads.append(
            [
                pltpu.make_async_copy(src.at[part], dst.at[part], load_sem.at[i, n])
                for n, (src, dst) in enumerate(((wq_hbm, wq), (wk_hbm, wk), (wv_hbm, wv)))
            ]
        )
        for load in loads[-1]:
            load.start()
    x = x_ref[...].astype(jnp.float32)
    mean = jnp.mean(x * x, axis=-1, keepdims=True)
    normed = (x * lax.rsqrt(mean + norm_eps) * gain_ref[...]).astype(jnp.bfloat16)

    shape = (own, slot_ref.shape[1])
    mine = place.s * own + lax.broadcasted_iota(jnp.int32, shape, 0)
    length = jnp.where(slot_ref[...] == mine, length_ref[...].astype(jnp.float32), 0.0)
    length = jnp.sum(length, axis=-1, keepdims=True)
    position = jnp.concatenate([length + float(i) for i in range(steps)], axis=0)
    angle = position * freq_ref[...]
    cosine = jnp.cos(angle)
    sine = jnp.sin(angle)
    low = lax.broadcasted_iota(jnp.int32, angle.shape, 1) < dim // 2
    sine = jnp.where(low, -sine, sine)

    def rotate(v):
        return v * cosine + pltpu.roll(v, dim // 2, 1) * sine

    q = k = v = 0.0
    for i in range(chunks):
        for load in loads[i]:
            load.wait()
        lhs = normed[:, i * depth : (i + 1) * depth]
        part = pl.ds(i * depth, depth)
        q = q + jnp.dot(lhs, wq[part, :], preferred_element_type=jnp.float32)
        k = k + jnp.dot(lhs, wk[part, :], preferred_element_type=jnp.float32)
        v = v + jnp.dot(lhs, wv[part, :], preferred_element_type=jnp.float32)
    for g in range(heads):
        turned = rotate(q[:, g * dim : (g + 1) * dim])
        for i in range(steps):
            q32[:, i * heads + g, :] = turned[i * own : (i + 1) * own]
    queries = q32[...].astype(jnp.bfloat16)
    s_at = (place.at["z"], place.at["x"])
    half = own // 2
    for n in range(2):
        q_all[n, s_at[0], s_at[1]] = queries[n * half : (n + 1) * half]
    gathers = [
        QueryGather(wire, place, axes, q_all.at[n])
        for n, axes in enumerate((("x", "z"), ("z", "x")))
    ]
    pl.semaphore_wait(barrier, 6)
    for g in gathers:
        g.open()

    new_k = rotate(k).astype(jnp.bfloat16)
    new_v = v.astype(jnp.bfloat16)
    count = steps * heads
    flat = queries.reshape(own * count, dim)
    s = lax.dot_general(
        flat, new_k, (((1,), (1,)), ((), ())), preferred_element_type=jnp.float32
    ) * (dim**-0.5)
    r = lax.broadcasted_iota(jnp.int32, s.shape, 0)
    c = lax.broadcasted_iota(jnp.int32, s.shape, 1)
    allowed = (r // count == c % own) & (c // own <= (r % count) // heads)
    s = jnp.where(allowed, s, masked_low)
    top = jnp.max(s, axis=-1, keepdims=True)
    w = jnp.where(allowed, jnp.exp(s - top), 0.0)
    total = jnp.sum(w, axis=-1, keepdims=True)
    acc = jnp.dot(w.astype(jnp.bfloat16), new_v, preferred_element_type=jnp.float32)
    fresh_ref[...] = acc.reshape(own, count, dim)
    shape = (own, count, dim)
    fresh_lse_ref[...] = compact(
        jnp.broadcast_to(top, (own * count, dim)).reshape(shape),
        jnp.broadcast_to(total, (own * count, dim)).reshape(shape),
    )

    for g in gathers:
        g.line()
    for g in gathers:
        g.plane()
    wire.drain()


def first_half(x, gain, slot, lengths, w_query, w_key, w_value):
    rows, width = x.shape
    dim = w_key.shape[1]
    count = STEPS * w_query.shape[1] // dim
    own = rows // STEPS
    bf, f32, vm = jnp.bfloat16, jnp.float32, pltpu.VMEM
    exponent = jnp.arange(dim // 2, dtype=f32) * (2.0 / dim)
    freq = rope_theta ** (-exponent)
    freq = jnp.concatenate([freq, freq])[None, :]
    whole = pl.BlockSpec(memory_space=pltpu.VMEM)
    hbm = pl.BlockSpec(memory_space=pl.ANY)
    return pl.pallas_call(
        project_kernel,
        out_shape=[
            jax.ShapeDtypeStruct((2, 4, 4, own // 2, count, dim), bf),
            jax.ShapeDtypeStruct((own, count, dim), f32),
            jax.ShapeDtypeStruct((own, dim), f32),
        ],
        in_specs=[whole] * 5 + [hbm] * 3,
        out_specs=[whole] * 3,
        scratch_shapes=[
            vm(w_query.shape, bf),
            vm(w_key.shape, bf),
            vm(w_value.shape, bf),
            vm((own, count, dim), f32),
            pltpu.SemaphoreType.DMA((8, 3)),
            pltpu.SemaphoreType.DMA((12,)),
            pltpu.SemaphoreType.DMA((12,)),
        ],
        compiler_params=pltpu.CompilerParams(
            collective_id=2, has_side_effects=True, vmem_limit_bytes=63 * 1024 * 1024
        ),
        name="first_half",
    )(x, gain[None, :], freq, slot[None, :], lengths[None, :], w_query, w_key, w_value)


def finish_kernel(a_ref, b_ref, c_ref, d_ref):
    c_ref[...] = a_ref[...].reshape(c_ref.shape)
    d_ref[...] = b_ref[...].reshape(d_ref.shape)


def finish(attended, layer_out, shape):
    out = jax.ShapeDtypeStruct(shape, attended.dtype)
    return pl.pallas_call(finish_kernel, out_shape=[out, out], name="finish")(attended, layer_out)


def local(
    token_inputs,
    attn_gain,
    w_query,
    key_projection,
    value_projection,
    w_output,
    mlp_gain,
    w_gate,
    w_up,
    w_down,
    key_cache,
    paged_value_cache,
    cache_lengths,
    page_request,
    page_number,
    request_slot,
):
    steps, row_count, width = token_inputs.shape
    x = token_inputs.reshape(steps * row_count, width)
    queries, fresh, fresh_lse = first_half(
        x, attn_gain, request_slot, cache_lengths, w_query, key_projection, value_projection
    )
    count, dim = queries.shape[-2:]
    seq = lax.axis_size("seq")
    queries = queries.reshape(2, seq, row_count // 2, count, dim)
    part, lse = paged_attention(
        page_request,
        page_number,
        request_slot,
        cache_lengths,
        queries,
        key_cache,
        paged_value_cache,
    )
    attended, layer_out = second_half(
        part.reshape(seq, row_count, count, dim),
        lse.reshape(seq, row_count, dim),
        fresh,
        fresh_lse,
        x,
        mlp_gain.reshape(-1, 128),
        w_output,
        w_gate,
        w_up,
        w_down,
    )
    shape = (steps, row_count, width)
    return tuple(finish(attended, layer_out, shape))


def solution(mesh):
    in_specs = (
        P(None, "seq", None),
        P(),
        P(None, "tp"),
        P(None, "tp"),
        P(None, "tp"),
        P("tp", None),
        P(),
        P(None, ("seq", "tp")),
        P(None, ("seq", "tp")),
        P(("seq", "tp"), None),
        P("seq", "tp", None, None),
        P("seq", "tp", None, None),
        P(),
        P("seq"),
        P("seq"),
        P(),
    )
    out_specs = (P(None, "seq", None), P(None, "seq", None))
    return jax.shard_map(local, mesh=mesh, in_specs=in_specs, out_specs=out_specs, check_vma=False)
```

```python
import functools

import jax
import jax.numpy as jnp
import numpy as np
from jax import lax
from jax.experimental import pallas as pl
from jax.experimental.pallas import tpu as pltpu
from jax.sharding import PartitionSpec as P

STEPS = 4
rope_theta = 100000000.0
norm_eps = 1e-05
masked_low = -1e30


def paged_kernel(
    pages, request_ref, number_ref, slot_ref, length_ref, q_ref, k_ref, v_ref, o_ref, lse_ref, m_s, l_s, acc_s
):
    step = pl.program_id(0)
    scale = k_ref.shape[-1] ** (-0.5)
    length = k_ref.shape[1]

    @pl.when(step == 0)
    def _():
        m_s[...] = jnp.full_like(m_s, masked_low)
        l_s[...] = jnp.zeros_like(l_s)
        acc_s[...] = jnp.zeros_like(acc_s)

    stats = []
    for i in range(pages):
        page = step * pages + i
        request = request_ref[page]
        live_page = request >= 0
        request = jnp.maximum(request, 0)
        row = slot_ref[request]
        valid = jnp.clip(length_ref[request] - number_ref[page] * length, 0, length)
        valid = jnp.where(live_page, valid, 0)
        q = q_ref[(row % 8) // 4, row // 8, row % 4]
        s = (
            lax.dot_general(
                q, k_ref[i], (((1,), (1,)), ((), ())), preferred_element_type=jnp.float32
            )
            * scale
        )
        live = lax.broadcasted_iota(jnp.int32, s.shape, 1) < valid
        s = jnp.where(live, s, masked_low)
        m = jnp.max(s, axis=-1, keepdims=True)
        w = jnp.where(live, jnp.exp(s - m), 0.0)
        l = jnp.sum(w, axis=-1, keepdims=True)
        acc = jnp.dot(w.astype(jnp.bfloat16), v_ref[i], preferred_element_type=jnp.float32)
        stats.append((row, m, l, acc))
    for row, m, l, acc in stats:
        m_old = m_s[row]
        m_new = jnp.maximum(m_old, m)
        a_old = jnp.exp(m_old - m_new)
        a_new = jnp.exp(m - m_new)
        m_s[row] = m_new
        l_s[row] = l_s[row] * a_old + l * a_new
        acc_s[row] = acc_s[row] * a_old + acc * a_new

    @pl.when(step == pl.num_programs(0) - 1)
    def _():
        o_ref[...] = acc_s[...].astype(o_ref.dtype)
        lse_ref[...] = compact(m_s[...], l_s[...])


def compact(tops, sums):
    row = lax.broadcasted_iota(jnp.int32, tops.shape, 1)
    lane = lax.broadcasted_iota(jnp.int32, tops.shape, 2)
    count = tops.shape[1]
    picked = jnp.where(lane == row, tops, jnp.where(lane == row + count, sums, 0.0))
    return jnp.sum(picked, axis=1)


def expand(values, count):
    shape = (values.shape[0], count, values.shape[1])
    eye = lax.broadcasted_iota(jnp.int32, shape, 1) == lax.broadcasted_iota(jnp.int32, shape, 2)
    wide = jnp.broadcast_to(values[:, None, :], shape)
    return jnp.sum(jnp.where(eye, wide, 0.0), axis=-1, keepdims=True)


def paged_attention(request, number, slot, lengths, queries, keys, values):
    group, dim = queries.shape[-2:]
    total = slot.shape[0]
    count, _, length, _ = keys.shape
    pages = next(n for n in (12, 9, 6, 4, 3, 2, 1) if count % n == 0)
    paged = pl.BlockSpec((pages, None, length, dim), lambda i, *_: (i, 0, 0, 0))
    return pl.pallas_call(
        functools.partial(paged_kernel, pages),
        grid_spec=pltpu.PrefetchScalarGridSpec(
            num_scalar_prefetch=4,
            grid=(count // pages,),
            in_specs=[
                pl.BlockSpec(queries.shape, lambda i, *_: (0, 0, 0, 0, 0)),
                paged,
                paged,
            ],
            out_specs=[
                pl.BlockSpec((total, group, dim), lambda i, *_: (0, 0, 0)),
                pl.BlockSpec((total, dim), lambda i, *_: (0, 0)),
            ],
            scratch_shapes=[
                pltpu.VMEM((total, group, dim), jnp.float32),
                pltpu.VMEM((total, group, dim), jnp.float32),
                pltpu.VMEM((total, group, dim), jnp.float32),
            ],
        ),
        out_shape=[
            jax.ShapeDtypeStruct((total, group, dim), jnp.bfloat16),
            jax.ShapeDtypeStruct((total, dim), jnp.float32),
        ],
        name="paged_attention",
    )(request, number, slot, lengths, queries, keys, values)


AXES = (("y", "x", "z"), ("x", "z", "y"), ("z", "y", "x"))
MESH = pl.DeviceIdType.MESH


class Place:
    def __init__(self):
        s = lax.axis_index("seq")
        t = lax.axis_index("tp")
        self.at = {"z": s // 4, "x": s % 4, "y": t // 2}
        self.core = t % 2
        self.s = s
        self.t = t

    def shifted(self, axis, by):
        return lax.rem(self.at[axis] + (by + 4), 4)

    def device(self, axis=None, by=0, flip=False):
        at = dict(self.at)
        if axis is not None:
            at[axis] = self.shifted(axis, by)
        core = 1 - self.core if flip else self.core
        return {"seq": at["z"] * 4 + at["x"], "tp": at["y"] * 2 + core}


class Wire:
    def __init__(self, send_sem, recv_sem):
        self.send_sem = send_sem
        self.recv_sem = recv_sem
        self.used = 0
        self.sent = []

    def slot(self):
        self.used += 1
        return self.used - 1

    def send(self, slot, src, dst, device):
        copy = pltpu.make_async_remote_copy(
            src_ref=src,
            dst_ref=dst,
            send_sem=self.send_sem.at[slot],
            recv_sem=self.recv_sem.at[slot],
            device_id=device,
            device_id_type=MESH,
        )
        copy.start()
        self.sent.append(copy)

    def recv(self, slot, dst, device):
        pltpu.make_async_remote_copy(
            src_ref=dst,
            dst_ref=dst,
            send_sem=self.send_sem.at[slot],
            recv_sem=self.recv_sem.at[slot],
            device_id=device,
            device_id_type=MESH,
        ).wait_recv()

    def drain(self):
        for copy in self.sent:
            copy.wait_send()


def greet(place):
    barrier = pltpu.get_barrier_semaphore()
    peers = [{"seq": place.s, "tp": lax.rem(place.t + j, 8)} for j in range(1, 8)]
    peers += [{"seq": seq_peer(place, j)[0], "tp": place.t} for j in SEQ_ORDER]
    for peer in peers:
        pl.semaphore_signal(barrier, inc=1, device_id=peer, device_id_type=MESH)
    return barrier, len(peers)


SEQ_ORDER = tuple(
    sorted(
        ((dz, dx) for dz in range(4) for dx in range(4) if (dz, dx) != (0, 0)),
        key=lambda d: -(min(d[0], 4 - d[0]) + min(d[1], 4 - d[1])),
    )
)


def seq_peer(place, by):
    on = place.shifted("z", by[0]) * 4 + place.shifted("x", by[1])
    back = place.shifted("z", -by[0]) * 4 + place.shifted("x", -by[1])
    return on, back


class Gather:
    def __init__(self, wire, place, axes, buf):
        self.wire, self.place, self.buf = wire, place, buf
        self.a, self.b, self.c = axes
        self.slots_a = [wire.slot() for _ in range(3)]
        self.slots_b = [wire.slot() for _ in range(3)]
        self.slots_c = [[wire.slot() for _ in range(4)] for _ in range(4)]
        self.slots_p = [[wire.slot() for _ in range(4)] for _ in range(4)]

    def group(self, db, dc, core=None):
        place = self.place
        core = place.core if core is None else core
        return self.buf.at[core, place.shifted(self.c, dc), place.shifted(self.b, db)]

    def half(self, db, dc, which):
        place = self.place
        return self.buf.at[
            place.core, place.shifted(self.c, dc), place.shifted(self.b, db), pl.ds(2 * which, 2)
        ]

    def block(self, da):
        place = self.place
        return self.buf.at[
            place.core, place.at[self.c], place.at[self.b], place.shifted(self.a, da)
        ]

    def open(self):
        mine = self.block(0)
        for j in (2, 1, 3):
            self.wire.send(self.slots_a[j - 1], mine, mine, self.place.device(self.a, j))

    def spread(self, db):
        mine = self.group(db, 0)
        slots = self.slots_c[db]
        self.wire.send(slots[0], mine, mine, self.place.device(self.c, 1))
        self.wire.send(slots[1], mine, mine, self.place.device(self.c, -1))
        self.over(db, 0)

    def over(self, db, dc):
        mine = self.group(db, dc)
        self.wire.send(self.slots_p[db][dc], mine, mine, self.place.device(flip=True))

    def line(self):
        for j in (1, 3, 2):
            self.wire.recv(self.slots_a[j - 1], self.block(-j), self.place.device(self.a, -j))
        mine = self.group(0, 0)
        for j in (2, 1, 3):
            self.wire.send(self.slots_b[j - 1], mine, mine, self.place.device(self.b, j))

    def plane(self, j):
        self.wire.recv(self.slots_b[j - 1], self.group(-j, 0), self.place.device(self.b, -j))
        self.spread(4 - j)

    def space_near(self, db):
        place, wire = self.place, self.wire
        slots = self.slots_c[db]
        wire.recv(slots[0], self.group(db, -1), place.device(self.c, -1))
        part = self.half(db, -1, 0)
        wire.send(slots[2], part, part, place.device(self.c, 1))
        wire.recv(slots[1], self.group(db, 1), place.device(self.c, 1))
        part = self.half(db, 1, 1)
        wire.send(slots[3], part, part, place.device(self.c, -1))
        self.over(db, 3)
        self.over(db, 1)

    def space_far(self, db):
        place, wire = self.place, self.wire
        slots = self.slots_c[db]
        wire.recv(slots[2], self.half(db, 2, 0), place.device(self.c, -1))
        wire.recv(slots[3], self.half(db, 2, 1), place.device(self.c, 1))
        self.over(db, 2)

    def other_core(self, dc):
        place = self.place
        for db in (0, 3, 1, 2):
            self.wire.recv(
                self.slots_p[db][dc], self.group(db, dc, 1 - place.core), place.device(flip=True)
            )


def add_into(dst, src, count):
    def body(i, carry):
        total = dst[i].astype(jnp.float32) + src[i].astype(jnp.float32)
        dst[i] = total.astype(dst.dtype)
        return carry

    lax.fori_loop(0, count, body, 0)


class Scatter:
    def __init__(self, wire, place, axis, piece, relay, near):
        self.wire, self.place, self.axis = wire, place, axis
        self.piece, self.relay, self.near = piece, relay, near
        self.slots = [wire.slot() for _ in range(6)]

    def open(self):
        w, p = self.wire, self.place
        up, down = p.device(self.axis, 1), p.device(self.axis, -1)
        w.send(self.slots[0], self.piece(2, 0), self.relay.at[0], up)
        w.send(self.slots[1], self.piece(2, 1), self.relay.at[1], down)
        w.send(self.slots[2], self.piece(1, 1), self.near.at[0, 1], up)
        w.send(self.slots[3], self.piece(-1, 0), self.near.at[1, 0], down)

    def pass_on(self, count):
        w, p = self.wire, self.place
        up, down = p.device(self.axis, 1), p.device(self.axis, -1)
        w.recv(self.slots[0], self.relay.at[0], down)
        add_into(self.piece(1, 0), self.relay.at[0], count)
        w.send(self.slots[4], self.piece(1, 0), self.near.at[0, 0], up)
        w.recv(self.slots[1], self.relay.at[1], up)
        add_into(self.piece(-1, 1), self.relay.at[1], count)
        w.send(self.slots[5], self.piece(-1, 1), self.near.at[1, 1], down)

    def close(self):
        w, p = self.wire, self.place
        up, down = p.device(self.axis, 1), p.device(self.axis, -1)
        w.recv(self.slots[2], self.near.at[0, 1], down)
        w.recv(self.slots[3], self.near.at[1, 0], up)
        w.recv(self.slots[4], self.near.at[0, 0], down)
        w.recv(self.slots[5], self.near.at[1, 1], up)


def slots_needed():
    return 30 + 7 + 3 * (3 + 3 + 16 + 16) + 12 + 3 * (6 + 3 + 3) + 7


def block_kernel(
    widths,
    part_ref,
    lse_ref,
    fresh_ref,
    fresh_lse_ref,
    x_ref,
    gain_ref,
    wo_hbm,
    wg_hbm,
    wu_hbm,
    wd_hbm,
    attended_ref,
    layer_ref,
    wo,
    wgu,
    wd,
    s1,
    r1,
    g0,
    g1,
    g2,
    acc,
    squares,
    act,
    p0,
    p1,
    p2,
    o0,
    o1,
    o2,
    rc0,
    rc1,
    rc2,
    nc0,
    nc1,
    nc2,
    q0,
    q1,
    q2,
    nb0,
    nb1,
    nb2,
    ta0,
    ta1,
    ta2,
    ra0,
    ra1,
    ra2,
    mine_s,
    last,
    parts,
    lses,
    att32,
    load_sem,
    send_sem,
    recv_sem,
):
    place = Place()
    t, core = place.t, place.core
    ff = wd.shape[0]
    cols = sum(widths)
    starts = (0, widths[0], widths[0] + widths[1])
    wire = Wire(send_sem, recv_sem)
    barrier, peers = greet(place)
    weights = (
        (wg_hbm, wgu.at[:, pl.ds(0, ff)]),
        (wu_hbm, wgu.at[:, pl.ds(ff, ff)]),
        (wo_hbm, wo),
        (wd_hbm, wd),
    )
    loads = [
        pltpu.make_async_copy(src, dst, load_sem.at[i]) for i, (src, dst) in enumerate(weights)
    ]
    for load in loads:
        load.start()

    def columns(index, start=0, size=cols):
        return pl.ds(pl.multiple_of(index * cols + start, 128), size)

    slots_e = [[wire.slot() for _ in range(2)] for _ in range(15)]
    pl.semaphore_wait(barrier, peers)
    for n, j in enumerate(SEQ_ORDER):
        to, _ = seq_peer(place, j)
        device = {"seq": to, "tp": t}
        wire.send(slots_e[n][0], part_ref.at[to], parts.at[n], device)
        wire.send(slots_e[n][1], lse_ref.at[to], lses.at[n], device)

    loads[0].wait()
    loads[1].wait()

    def gain_body(n, carry):
        rows = pl.ds(pl.multiple_of(n * 128, 128), 128)
        row = jnp.broadcast_to(gain_ref[pl.ds(n, 1), :], (128, 128))
        eye = lax.broadcasted_iota(jnp.int32, row.shape, 0) == lax.broadcasted_iota(
            jnp.int32, row.shape, 1
        )
        column = jnp.sum(jnp.where(eye, row, 0.0), axis=1, keepdims=True)
        wgu[rows, :] = (wgu[rows, :].astype(jnp.float32) * column).astype(wgu.dtype)
        return carry

    lax.fori_loop(0, wgu.shape[0] // 128, gain_body, 0)

    for n, j in enumerate(SEQ_ORDER):
        _, back = seq_peer(place, j)
        device = {"seq": back, "tp": t}
        wire.recv(slots_e[n][0], parts.at[n], device)
        wire.recv(slots_e[n][1], lses.at[n], device)
    count = part_ref.shape[2]
    sums = [lses[n] for n in range(15)] + [lse_ref[place.s], fresh_lse_ref[...]]
    top = functools.reduce(jnp.maximum, sums)
    shares = [jnp.exp(v - top) for v in sums]
    totals = [pltpu.roll(v, v.shape[1] - count, 1) for v in sums]
    whole = functools.reduce(jnp.add, [w * v for w, v in zip(shares, totals)])
    used = lax.broadcasted_iota(jnp.int32, top.shape, 1) < count
    shares = [jnp.where(used, w / jnp.where(used, whole, 1.0), 0.0) for w in shares]
    attention = fresh_ref[...] * expand(shares[16], count)
    for n in range(15):
        attention += parts[n].astype(jnp.float32) * expand(shares[n], count)
    attention += part_ref[place.s].astype(jnp.float32) * expand(shares[15], count)
    att32[...] = attention
    per_step = count // STEPS
    heads = jnp.concatenate(
        [
            jnp.concatenate(
                [att32[:, i * per_step + g, :].astype(jnp.bfloat16) for g in range(per_step)],
                axis=1,
            )
            for i in range(STEPS)
        ],
        axis=0,
    )

    slots1 = [wire.slot() for _ in range(7)]
    loads[2].wait()
    own = None
    for j in (4, 3, 5, 2, 6, 1, 7, 0):
        to = lax.rem(t + j, 8)
        part = jnp.dot(heads, wo[:, columns(to)], preferred_element_type=jnp.float32)
        if j == 0:
            own = part
            break
        s1[j - 1] = part.astype(s1.dtype)
        wire.send(slots1[j - 1], s1.at[j - 1], r1.at[j - 1], {"seq": place.s, "tp": to})
    total = own + x_ref[:, columns(t)].astype(jnp.float32)
    for j in (1, 7, 2, 6, 3, 5, 4):
        wire.recv(slots1[j - 1], r1.at[j - 1], {"seq": place.s, "tp": lax.rem(t + 8 - j, 8)})
        total = total + r1[j - 1].astype(jnp.float32)
    mine = total.astype(jnp.bfloat16)
    mine_s[...] = mine

    gs = (g0, g1, g2)
    gathers = [Gather(wire, place, axes, buf) for axes, buf in zip(AXES, gs)]
    for g, w, start in zip(gathers, widths, starts):
        g.buf[core, place.at[g.c], place.at[g.b], place.at[g.a]] = mine[:, start : start + w]
        g.open()
    for g in gathers:
        g.line()
    for j in (1, 3, 2):
        for g in gathers:
            g.plane(j)
            if j == 1:
                g.spread(0)

    acc[...] = jnp.zeros_like(acc)
    squares[...] = jnp.zeros_like(squares)

    def squared(v):
        total = None
        for n in range(v.shape[-1] // 128):
            f = v[:, n * 128 : n * 128 + 128].astype(jnp.float32)
            total = f * f if total is None else total + f * f
        return total

    def product(v, w):
        return jnp.dot(v, w, preferred_element_type=jnp.float32)

    def take(v, w):
        acc[...] += product(v, w).reshape(acc.shape)
        squares[...] += squared(v).reshape(squares.shape)

    def use_slab(dc, c):
        y = place.shifted("y", dc)
        v = g1[c, y].reshape(512, widths[1])
        take(v, wgu[columns(y * 2 + c, starts[1], widths[1]), :])

    use_slab(0, core)
    for db in (0, 3, 1, 2):
        for g in gathers:
            g.space_near(db)
    use_slab(3, core)
    use_slab(1, core)
    gathers[1].other_core(0)
    use_slab(0, 1 - core)
    for db in (0, 3, 1, 2):
        for g in (gathers[2], gathers[1], gathers[0]):
            g.space_far(db)
    for dc in (3, 1):
        gathers[1].other_core(dc)
        use_slab(dc, 1 - core)
    use_slab(2, core)
    gathers[1].other_core(2)
    use_slab(2, 1 - core)
    for dc in range(4):
        gathers[2].other_core(dc)

    def last_body(i, carry):
        c, half = i // 2, i % 2
        vs = []
        ws = []
        for n in range(2):
            y = half * 2 + n
            v = jnp.stack([jnp.stack([g2[c, x, y, z] for x in range(4)]) for z in range(4)])
            vs.append(v.reshape(512, widths[2]))
            ws.append(wgu[columns(y * 2 + c, starts[2], widths[2]), :])
        take(jnp.concatenate(vs, axis=1), jnp.concatenate(ws, axis=0))
        return carry

    lax.fori_loop(0, 4, last_body, 0)
    for dc in range(4):
        gathers[0].other_core(dc)

    def first_body(i, carry):
        c, y = i // 4, i % 4
        v = g0[c, :, :, y].reshape(512, widths[0])
        take(v, wgu[columns(y * 2 + c, 0, widths[0]), :])
        return carry

    lax.fori_loop(0, 8, first_body, 0)

    def act_body(i, carry):
        rows = pl.ds(pl.multiple_of(i * 128, 128), 128)
        mean = jnp.sum(squares[i].reshape(128, 128), axis=-1, keepdims=True) / (8 * cols)
        r = lax.rsqrt(mean + norm_eps)
        both = acc[i].reshape(128, 2 * ff) * r
        gate = both[:, :ff]
        up = both[:, ff:]
        act[rows, :] = (gate / (1.0 + jnp.exp(-gate)) * up).astype(act.dtype)
        return carry

    lax.fori_loop(0, 4, act_body, 0)
    loads[3].wait()

    ps, os_ = (p0, p1, p2), (o0, o1, o2)

    def at_y(k, ref, y):
        return ref.at[:, :, y] if k == 0 else (ref.at[y] if k == 1 else ref.at[:, y])

    def down_rows(tt, z):
        rows = act[pl.ds(pl.multiple_of(z * 128, 128), 128), :]
        return jnp.dot(rows, wd[:, columns(tt)], preferred_element_type=jnp.float32)

    slots_o = [[wire.slot() for _ in range(3)] for _ in range(4)]
    for y in range(4):

        def other_body(z, carry):
            d = down_rows(y * 2 + 1 - core, z).astype(jnp.bfloat16).reshape(4, 32, cols)
            ps[0][1 - core, z, :, y] = d[:, :, : widths[0]]
            ps[1][1 - core, y, z] = d[:, :, starts[1] : starts[2]]
            for x in range(4):
                ps[2][1 - core, x, y, z] = d[x, :, starts[2] :]
            return carry

        lax.fori_loop(0, 4, other_body, 0)
        for k in range(3):
            wire.send(
                slots_o[y][k],
                at_y(k, ps[k].at[1 - core], y),
                at_y(k, os_[k], y),
                place.device(flip=True),
            )
    for y in range(4):
        for k in range(3):
            wire.recv(slots_o[y][k], at_y(k, os_[k], y), place.device(flip=True))

        def own_body(z, carry):
            d = down_rows(y * 2 + core, z).reshape(4, 32, cols)
            d0 = d[:, :, : widths[0]] + os_[0][z, :, y].astype(jnp.float32)
            ps[0][core, z, :, y] = d0.astype(jnp.bfloat16)
            d1 = d[:, :, starts[1] : starts[2]] + os_[1][y, z].astype(jnp.float32)
            ps[1][core, y, z] = d1.astype(jnp.bfloat16)
            for x in range(4):
                d2 = d[x, :, starts[2] :] + os_[2][x, y, z].astype(jnp.float32)
                ps[2][core, x, y, z] = d2.astype(jnp.bfloat16)
            return carry

        lax.fori_loop(0, 4, own_body, 0)

    rcs, ncs, qs = (rc0, rc1, rc2), (nc0, nc1, nc2), (q0, q1, q2)
    nbs, tas, ras = (nb0, nb1, nb2), (ta0, ta1, ta2), (ra0, ra1, ra2)

    def piece_c(k):
        def view(d, half):
            at = place.shifted(AXES[k][2], d)
            return ps[k].at[core, at, pl.ds(2 * half, 2)]

        return view

    along_c = [
        Scatter(wire, place, AXES[k][2], piece_c(k), rcs[k], ncs[k]) for k in range(3)
    ]
    slots_b = [[wire.slot() for _ in range(3)] for _ in range(3)]
    slots_a = [[wire.slot() for _ in range(3)] for _ in range(3)]
    for s in along_c:
        s.open()
    for s in along_c:
        s.pass_on(2)
    for k, s in enumerate(along_c):
        s.close()
        at = place.at[AXES[k][2]]

        def sum_c(b, carry):
            v = ps[k][core, at, b].astype(jnp.float32)
            v = v + ncs[k][0, b // 2, b % 2].astype(jnp.float32)
            v = v + ncs[k][1, b // 2, b % 2].astype(jnp.float32)
            qs[k][b] = v.astype(jnp.bfloat16)
            return carry

        lax.fori_loop(0, 4, sum_c, 0)
        axis = AXES[k][1]
        for j in (2, 1, 3):
            wire.send(
                slots_b[k][j - 1],
                qs[k].at[place.shifted(axis, j)],
                nbs[k].at[j - 1],
                place.device(axis, j),
            )
    for k in range(3):
        axis = AXES[k][1]
        at = place.at[axis]
        for j in (1, 3, 2):
            wire.recv(slots_b[k][j - 1], nbs[k].at[j - 1], place.device(axis, -j))
        for a in range(4):
            v = qs[k][at, a].astype(jnp.float32)
            for j in range(3):
                v = v + nbs[k][j, a].astype(jnp.float32)
            tas[k][a] = v.astype(jnp.bfloat16)
        for j in (2, 1, 3):
            axis = AXES[k][0]
            wire.send(
                slots_a[k][j - 1],
                tas[k].at[place.shifted(axis, j)],
                ras[k].at[j - 1],
                place.device(axis, j),
            )
    for k in range(3):
        axis = AXES[k][0]
        v = tas[k][place.at[axis]].astype(jnp.float32)
        for j in (1, 3, 2):
            wire.recv(slots_a[k][j - 1], ras[k].at[j - 1], place.device(axis, -j))
            v = v + ras[k][j - 1].astype(jnp.float32)
        lo = starts[k]
        v = v + mine_s[:, lo : lo + widths[k]].astype(jnp.float32)
        last[t, :, lo : lo + widths[k]] = v.astype(jnp.bfloat16)
    slots_l = [wire.slot() for _ in range(7)]
    for j in (4, 3, 5, 2, 6, 1, 7):
        to = {"seq": place.s, "tp": lax.rem(t + j, 8)}
        wire.send(slots_l[j - 1], last.at[t], last.at[t], to)
    for y in range(4):
        for c in range(2):
            tt = y * 2 + c
            z, x = place.at["z"], place.at["x"]
            attended_ref[:, tt * cols : tt * cols + widths[0]] = g0[c, z, x, y]
            attended_ref[:, tt * cols + starts[1] : tt * cols + starts[2]] = g1[c, y, z, x]
            attended_ref[:, tt * cols + starts[2] : tt * cols + cols] = g2[c, x, y, z]
    for j in range(1, 8):
        tt = lax.rem(t + 8 - j, 8)
        wire.recv(slots_l[j - 1], last.at[tt], {"seq": place.s, "tp": tt})
    for tt in range(8):
        layer_ref[:, tt * cols : tt * cols + cols] = last[tt]
    wire.drain()


def second_half(part, lse, fresh, fresh_lse, x, gain, w_output, w_gate, w_up, w_down):
    rows, width = x.shape
    cols = width // 8
    ff = w_down.shape[0]
    tiles = cols // 128
    first = -(-2 * tiles // 5)
    widths = (first * 128, first * 128, (tiles - 2 * first) * 128)
    assert rows == 32 and min(widths) > 0
    bf, f32 = jnp.bfloat16, jnp.float32
    vm = pltpu.VMEM

    def each(*shape):
        return [vm(shape + (rows, w), bf) for w in widths]

    count = slots_needed()
    scratch = [
        vm(w_output.shape, bf),
        vm((width, 2 * ff), bf),
        vm(w_down.shape, bf),
        vm((7, rows, cols), bf),
        vm((7, rows, cols), bf),
        *each(2, 4, 4, 4),
        vm((4, 4, 32, 2 * ff), f32),
        vm((4, 4, 32, 128), f32),
        vm((512, ff), bf),
        *each(2, 4, 4, 4),
        *each(4, 4, 4),
        *each(2, 2, 4),
        *each(2, 2, 2, 4),
        *each(4, 4),
        *each(3, 4),
        *each(4),
        *each(3),
        vm((rows, cols), bf),
        vm((8, rows, cols), bf),
        vm((15,) + part.shape[1:], bf),
        vm((15,) + lse.shape[1:], f32),
        vm(part.shape[1:], f32),
        pltpu.SemaphoreType.DMA((4,)),
        pltpu.SemaphoreType.DMA((count,)),
        pltpu.SemaphoreType.DMA((count,)),
    ]
    whole = pl.BlockSpec(memory_space=pltpu.VMEM)
    hbm = pl.BlockSpec(memory_space=pl.ANY)
    out = jax.ShapeDtypeStruct((rows, width), bf)
    return pl.pallas_call(
        functools.partial(block_kernel, widths),
        out_shape=[out, out],
        in_specs=[whole] * 6 + [hbm] * 4,
        out_specs=[whole, whole],
        scratch_shapes=scratch,
        compiler_params=pltpu.CompilerParams(
            collective_id=1, has_side_effects=True, vmem_limit_bytes=63 * 1024 * 1024
        ),
        name="second_half",
    )(part, lse, fresh, fresh_lse, x, gain, w_output, w_gate, w_up, w_down)


class QueryGather:
    def __init__(self, wire, place, axes, buf):
        self.wire, self.place, self.buf = wire, place, buf
        self.a, self.b = axes
        self.slots_a = [wire.slot() for _ in range(3)]
        self.slots_b = [wire.slot() for _ in range(3)]

    def cut(self, b, a):
        return self.buf.at[b, a] if self.b == "z" else self.buf.at[a, b]

    def block(self, da):
        return self.cut(self.place.at[self.b], self.place.shifted(self.a, da))

    def group(self, db):
        return self.cut(self.place.shifted(self.b, db), pl.ds(0, 4))

    def open(self):
        mine = self.block(0)
        for j in (2, 1, 3):
            self.wire.send(self.slots_a[j - 1], mine, mine, self.place.device(self.a, j))

    def line(self):
        for j in (1, 3, 2):
            self.wire.recv(self.slots_a[j - 1], self.block(-j), self.place.device(self.a, -j))
        mine = self.group(0)
        for j in (2, 1, 3):
            self.wire.send(self.slots_b[j - 1], mine, mine, self.place.device(self.b, j))

    def plane(self):
        for j in (1, 3, 2):
            self.wire.recv(self.slots_b[j - 1], self.group(-j), self.place.device(self.b, -j))


def project_kernel(
    x_ref,
    gain_ref,
    freq_ref,
    slot_ref,
    length_ref,
    wq_hbm,
    wk_hbm,
    wv_hbm,
    q_all,
    fresh_ref,
    fresh_lse_ref,
    wq,
    wk,
    wv,
    q32,
    load_sem,
    send_sem,
    recv_sem,
):
    place = Place()
    wire = Wire(send_sem, recv_sem)
    rows, width = x_ref.shape
    dim = wk.shape[1]
    heads = wq.shape[1] // dim
    steps = STEPS
    own = rows // steps
    barrier = pltpu.get_barrier_semaphore()
    for axis in ("x", "z"):
        for by in (1, 2, 3):
            pl.semaphore_signal(
                barrier, inc=1, device_id=place.device(axis, by), device_id_type=MESH
            )
    chunks = load_sem.shape[0]
    depth = width // chunks
    loads = []
    for i in range(chunks):
        part = pl.ds(i * depth, depth)
        loads.append(
            [
                pltpu.make_async_copy(src.at[part], dst.at[part], load_sem.at[i, n])
                for n, (src, dst) in enumerate(((wq_hbm, wq), (wk_hbm, wk), (wv_hbm, wv)))
            ]
        )
        for load in loads[-1]:
            load.start()
    x = x_ref[...].astype(jnp.float32)
    mean = jnp.mean(x * x, axis=-1, keepdims=True)
    normed = (x * lax.rsqrt(mean + norm_eps) * gain_ref[...]).astype(jnp.bfloat16)

    shape = (own, slot_ref.shape[1])
    mine = place.s * own + lax.broadcasted_iota(jnp.int32, shape, 0)
    length = jnp.where(slot_ref[...] == mine, length_ref[...].astype(jnp.float32), 0.0)
    length = jnp.sum(length, axis=-1, keepdims=True)
    position = jnp.concatenate([length + float(i) for i in range(steps)], axis=0)
    angle = position * freq_ref[...]
    cosine = jnp.cos(angle)
    sine = jnp.sin(angle)
    low = lax.broadcasted_iota(jnp.int32, angle.shape, 1) < dim // 2
    sine = jnp.where(low, -sine, sine)

    def rotate(v):
        return v * cosine + pltpu.roll(v, dim // 2, 1) * sine

    q = k = v = 0.0
    for i in range(chunks):
        for load in loads[i]:
            load.wait()
        lhs = normed[:, i * depth : (i + 1) * depth]
        part = pl.ds(i * depth, depth)
        q = q + jnp.dot(lhs, wq[part, :], preferred_element_type=jnp.float32)
        k = k + jnp.dot(lhs, wk[part, :], preferred_element_type=jnp.float32)
        v = v + jnp.dot(lhs, wv[part, :], preferred_element_type=jnp.float32)
    for g in range(heads):
        turned = rotate(q[:, g * dim : (g + 1) * dim])
        for i in range(steps):
            q32[:, i * heads + g, :] = turned[i * own : (i + 1) * own]
    queries = q32[...].astype(jnp.bfloat16)
    s_at = (place.at["z"], place.at["x"])
    half = own // 2
    for n in range(2):
        q_all[n, s_at[0], s_at[1]] = queries[n * half : (n + 1) * half]
    gathers = [
        QueryGather(wire, place, axes, q_all.at[n])
        for n, axes in enumerate((("x", "z"), ("z", "x")))
    ]
    pl.semaphore_wait(barrier, 6)
    for g in gathers:
        g.open()

    new_k = rotate(k).astype(jnp.bfloat16)
    new_v = v.astype(jnp.bfloat16)
    count = steps * heads
    flat = queries.reshape(own * count, dim)
    s = lax.dot_general(
        flat, new_k, (((1,), (1,)), ((), ())), preferred_element_type=jnp.float32
    ) * (dim**-0.5)
    r = lax.broadcasted_iota(jnp.int32, s.shape, 0)
    c = lax.broadcasted_iota(jnp.int32, s.shape, 1)
    allowed = (r // count == c % own) & (c // own <= (r % count) // heads)
    s = jnp.where(allowed, s, masked_low)
    top = jnp.max(s, axis=-1, keepdims=True)
    w = jnp.where(allowed, jnp.exp(s - top), 0.0)
    total = jnp.sum(w, axis=-1, keepdims=True)
    acc = jnp.dot(w.astype(jnp.bfloat16), new_v, preferred_element_type=jnp.float32)
    fresh_ref[...] = acc.reshape(own, count, dim)
    shape = (own, count, dim)
    fresh_lse_ref[...] = compact(
        jnp.broadcast_to(top, (own * count, dim)).reshape(shape),
        jnp.broadcast_to(total, (own * count, dim)).reshape(shape),
    )

    for g in gathers:
        g.line()
    for g in gathers:
        g.plane()
    wire.drain()


def first_half(x, gain, slot, lengths, w_query, w_key, w_value):
    rows, width = x.shape
    dim = w_key.shape[1]
    count = STEPS * w_query.shape[1] // dim
    own = rows // STEPS
    bf, f32, vm = jnp.bfloat16, jnp.float32, pltpu.VMEM
    exponent = np.arange(dim // 2, dtype=np.float32) * np.float32(2.0 / dim)
    freq = (rope_theta ** -exponent.astype(np.float64)).astype(np.float32)
    freq = jnp.asarray(np.concatenate([freq, freq])[None, :])
    whole = pl.BlockSpec(memory_space=pltpu.VMEM)
    hbm = pl.BlockSpec(memory_space=pl.ANY)
    return pl.pallas_call(
        project_kernel,
        out_shape=[
            jax.ShapeDtypeStruct((2, 4, 4, own // 2, count, dim), bf),
            jax.ShapeDtypeStruct((own, count, dim), f32),
            jax.ShapeDtypeStruct((own, dim), f32),
        ],
        in_specs=[whole] * 5 + [hbm] * 3,
        out_specs=[whole] * 3,
        scratch_shapes=[
            vm(w_query.shape, bf),
            vm(w_key.shape, bf),
            vm(w_value.shape, bf),
            vm((own, count, dim), f32),
            pltpu.SemaphoreType.DMA((8, 3)),
            pltpu.SemaphoreType.DMA((12,)),
            pltpu.SemaphoreType.DMA((12,)),
        ],
        compiler_params=pltpu.CompilerParams(
            collective_id=2, has_side_effects=True, vmem_limit_bytes=63 * 1024 * 1024
        ),
        name="first_half",
    )(x, gain[None, :], freq, slot[None, :], lengths[None, :], w_query, w_key, w_value)


def finish_kernel(a_ref, b_ref, c_ref, d_ref):
    c_ref[...] = a_ref[...].reshape(c_ref.shape)
    d_ref[...] = b_ref[...].reshape(d_ref.shape)


def finish(attended, layer_out, shape):
    out = jax.ShapeDtypeStruct(shape, attended.dtype)
    return pl.pallas_call(finish_kernel, out_shape=[out, out], name="finish")(attended, layer_out)


def local(
    token_inputs,
    attn_gain,
    w_query,
    key_projection,
    value_projection,
    w_output,
    mlp_gain,
    w_gate,
    w_up,
    w_down,
    key_cache,
    paged_value_cache,
    cache_lengths,
    page_request,
    page_number,
    request_slot,
):
    steps, row_count, width = token_inputs.shape
    x = token_inputs.reshape(steps * row_count, width)
    queries, fresh, fresh_lse = first_half(
        x, attn_gain, request_slot, cache_lengths, w_query, key_projection, value_projection
    )
    count, dim = queries.shape[-2:]
    seq = lax.axis_size("seq")
    queries = queries.reshape(2, seq, row_count // 2, count, dim)
    part, lse = paged_attention(
        page_request,
        page_number,
        request_slot,
        cache_lengths,
        queries,
        key_cache,
        paged_value_cache,
    )
    attended, layer_out = second_half(
        part.reshape(seq, row_count, count, dim),
        lse.reshape(seq, row_count, dim),
        fresh,
        fresh_lse,
        x,
        mlp_gain.reshape(-1, 128),
        w_output,
        w_gate,
        w_up,
        w_down,
    )
    shape = (steps, row_count, width)
    return tuple(finish(attended, layer_out, shape))


def solution(mesh):
    in_specs = (
        P(None, "seq", None),
        P(),
        P(None, "tp"),
        P(None, "tp"),
        P(None, "tp"),
        P("tp", None),
        P(),
        P(None, ("seq", "tp")),
        P(None, ("seq", "tp")),
        P(("seq", "tp"), None),
        P("seq", "tp", None, None),
        P("seq", "tp", None, None),
        P(),
        P("seq"),
        P("seq"),
        P(),
    )
    out_specs = (P(None, "seq", None), P(None, "seq", None))
    return jax.shard_map(local, mesh=mesh, in_specs=in_specs, out_specs=out_specs, check_vma=False)
```

```python
import functools

import jax
import jax.numpy as jnp
import numpy as np
from jax import lax
from jax.experimental import pallas as pl
from jax.experimental.pallas import tpu as pltpu
from jax.sharding import PartitionSpec as P

STEPS = 4
rope_theta = 100000000.0
norm_eps = 1e-05
masked_low = -1e30


def paged_kernel(
    pages, request_ref, number_ref, slot_ref, length_ref, q_ref, k_ref, v_ref, o_ref, lse_ref, m_s, l_s, acc_s
):
    step = pl.program_id(0)
    scale = k_ref.shape[-1] ** (-0.5)
    length = k_ref.shape[1]

    @pl.when(step == 0)
    def _():
        m_s[...] = jnp.full_like(m_s, masked_low)
        l_s[...] = jnp.zeros_like(l_s)
        acc_s[...] = jnp.zeros_like(acc_s)

    stats = []
    for i in range(pages):
        page = step * pages + i
        request = request_ref[page]
        live_page = request >= 0
        request = jnp.maximum(request, 0)
        row = slot_ref[request]
        valid = jnp.clip(length_ref[request] - number_ref[page] * length, 0, length)
        valid = jnp.where(live_page, valid, 0)
        q = q_ref[(row % 8) // 4, row // 8, row % 4]
        s = (
            lax.dot_general(
                q, k_ref[i], (((1,), (1,)), ((), ())), preferred_element_type=jnp.float32
            )
            * scale
        )
        live = lax.broadcasted_iota(jnp.int32, s.shape, 1) < valid
        s = jnp.where(live, s, masked_low)
        m = jnp.max(s, axis=-1, keepdims=True)
        w = jnp.where(live, jnp.exp(s - m), 0.0)
        l = jnp.sum(w, axis=-1, keepdims=True)
        acc = jnp.dot(w.astype(jnp.bfloat16), v_ref[i], preferred_element_type=jnp.float32)
        stats.append((row, m, l, acc))
    for row, m, l, acc in stats:
        m_old = m_s[row]
        m_new = jnp.maximum(m_old, m)
        a_old = jnp.exp(m_old - m_new)
        a_new = jnp.exp(m - m_new)
        m_s[row] = m_new
        l_s[row] = l_s[row] * a_old + l * a_new
        acc_s[row] = acc_s[row] * a_old + acc * a_new

    @pl.when(step == pl.num_programs(0) - 1)
    def _():
        o_ref[...] = acc_s[...].astype(o_ref.dtype)
        lse_ref[...] = compact(m_s[...], l_s[...])


def compact(tops, sums):
    row = lax.broadcasted_iota(jnp.int32, tops.shape, 1)
    lane = lax.broadcasted_iota(jnp.int32, tops.shape, 2)
    count = tops.shape[1]
    picked = jnp.where(lane == row, tops, jnp.where(lane == row + count, sums, 0.0))
    return jnp.sum(picked, axis=1)


def expand(values, count):
    shape = (values.shape[0], count, values.shape[1])
    eye = lax.broadcasted_iota(jnp.int32, shape, 1) == lax.broadcasted_iota(jnp.int32, shape, 2)
    wide = jnp.broadcast_to(values[:, None, :], shape)
    return jnp.sum(jnp.where(eye, wide, 0.0), axis=-1, keepdims=True)


def paged_attention(request, number, slot, lengths, queries, keys, values):
    group, dim = queries.shape[-2:]
    total = slot.shape[0]
    count, _, length, _ = keys.shape
    pages = next(n for n in (12, 9, 6, 4, 3, 2, 1) if count % n == 0)
    paged = pl.BlockSpec((pages, None, length, dim), lambda i, *_: (i, 0, 0, 0))
    return pl.pallas_call(
        functools.partial(paged_kernel, pages),
        grid_spec=pltpu.PrefetchScalarGridSpec(
            num_scalar_prefetch=4,
            grid=(count // pages,),
            in_specs=[
                pl.BlockSpec(queries.shape, lambda i, *_: (0, 0, 0, 0, 0)),
                paged,
                paged,
            ],
            out_specs=[
                pl.BlockSpec((total, group, dim), lambda i, *_: (0, 0, 0)),
                pl.BlockSpec((total, dim), lambda i, *_: (0, 0)),
            ],
            scratch_shapes=[
                pltpu.VMEM((total, group, dim), jnp.float32),
                pltpu.VMEM((total, group, dim), jnp.float32),
                pltpu.VMEM((total, group, dim), jnp.float32),
            ],
        ),
        out_shape=[
            jax.ShapeDtypeStruct((total, group, dim), jnp.bfloat16),
            jax.ShapeDtypeStruct((total, dim), jnp.float32),
        ],
        name="paged_attention",
    )(request, number, slot, lengths, queries, keys, values)


AXES = (("y", "x", "z"), ("x", "z", "y"), ("z", "y", "x"))
MESH = pl.DeviceIdType.MESH


class Place:
    def __init__(self):
        s = lax.axis_index("seq")
        t = lax.axis_index("tp")
        self.at = {"z": s // 4, "x": s % 4, "y": t // 2}
        self.core = t % 2
        self.s = s
        self.t = t

    def shifted(self, axis, by):
        return lax.rem(self.at[axis] + (by + 4), 4)

    def device(self, axis=None, by=0, flip=False):
        at = dict(self.at)
        if axis is not None:
            at[axis] = self.shifted(axis, by)
        core = 1 - self.core if flip else self.core
        return {"seq": at["z"] * 4 + at["x"], "tp": at["y"] * 2 + core}


class Wire:
    def __init__(self, send_sem, recv_sem):
        self.send_sem = send_sem
        self.recv_sem = recv_sem
        self.used = 0
        self.sent = []

    def slot(self):
        self.used += 1
        return self.used - 1

    def send(self, slot, src, dst, device):
        copy = pltpu.make_async_remote_copy(
            src_ref=src,
            dst_ref=dst,
            send_sem=self.send_sem.at[slot],
            recv_sem=self.recv_sem.at[slot],
            device_id=device,
            device_id_type=MESH,
        )
        copy.start()
        self.sent.append(copy)

    def recv(self, slot, dst, device):
        pltpu.make_async_remote_copy(
            src_ref=dst,
            dst_ref=dst,
            send_sem=self.send_sem.at[slot],
            recv_sem=self.recv_sem.at[slot],
            device_id=device,
            device_id_type=MESH,
        ).wait_recv()

    def drain(self):
        for copy in self.sent:
            copy.wait_send()


def greet(place):
    barrier = pltpu.get_barrier_semaphore()
    peers = [{"seq": place.s, "tp": lax.rem(place.t + j, 8)} for j in range(1, 8)]
    peers += [{"seq": seq_peer(place, j)[0], "tp": place.t} for j in SEQ_ORDER]
    for peer in peers:
        pl.semaphore_signal(barrier, inc=1, device_id=peer, device_id_type=MESH)
    return barrier, len(peers)


SEQ_ORDER = tuple(
    sorted(
        ((dz, dx) for dz in range(4) for dx in range(4) if (dz, dx) != (0, 0)),
        key=lambda d: -(min(d[0], 4 - d[0]) + min(d[1], 4 - d[1])),
    )
)


def seq_peer(place, by):
    on = place.shifted("z", by[0]) * 4 + place.shifted("x", by[1])
    back = place.shifted("z", -by[0]) * 4 + place.shifted("x", -by[1])
    return on, back


class Gather:
    def __init__(self, wire, place, axes, buf):
        self.wire, self.place, self.buf = wire, place, buf
        self.a, self.b, self.c = axes
        self.slots_a = [wire.slot() for _ in range(3)]
        self.slots_b = [wire.slot() for _ in range(3)]
        self.slots_c = [[wire.slot() for _ in range(4)] for _ in range(4)]
        self.slots_p = [[wire.slot() for _ in range(4)] for _ in range(4)]

    def group(self, db, dc, core=None):
        place = self.place
        core = place.core if core is None else core
        return self.buf.at[core, place.shifted(self.c, dc), place.shifted(self.b, db)]

    def half(self, db, dc, which):
        place = self.place
        return self.buf.at[
            place.core, place.shifted(self.c, dc), place.shifted(self.b, db), pl.ds(2 * which, 2)
        ]

    def block(self, da):
        place = self.place
        return self.buf.at[
            place.core, place.at[self.c], place.at[self.b], place.shifted(self.a, da)
        ]

    def open(self):
        mine = self.block(0)
        for j in (2, 1, 3):
            self.wire.send(self.slots_a[j - 1], mine, mine, self.place.device(self.a, j))

    def spread(self, db):
        mine = self.group(db, 0)
        slots = self.slots_c[db]
        self.wire.send(slots[0], mine, mine, self.place.device(self.c, 1))
        self.wire.send(slots[1], mine, mine, self.place.device(self.c, -1))
        self.over(db, 0)

    def over(self, db, dc):
        mine = self.group(db, dc)
        self.wire.send(self.slots_p[db][dc], mine, mine, self.place.device(flip=True))

    def line(self):
        for j in (1, 3, 2):
            self.wire.recv(self.slots_a[j - 1], self.block(-j), self.place.device(self.a, -j))
        mine = self.group(0, 0)
        for j in (2, 1, 3):
            self.wire.send(self.slots_b[j - 1], mine, mine, self.place.device(self.b, j))

    def plane(self, j):
        self.wire.recv(self.slots_b[j - 1], self.group(-j, 0), self.place.device(self.b, -j))
        self.spread(4 - j)

    def space_near(self, db):
        place, wire = self.place, self.wire
        slots = self.slots_c[db]
        wire.recv(slots[0], self.group(db, -1), place.device(self.c, -1))
        part = self.half(db, -1, 0)
        wire.send(slots[2], part, part, place.device(self.c, 1))
        wire.recv(slots[1], self.group(db, 1), place.device(self.c, 1))
        part = self.half(db, 1, 1)
        wire.send(slots[3], part, part, place.device(self.c, -1))
        self.over(db, 3)
        self.over(db, 1)

    def space_far(self, db):
        place, wire = self.place, self.wire
        slots = self.slots_c[db]
        wire.recv(slots[2], self.half(db, 2, 0), place.device(self.c, -1))
        wire.recv(slots[3], self.half(db, 2, 1), place.device(self.c, 1))
        self.over(db, 2)

    def other_core(self, dc):
        place = self.place
        for db in (0, 3, 1, 2):
            self.wire.recv(
                self.slots_p[db][dc], self.group(db, dc, 1 - place.core), place.device(flip=True)
            )


def add_into(dst, src, count):
    def body(i, carry):
        total = dst[i].astype(jnp.float32) + src[i].astype(jnp.float32)
        dst[i] = total.astype(dst.dtype)
        return carry

    lax.fori_loop(0, count, body, 0)


class Scatter:
    def __init__(self, wire, place, axis, piece, relay, near):
        self.wire, self.place, self.axis = wire, place, axis
        self.piece, self.relay, self.near = piece, relay, near
        self.slots = [wire.slot() for _ in range(6)]

    def open(self):
        w, p = self.wire, self.place
        up, down = p.device(self.axis, 1), p.device(self.axis, -1)
        w.send(self.slots[0], self.piece(2, 0), self.relay.at[0], up)
        w.send(self.slots[1], self.piece(2, 1), self.relay.at[1], down)
        w.send(self.slots[2], self.piece(1, 1), self.near.at[0, 1], up)
        w.send(self.slots[3], self.piece(-1, 0), self.near.at[1, 0], down)

    def pass_on(self, count):
        w, p = self.wire, self.place
        up, down = p.device(self.axis, 1), p.device(self.axis, -1)
        w.recv(self.slots[0], self.relay.at[0], down)
        add_into(self.piece(1, 0), self.relay.at[0], count)
        w.send(self.slots[4], self.piece(1, 0), self.near.at[0, 0], up)
        w.recv(self.slots[1], self.relay.at[1], up)
        add_into(self.piece(-1, 1), self.relay.at[1], count)
        w.send(self.slots[5], self.piece(-1, 1), self.near.at[1, 1], down)

    def close(self):
        w, p = self.wire, self.place
        up, down = p.device(self.axis, 1), p.device(self.axis, -1)
        w.recv(self.slots[2], self.near.at[0, 1], down)
        w.recv(self.slots[3], self.near.at[1, 0], up)
        w.recv(self.slots[4], self.near.at[0, 0], down)
        w.recv(self.slots[5], self.near.at[1, 1], up)


def slots_needed():
    return 30 + 7 + 3 * (3 + 3 + 16 + 16) + 12 + 3 * (6 + 3 + 3) + 7


def block_kernel(
    widths,
    part_ref,
    lse_ref,
    fresh_ref,
    fresh_lse_ref,
    x_ref,
    gain_ref,
    wo_hbm,
    wg_hbm,
    wu_hbm,
    wd_hbm,
    attended_ref,
    layer_ref,
    wo,
    wgu,
    wd,
    s1,
    r1,
    g0,
    g1,
    g2,
    acc,
    squares,
    act,
    p0,
    p1,
    p2,
    o0,
    o1,
    o2,
    rc0,
    rc1,
    rc2,
    nc0,
    nc1,
    nc2,
    q0,
    q1,
    q2,
    nb0,
    nb1,
    nb2,
    ta0,
    ta1,
    ta2,
    ra0,
    ra1,
    ra2,
    mine_s,
    last,
    parts,
    lses,
    att32,
    load_sem,
    send_sem,
    recv_sem,
):
    place = Place()
    t, core = place.t, place.core
    ff = wd.shape[0]
    cols = sum(widths)
    starts = (0, widths[0], widths[0] + widths[1])
    wire = Wire(send_sem, recv_sem)
    barrier, peers = greet(place)
    weights = (
        (wg_hbm, wgu.at[:, pl.ds(0, ff)]),
        (wu_hbm, wgu.at[:, pl.ds(ff, ff)]),
        (wo_hbm, wo),
        (wd_hbm, wd),
    )
    loads = [
        pltpu.make_async_copy(src, dst, load_sem.at[i]) for i, (src, dst) in enumerate(weights)
    ]
    for load in loads:
        load.start()

    def columns(index, start=0, size=cols):
        return pl.ds(pl.multiple_of(index * cols + start, 128), size)

    slots_e = [[wire.slot() for _ in range(2)] for _ in range(15)]
    pl.semaphore_wait(barrier, peers)
    for n, j in enumerate(SEQ_ORDER):
        to, _ = seq_peer(place, j)
        device = {"seq": to, "tp": t}
        wire.send(slots_e[n][0], part_ref.at[to], parts.at[n], device)
        wire.send(slots_e[n][1], lse_ref.at[to], lses.at[n], device)

    loads[0].wait()
    loads[1].wait()

    def gain_body(n, carry):
        rows = pl.ds(pl.multiple_of(n * 128, 128), 128)
        row = jnp.broadcast_to(gain_ref[pl.ds(n, 1), :], (128, 128))
        eye = lax.broadcasted_iota(jnp.int32, row.shape, 0) == lax.broadcasted_iota(
            jnp.int32, row.shape, 1
        )
        column = jnp.sum(jnp.where(eye, row, 0.0), axis=1, keepdims=True)
        wgu[rows, :] = (wgu[rows, :].astype(jnp.float32) * column).astype(wgu.dtype)
        return carry

    lax.fori_loop(0, wgu.shape[0] // 128, gain_body, 0)

    for n, j in enumerate(SEQ_ORDER):
        _, back = seq_peer(place, j)
        device = {"seq": back, "tp": t}
        wire.recv(slots_e[n][0], parts.at[n], device)
        wire.recv(slots_e[n][1], lses.at[n], device)
    count = part_ref.shape[2]
    sums = [lses[n] for n in range(15)] + [lse_ref[place.s], fresh_lse_ref[...]]
    top = functools.reduce(jnp.maximum, sums)
    shares = [jnp.exp(v - top) for v in sums]
    totals = [pltpu.roll(v, v.shape[1] - count, 1) for v in sums]
    whole = functools.reduce(jnp.add, [w * v for w, v in zip(shares, totals)])
    used = lax.broadcasted_iota(jnp.int32, top.shape, 1) < count
    shares = [jnp.where(used, w / jnp.where(used, whole, 1.0), 0.0) for w in shares]
    attention = fresh_ref[...] * expand(shares[16], count)
    for n in range(15):
        attention += parts[n].astype(jnp.float32) * expand(shares[n], count)
    attention += part_ref[place.s].astype(jnp.float32) * expand(shares[15], count)
    att32[...] = attention
    per_step = count // STEPS
    heads = jnp.concatenate(
        [
            jnp.concatenate(
                [att32[:, i * per_step + g, :].astype(jnp.bfloat16) for g in range(per_step)],
                axis=1,
            )
            for i in range(STEPS)
        ],
        axis=0,
    )

    slots1 = [wire.slot() for _ in range(7)]
    loads[2].wait()
    own = None
    for j in (4, 3, 5, 2, 6, 1, 7, 0):
        to = lax.rem(t + j, 8)
        part = jnp.dot(heads, wo[:, columns(to)], preferred_element_type=jnp.float32)
        if j == 0:
            own = part
            break
        s1[j - 1] = part.astype(s1.dtype)
        wire.send(slots1[j - 1], s1.at[j - 1], r1.at[j - 1], {"seq": place.s, "tp": to})
    total = own + x_ref[:, columns(t)].astype(jnp.float32)
    for j in (1, 7, 2, 6, 3, 5, 4):
        wire.recv(slots1[j - 1], r1.at[j - 1], {"seq": place.s, "tp": lax.rem(t + 8 - j, 8)})
        total = total + r1[j - 1].astype(jnp.float32)
    mine = total.astype(jnp.bfloat16)
    mine_s[...] = mine

    gs = (g0, g1, g2)
    gathers = [Gather(wire, place, axes, buf) for axes, buf in zip(AXES, gs)]
    for g, w, start in zip(gathers, widths, starts):
        g.buf[core, place.at[g.c], place.at[g.b], place.at[g.a]] = mine[:, start : start + w]
        g.open()
    for g in gathers:
        g.line()
    for j in (1, 3, 2):
        for g in gathers:
            g.plane(j)
            if j == 1:
                g.spread(0)

    acc[...] = jnp.zeros_like(acc)
    squares[...] = jnp.zeros_like(squares)

    def squared(v):
        total = None
        for n in range(v.shape[-1] // 128):
            f = v[:, n * 128 : n * 128 + 128].astype(jnp.float32)
            total = f * f if total is None else total + f * f
        return total

    def product(v, w):
        return jnp.dot(v, w, preferred_element_type=jnp.float32)

    def take(v, w):
        acc[...] += product(v, w).reshape(acc.shape)
        squares[...] += squared(v).reshape(squares.shape)

    def use_slab(dc, c):
        y = place.shifted("y", dc)
        v = g1[c, y].reshape(512, widths[1])
        take(v, wgu[columns(y * 2 + c, starts[1], widths[1]), :])

    use_slab(0, core)
    for db in (0, 3, 1, 2):
        for g in (gathers[2], gathers[1], gathers[0]):
            g.space_near(db)
    use_slab(3, core)
    use_slab(1, core)
    gathers[1].other_core(0)
    use_slab(0, 1 - core)
    for db in (0, 3, 1, 2):
        for g in (gathers[2], gathers[1], gathers[0]):
            g.space_far(db)
    for dc in (3, 1):
        gathers[1].other_core(dc)
        use_slab(dc, 1 - core)
    use_slab(2, core)
    gathers[1].other_core(2)
    use_slab(2, 1 - core)
    for dc in range(4):
        gathers[2].other_core(dc)

    def last_body(i, carry):
        c, half = i // 2, i % 2
        vs = []
        ws = []
        for n in range(2):
            y = half * 2 + n
            v = jnp.stack([jnp.stack([g2[c, x, y, z] for x in range(4)]) for z in range(4)])
            vs.append(v.reshape(512, widths[2]))
            ws.append(wgu[columns(y * 2 + c, starts[2], widths[2]), :])
        take(jnp.concatenate(vs, axis=1), jnp.concatenate(ws, axis=0))
        return carry

    lax.fori_loop(0, 4, last_body, 0)
    for dc in range(4):
        gathers[0].other_core(dc)

    def first_body(i, carry):
        c, y = i // 4, i % 4
        v = g0[c, :, :, y].reshape(512, widths[0])
        take(v, wgu[columns(y * 2 + c, 0, widths[0]), :])
        return carry

    lax.fori_loop(0, 8, first_body, 0)

    def act_body(i, carry):
        rows = pl.ds(pl.multiple_of(i * 128, 128), 128)
        mean = jnp.sum(squares[i].reshape(128, 128), axis=-1, keepdims=True) / (8 * cols)
        r = lax.rsqrt(mean + norm_eps)
        both = acc[i].reshape(128, 2 * ff) * r
        gate = both[:, :ff]
        up = both[:, ff:]
        act[rows, :] = (gate / (1.0 + jnp.exp(-gate)) * up).astype(act.dtype)
        return carry

    lax.fori_loop(0, 4, act_body, 0)
    loads[3].wait()

    ps, os_ = (p0, p1, p2), (o0, o1, o2)

    def at_y(k, ref, y):
        return ref.at[:, :, y] if k == 0 else (ref.at[y] if k == 1 else ref.at[:, y])

    def down_rows(tt, z):
        rows = act[pl.ds(pl.multiple_of(z * 128, 128), 128), :]
        return jnp.dot(rows, wd[:, columns(tt)], preferred_element_type=jnp.float32)

    slots_o = [[wire.slot() for _ in range(3)] for _ in range(4)]
    for y in range(4):

        def other_body(z, carry):
            d = down_rows(y * 2 + 1 - core, z).astype(jnp.bfloat16).reshape(4, 32, cols)
            ps[0][1 - core, z, :, y] = d[:, :, : widths[0]]
            ps[1][1 - core, y, z] = d[:, :, starts[1] : starts[2]]
            for x in range(4):
                ps[2][1 - core, x, y, z] = d[x, :, starts[2] :]
            return carry

        lax.fori_loop(0, 4, other_body, 0)
        for k in range(3):
            wire.send(
                slots_o[y][k],
                at_y(k, ps[k].at[1 - core], y),
                at_y(k, os_[k], y),
                place.device(flip=True),
            )
    for y in range(4):
        for k in range(3):
            wire.recv(slots_o[y][k], at_y(k, os_[k], y), place.device(flip=True))

        def own_body(z, carry):
            d = down_rows(y * 2 + core, z).reshape(4, 32, cols)
            d0 = d[:, :, : widths[0]] + os_[0][z, :, y].astype(jnp.float32)
            ps[0][core, z, :, y] = d0.astype(jnp.bfloat16)
            d1 = d[:, :, starts[1] : starts[2]] + os_[1][y, z].astype(jnp.float32)
            ps[1][core, y, z] = d1.astype(jnp.bfloat16)
            for x in range(4):
                d2 = d[x, :, starts[2] :] + os_[2][x, y, z].astype(jnp.float32)
                ps[2][core, x, y, z] = d2.astype(jnp.bfloat16)
            return carry

        lax.fori_loop(0, 4, own_body, 0)

    rcs, ncs, qs = (rc0, rc1, rc2), (nc0, nc1, nc2), (q0, q1, q2)
    nbs, tas, ras = (nb0, nb1, nb2), (ta0, ta1, ta2), (ra0, ra1, ra2)

    def piece_c(k):
        def view(d, half):
            at = place.shifted(AXES[k][2], d)
            return ps[k].at[core, at, pl.ds(2 * half, 2)]

        return view

    along_c = [
        Scatter(wire, place, AXES[k][2], piece_c(k), rcs[k], ncs[k]) for k in range(3)
    ]
    slots_b = [[wire.slot() for _ in range(3)] for _ in range(3)]
    slots_a = [[wire.slot() for _ in range(3)] for _ in range(3)]
    for s in along_c:
        s.open()
    order = (2, 0, 1)
    for k in order:
        along_c[k].pass_on(2)
    for k in order:
        along_c[k].close()
        at = place.at[AXES[k][2]]

        def sum_c(b, carry):
            v = ps[k][core, at, b].astype(jnp.float32)
            v = v + ncs[k][0, b // 2, b % 2].astype(jnp.float32)
            v = v + ncs[k][1, b // 2, b % 2].astype(jnp.float32)
            qs[k][b] = v.astype(jnp.bfloat16)
            return carry

        lax.fori_loop(0, 4, sum_c, 0)
        axis = AXES[k][1]
        for j in (2, 1, 3):
            wire.send(
                slots_b[k][j - 1],
                qs[k].at[place.shifted(axis, j)],
                nbs[k].at[j - 1],
                place.device(axis, j),
            )
    for k in order:
        axis = AXES[k][1]
        at = place.at[axis]
        for j in (1, 3, 2):
            wire.recv(slots_b[k][j - 1], nbs[k].at[j - 1], place.device(axis, -j))
        for a in range(4):
            v = qs[k][at, a].astype(jnp.float32)
            for j in range(3):
                v = v + nbs[k][j, a].astype(jnp.float32)
            tas[k][a] = v.astype(jnp.bfloat16)
        for j in (2, 1, 3):
            axis = AXES[k][0]
            wire.send(
                slots_a[k][j - 1],
                tas[k].at[place.shifted(axis, j)],
                ras[k].at[j - 1],
                place.device(axis, j),
            )
    for k in order:
        axis = AXES[k][0]
        v = tas[k][place.at[axis]].astype(jnp.float32)
        for j in (1, 3, 2):
            wire.recv(slots_a[k][j - 1], ras[k].at[j - 1], place.device(axis, -j))
            v = v + ras[k][j - 1].astype(jnp.float32)
        lo = starts[k]
        v = v + mine_s[:, lo : lo + widths[k]].astype(jnp.float32)
        last[t, :, lo : lo + widths[k]] = v.astype(jnp.bfloat16)
    slots_l = [wire.slot() for _ in range(7)]
    for j in (4, 3, 5, 2, 6, 1, 7):
        to = {"seq": place.s, "tp": lax.rem(t + j, 8)}
        wire.send(slots_l[j - 1], last.at[t], last.at[t], to)
    for y in range(4):
        for c in range(2):
            tt = y * 2 + c
            z, x = place.at["z"], place.at["x"]
            attended_ref[:, tt * cols : tt * cols + widths[0]] = g0[c, z, x, y]
            attended_ref[:, tt * cols + starts[1] : tt * cols + starts[2]] = g1[c, y, z, x]
            attended_ref[:, tt * cols + starts[2] : tt * cols + cols] = g2[c, x, y, z]
    for j in range(1, 8):
        tt = lax.rem(t + 8 - j, 8)
        wire.recv(slots_l[j - 1], last.at[tt], {"seq": place.s, "tp": tt})
    for tt in range(8):
        layer_ref[:, tt * cols : tt * cols + cols] = last[tt]
    wire.drain()


def second_half(part, lse, fresh, fresh_lse, x, gain, w_output, w_gate, w_up, w_down):
    rows, width = x.shape
    cols = width // 8
    ff = w_down.shape[0]
    tiles = cols // 128
    first = -(-2 * tiles // 5)
    widths = (first * 128, first * 128, (tiles - 2 * first) * 128)
    assert rows == 32 and min(widths) > 0
    bf, f32 = jnp.bfloat16, jnp.float32
    vm = pltpu.VMEM

    def each(*shape):
        return [vm(shape + (rows, w), bf) for w in widths]

    count = slots_needed()
    scratch = [
        vm(w_output.shape, bf),
        vm((width, 2 * ff), bf),
        vm(w_down.shape, bf),
        vm((7, rows, cols), bf),
        vm((7, rows, cols), bf),
        *each(2, 4, 4, 4),
        vm((4, 4, 32, 2 * ff), f32),
        vm((4, 4, 32, 128), f32),
        vm((512, ff), bf),
        *each(2, 4, 4, 4),
        *each(4, 4, 4),
        *each(2, 2, 4),
        *each(2, 2, 2, 4),
        *each(4, 4),
        *each(3, 4),
        *each(4),
        *each(3),
        vm((rows, cols), bf),
        vm((8, rows, cols), bf),
        vm((15,) + part.shape[1:], bf),
        vm((15,) + lse.shape[1:], f32),
        vm(part.shape[1:], f32),
        pltpu.SemaphoreType.DMA((4,)),
        pltpu.SemaphoreType.DMA((count,)),
        pltpu.SemaphoreType.DMA((count,)),
    ]
    whole = pl.BlockSpec(memory_space=pltpu.VMEM)
    hbm = pl.BlockSpec(memory_space=pl.ANY)
    out = jax.ShapeDtypeStruct((rows, width), bf)
    return pl.pallas_call(
        functools.partial(block_kernel, widths),
        out_shape=[out, out],
        in_specs=[whole] * 6 + [hbm] * 4,
        out_specs=[whole, whole],
        scratch_shapes=scratch,
        compiler_params=pltpu.CompilerParams(
            collective_id=1, has_side_effects=True, vmem_limit_bytes=63 * 1024 * 1024
        ),
        name="second_half",
    )(part, lse, fresh, fresh_lse, x, gain, w_output, w_gate, w_up, w_down)


class QueryGather:
    def __init__(self, wire, place, axes, buf):
        self.wire, self.place, self.buf = wire, place, buf
        self.a, self.b = axes
        self.slots_a = [wire.slot() for _ in range(3)]
        self.slots_b = [wire.slot() for _ in range(3)]

    def cut(self, b, a):
        return self.buf.at[b, a] if self.b == "z" else self.buf.at[a, b]

    def block(self, da):
        return self.cut(self.place.at[self.b], self.place.shifted(self.a, da))

    def group(self, db):
        return self.cut(self.place.shifted(self.b, db), pl.ds(0, 4))

    def open(self):
        mine = self.block(0)
        for j in (2, 1, 3):
            self.wire.send(self.slots_a[j - 1], mine, mine, self.place.device(self.a, j))

    def line(self):
        for j in (1, 3, 2):
            self.wire.recv(self.slots_a[j - 1], self.block(-j), self.place.device(self.a, -j))
        mine = self.group(0)
        for j in (2, 1, 3):
            self.wire.send(self.slots_b[j - 1], mine, mine, self.place.device(self.b, j))

    def plane(self):
        for j in (1, 3, 2):
            self.wire.recv(self.slots_b[j - 1], self.group(-j), self.place.device(self.b, -j))


def project_kernel(
    x_ref,
    gain_ref,
    freq_ref,
    slot_ref,
    length_ref,
    wq_hbm,
    wk_hbm,
    wv_hbm,
    q_all,
    fresh_ref,
    fresh_lse_ref,
    wq,
    wk,
    wv,
    q32,
    load_sem,
    send_sem,
    recv_sem,
):
    place = Place()
    wire = Wire(send_sem, recv_sem)
    rows, width = x_ref.shape
    dim = wk.shape[1]
    heads = wq.shape[1] // dim
    steps = STEPS
    own = rows // steps
    barrier = pltpu.get_barrier_semaphore()
    for axis in ("x", "z"):
        for by in (1, 2, 3):
            pl.semaphore_signal(
                barrier, inc=1, device_id=place.device(axis, by), device_id_type=MESH
            )
    chunks = load_sem.shape[0]
    depth = width // chunks
    loads = []
    for i in range(chunks):
        part = pl.ds(i * depth, depth)
        loads.append(
            [
                pltpu.make_async_copy(src.at[part], dst.at[part], load_sem.at[i, n])
                for n, (src, dst) in enumerate(((wq_hbm, wq), (wk_hbm, wk), (wv_hbm, wv)))
            ]
        )
        for load in loads[-1]:
            load.start()
    x = x_ref[...].astype(jnp.float32)
    mean = jnp.mean(x * x, axis=-1, keepdims=True)
    normed = (x * lax.rsqrt(mean + norm_eps) * gain_ref[...]).astype(jnp.bfloat16)

    shape = (own, slot_ref.shape[1])
    mine = place.s * own + lax.broadcasted_iota(jnp.int32, shape, 0)
    length = jnp.where(slot_ref[...] == mine, length_ref[...].astype(jnp.float32), 0.0)
    length = jnp.sum(length, axis=-1, keepdims=True)
    position = jnp.concatenate([length + float(i) for i in range(steps)], axis=0)
    angle = position * freq_ref[...]
    cosine = jnp.cos(angle)
    sine = jnp.sin(angle)
    low = lax.broadcasted_iota(jnp.int32, angle.shape, 1) < dim // 2
    sine = jnp.where(low, -sine, sine)

    def rotate(v):
        return v * cosine + pltpu.roll(v, dim // 2, 1) * sine

    q = k = v = 0.0
    for i in range(chunks):
        for load in loads[i]:
            load.wait()
        lhs = normed[:, i * depth : (i + 1) * depth]
        part = pl.ds(i * depth, depth)
        q = q + jnp.dot(lhs, wq[part, :], preferred_element_type=jnp.float32)
        k = k + jnp.dot(lhs, wk[part, :], preferred_element_type=jnp.float32)
        v = v + jnp.dot(lhs, wv[part, :], preferred_element_type=jnp.float32)
    for g in range(heads):
        turned = rotate(q[:, g * dim : (g + 1) * dim])
        for i in range(steps):
            q32[:, i * heads + g, :] = turned[i * own : (i + 1) * own]
    queries = q32[...].astype(jnp.bfloat16)
    s_at = (place.at["z"], place.at["x"])
    half = own // 2
    for n in range(2):
        q_all[n, s_at[0], s_at[1]] = queries[n * half : (n + 1) * half]
    gathers = [
        QueryGather(wire, place, axes, q_all.at[n])
        for n, axes in enumerate((("x", "z"), ("z", "x")))
    ]
    pl.semaphore_wait(barrier, 6)
    for g in gathers:
        g.open()

    new_k = rotate(k).astype(jnp.bfloat16)
    new_v = v.astype(jnp.bfloat16)
    count = steps * heads
    flat = queries.reshape(own * count, dim)
    s = lax.dot_general(
        flat, new_k, (((1,), (1,)), ((), ())), preferred_element_type=jnp.float32
    ) * (dim**-0.5)
    r = lax.broadcasted_iota(jnp.int32, s.shape, 0)
    c = lax.broadcasted_iota(jnp.int32, s.shape, 1)
    allowed = (r // count == c % own) & (c // own <= (r % count) // heads)
    s = jnp.where(allowed, s, masked_low)
    top = jnp.max(s, axis=-1, keepdims=True)
    w = jnp.where(allowed, jnp.exp(s - top), 0.0)
    total = jnp.sum(w, axis=-1, keepdims=True)
    acc = jnp.dot(w.astype(jnp.bfloat16), new_v, preferred_element_type=jnp.float32)
    fresh_ref[...] = acc.reshape(own, count, dim)
    shape = (own, count, dim)
    fresh_lse_ref[...] = compact(
        jnp.broadcast_to(top, (own * count, dim)).reshape(shape),
        jnp.broadcast_to(total, (own * count, dim)).reshape(shape),
    )

    for g in gathers:
        g.line()
    for g in gathers:
        g.plane()
    wire.drain()


def first_half(x, gain, slot, lengths, w_query, w_key, w_value):
    rows, width = x.shape
    dim = w_key.shape[1]
    count = STEPS * w_query.shape[1] // dim
    own = rows // STEPS
    bf, f32, vm = jnp.bfloat16, jnp.float32, pltpu.VMEM
    exponent = np.arange(dim // 2, dtype=np.float32) * np.float32(2.0 / dim)
    freq = (rope_theta ** -exponent.astype(np.float64)).astype(np.float32)
    freq = jnp.asarray(np.concatenate([freq, freq])[None, :])
    whole = pl.BlockSpec(memory_space=pltpu.VMEM)
    hbm = pl.BlockSpec(memory_space=pl.ANY)
    return pl.pallas_call(
        project_kernel,
        out_shape=[
            jax.ShapeDtypeStruct((2, 4, 4, own // 2, count, dim), bf),
            jax.ShapeDtypeStruct((own, count, dim), f32),
            jax.ShapeDtypeStruct((own, dim), f32),
        ],
        in_specs=[whole] * 5 + [hbm] * 3,
        out_specs=[whole] * 3,
        scratch_shapes=[
            vm(w_query.shape, bf),
            vm(w_key.shape, bf),
            vm(w_value.shape, bf),
            vm((own, count, dim), f32),
            pltpu.SemaphoreType.DMA((8, 3)),
            pltpu.SemaphoreType.DMA((12,)),
            pltpu.SemaphoreType.DMA((12,)),
        ],
        compiler_params=pltpu.CompilerParams(
            collective_id=2, has_side_effects=True, vmem_limit_bytes=63 * 1024 * 1024
        ),
        name="first_half",
    )(x, gain[None, :], freq, slot[None, :], lengths[None, :], w_query, w_key, w_value)


def finish_kernel(a_ref, b_ref, c_ref, d_ref):
    c_ref[...] = a_ref[...].reshape(c_ref.shape)
    d_ref[...] = b_ref[...].reshape(d_ref.shape)


def finish(attended, layer_out, shape):
    out = jax.ShapeDtypeStruct(shape, attended.dtype)
    return pl.pallas_call(finish_kernel, out_shape=[out, out], name="finish")(attended, layer_out)


def local(
    token_inputs,
    attn_gain,
    w_query,
    key_projection,
    value_projection,
    w_output,
    mlp_gain,
    w_gate,
    w_up,
    w_down,
    key_cache,
    paged_value_cache,
    cache_lengths,
    page_request,
    page_number,
    request_slot,
):
    steps, row_count, width = token_inputs.shape
    x = token_inputs.reshape(steps * row_count, width)
    queries, fresh, fresh_lse = first_half(
        x, attn_gain, request_slot, cache_lengths, w_query, key_projection, value_projection
    )
    count, dim = queries.shape[-2:]
    seq = lax.axis_size("seq")
    queries = queries.reshape(2, seq, row_count // 2, count, dim)
    part, lse = paged_attention(
        page_request,
        page_number,
        request_slot,
        cache_lengths,
        queries,
        key_cache,
        paged_value_cache,
    )
    attended, layer_out = second_half(
        part.reshape(seq, row_count, count, dim),
        lse.reshape(seq, row_count, dim),
        fresh,
        fresh_lse,
        x,
        mlp_gain.reshape(-1, 128),
        w_output,
        w_gate,
        w_up,
        w_down,
    )
    shape = (steps, row_count, width)
    return tuple(finish(attended, layer_out, shape))


def solution(mesh):
    in_specs = (
        P(None, "seq", None),
        P(),
        P(None, "tp"),
        P(None, "tp"),
        P(None, "tp"),
        P("tp", None),
        P(),
        P(None, ("seq", "tp")),
        P(None, ("seq", "tp")),
        P(("seq", "tp"), None),
        P("seq", "tp", None, None),
        P("seq", "tp", None, None),
        P(),
        P("seq"),
        P("seq"),
        P(),
    )
    out_specs = (P(None, "seq", None), P(None, "seq", None))
    return jax.shard_map(local, mesh=mesh, in_specs=in_specs, out_specs=out_specs, check_vma=False)
```
